32 devices in a mesh: rep: 8 (over y, x, core), shard: 4 (over z).
Axes of the slice: x: 2, y: 2, z: 4, core: 2. Of those that a mesh axis runs over, the one named last changes fastest.
Arguments:
- char_ids: int32 [128, 48], P(('rep', 'shard')), may hold values from 0 to 274
- prefix: int32 [128], P(('rep', 'shard')), may hold values from 4 to 24, as said below
- embedding: bfloat16 [2, 275, 100], replicated, may hold values from -6 to 6
- w_in: bfloat16 [2, 4, 100, 2048], P(None, None, None, 'shard'), may hold values from -0.625 to 0.625
- w_rec: bfloat16 [2, 4, 2048, 2048], P(None, None, None, 'shard'), may hold values from -0.125 to 0.125
- gate_bias: bfloat16 [2, 4, 2048], P(None, None, 'shard'), may hold values from -3 to 4
- w_out: bfloat16 [2, 2048, 275], P(None, 'shard'), may hold values from -0.875 to 0.875
- b_out: bfloat16 [2, 275], replicated, may hold values from -3 to 3
Outputs:
- grad_embed: float32 [2, 275, 100], replicated
- grad_in: float32 [2, 4, 100, 2048], P(None, None, None, 'shard')
- grad_rec: float32 [2, 4, 2048, 2048], P(None, None, 'rep', 'shard')
- grad_bias: float32 [2, 4, 2048], P(None, None, 'shard')
- grad_out: float32 [2, 2048, 275], P(None, 'shard')
- grad_bout: float32 [2, 275], replicated
The draws below stay inside these ranges and needn't reach their ends.
Inputs may be any that keep to these rules, and one draw needn't show every extreme that they name: Some sequence has a prefix of exactly 24 characters.
All inputs are finite; a program needn't handle non-finite values.
Results may differ from the reference program's by a relative error of at most 0.0015.
Values may be sent and summed in bfloat16 or wider, within the bound.
A program may use at most 192 MiB of HBM per device.

```python
import math
import jax
import jax.numpy as jnp
import numpy as np
from jax import lax

UNITS = 2048
EMBED = 100
VOCAB = 275
SEQ_DEV = 4
LENGTH = 48
PREFIX = 24
SEQS = 128
TOKENS = 6144
N_REP = 8
N_SHARD = 4


def draw_prefix(key, part):
    lowest = max(2, LENGTH // 10)
    values = jax.random.randint(jax.random.fold_in(key, 7), (SEQS,), lowest, PREFIX + 1, dtype=jnp.int32)
    chosen = jax.random.randint(jax.random.fold_in(key, 11), (), 0, SEQS, dtype=jnp.int32)
    return values.at[chosen].set(PREFIX)


def draw_gate_bias(key, part):
    base = jnp.clip(0.5 * jax.random.normal(jax.random.fold_in(key, 3), (2, 4, UNITS), jnp.float32), -3.0, 3.0)
    lowest = 1.5
    forget_bias = jax.random.uniform(jax.random.fold_in(key, 5), (2, UNITS), jnp.float32, lowest, 4.0)
    forget_row = (jnp.arange(4, dtype=jnp.int32) == 1)[None, :, None]
    return jnp.where(forget_row, forget_bias[:, None, :], base).astype(jnp.bfloat16)


def set_ends(values, rng, least, high):
    dims = values.shape
    spot = [jax.random.randint(jax.random.fold_in(rng, axis), (), 0, dims[axis]) for axis in range(len(dims))]
    values = values.at[tuple(spot)].set(least)
    longest = dims.index(max(dims))
    spot[longest] = (spot[longest] + 1) % dims[longest]
    return values.at[tuple(spot)].set(high)


def block_levels(own_key, shape, split, low, top_value):
    def one(dim, shards_of):
        steps = jax.random.uniform(jax.random.fold_in(jax.random.fold_in(own_key, 6), dim), (shards_of,), jnp.float32, low / len(split), top_value / len(split))
        return jnp.repeat(jnp.exp(steps), shape[dim] // shards_of).reshape((-1,) + (1,) * (len(shape) - dim - 1))

    level = one(*split[0])
    for cut in split[1:]:
        level = level * one(*cut)
    return level


def rank_bounds(amount, slope):
    loads = [(1 << 20) // math.isqrt(rank ** slope) + 1 for rank in range(1, amount + 1)]
    deviation = 1 + sum(loads) // (1 << 30)
    return np.cumsum(np.array([max(1, weight // deviation) for weight in loads]))


def ranked_ids(own_key, dims, amount, skew):
    listing = rank_bounds(amount, skew)
    lot = jax.random.randint(jax.random.fold_in(own_key, 1), dims, 0, int(listing[amount - 1]))
    standing = jnp.searchsorted(jnp.asarray(listing, jnp.int32), lot, side="right")
    return jax.random.permutation(jax.random.fold_in(own_key, 2), amount)[standing].astype(jnp.int32)


def normal_values(key, dims, width, reach, cuts=(), kind=jnp.bfloat16):
    level = block_levels(key, dims, cuts, -0.22, 0.18) if cuts else 1.0
    drawn = jax.random.normal(key, dims, jnp.float32) * width * level
    return jnp.minimum(jnp.maximum(drawn, -reach), reach).astype(kind)


def setup_inputs(seed: int = 0) -> dict:
    seeds = jax.random.split(jax.random.key(seed), 9)
    return {
        "char_ids": set_ends(ranked_ids(seeds[0], (SEQS, LENGTH), VOCAB, 2), jax.random.fold_in(seeds[0], 3), 0, VOCAB - 1).astype(jnp.int32),
        "prefix": draw_prefix(jax.random.fold_in(seeds[8], 71), 0),
        "embedding": normal_values(seeds[2], (2, VOCAB, EMBED), 1.0, 6.0),
        "w_in": normal_values(seeds[3], (2, 4, EMBED, UNITS), EMBED ** -0.5, 0.625, ((3, 4),)),
        "w_rec": normal_values(seeds[4], (2, 4, UNITS, UNITS), UNITS ** -0.5, 0.125, ((3, 4),)),
        "gate_bias": draw_gate_bias(jax.random.fold_in(seeds[8], 71), 0),
        "w_out": normal_values(seeds[6], (2, UNITS, VOCAB), 48 ** -0.5, 0.875, ((1, 4),)),
        "b_out": normal_values(seeds[7], (2, VOCAB), 0.5, 3.0),
    }


@jax.custom_vjp
def low(v):
    return lax.optimization_barrier(v.astype(jnp.bfloat16)).astype(jnp.float32)

@jax.custom_vjp
def low_back(v):
    return v

def low_keep(v):
    return (low(v), None)

def low_pass(kept, grad):
    return (grad,)

def back_keep(v):
    return (v, None)

def back_low(kept, grad):
    return (low(grad),)
low.defvjp(low_keep, low_pass)
low_back.defvjp(back_keep, back_low)
PRECISE = lax.Precision.HIGHEST

def run_cells(projected, w_rec):

    def advance(state_pair, slot_proj):
        hidden, memory = state_pair
        gate_sum = low_back(slot_proj + jnp.einsum('bk,gkn->bgn', hidden, w_rec, precision=PRECISE))
        in_gate = jax.nn.sigmoid(gate_sum[:, 0])
        forget = jax.nn.sigmoid(gate_sum[:, 1])
        candidate = jnp.tanh(gate_sum[:, 2])
        out_gate = jax.nn.sigmoid(gate_sum[:, 3])
        memory = forget * memory + in_gate * candidate
        hidden = low(out_gate * jnp.tanh(memory))
        return ((hidden, memory), hidden)
    blank_state = jnp.zeros((projected.shape[1], projected.shape[3]), jnp.float32)
    ignored, states = lax.scan(advance, (blank_state, blank_state), projected)
    return states

def model_loss(char_table, w_in, w_rec, gate_bias, w_out, b_out, in_ids, targets, active):
    inputs = char_table[in_ids]
    projected = jnp.einsum('tbe,gen->tbgn', inputs, w_in, precision=PRECISE) + gate_bias
    states = run_cells(projected, w_rec)
    logits = jnp.einsum('tbk,kv->tbv', states, w_out, precision=PRECISE) + b_out
    logits = low_back(logits)
    normal_part = jax.nn.logsumexp(logits, axis=-1)
    picked = jnp.take_along_axis(logits, targets[..., None], axis=-1)[..., 0]
    return jnp.sum((normal_part - picked) * active)

def group_loss(weights, group_chars, group_prefix):
    char_table, w_in, w_rec, gate_bias, w_out, b_out = weights
    front_in = group_chars.T
    front_target = jnp.concatenate([group_chars[:, 1:], group_chars[:, :1]], axis=1).T
    timeline = jnp.arange(LENGTH, dtype=jnp.int32)[:, None]
    front_active = jnp.broadcast_to((timeline < LENGTH - 1).astype(jnp.float32), front_in.shape)
    reverse_steps = jnp.arange(PREFIX, dtype=jnp.int32)[:, None]
    back_in = jnp.take_along_axis(front_in, jnp.maximum(group_prefix[None, :] - 1 - reverse_steps, 0), axis=0)
    back_target = jnp.take_along_axis(front_in, jnp.maximum(group_prefix[None, :] - 2 - reverse_steps, 0), axis=0)
    back_active = (reverse_steps <= group_prefix[None, :] - 2).astype(jnp.float32)
    front_loss = model_loss(char_table[0], w_in[0], w_rec[0], gate_bias[0], w_out[0], b_out[0], front_in, front_target, front_active)
    back_loss = model_loss(char_table[1], w_in[1], w_rec[1], gate_bias[1], w_out[1], b_out[1], back_in, back_target, back_active)
    return (front_loss + back_loss) / math.sqrt(TOKENS)

def reference(char_ids, prefix, embedding, w_in, w_rec, gate_bias, w_out, b_out):
    weights = tuple((operand.astype(jnp.float32) for operand in (embedding, w_in, w_rec, gate_bias, w_out, b_out)))
    group_size = SEQ_DEV * N_SHARD
    grouped_chars = char_ids.reshape(N_REP, group_size, LENGTH)
    grouped_prefix = prefix.reshape(N_REP, group_size)

    def accumulate(summed, group_batch):
        chars_block, prefix_block = group_batch
        loss_value, pullback = jax.vjp(lambda *operands: group_loss(operands, chars_block, prefix_block), *weights)
        gradients = pullback(jnp.ones_like(loss_value))
        return (tuple((head_part + tail_part for head_part, tail_part in zip(summed, gradients))), None)
    start_sums = tuple((jnp.zeros_like(operand) for operand in weights))
    summed, ignored = lax.scan(accumulate, start_sums, (grouped_chars, grouped_prefix))
    return (summed[0], summed[1], summed[2], summed[3], summed[4], summed[5])
```

```python
import functools
import math

import jax
import jax.numpy as jnp
from jax import lax
from jax.experimental import pallas as pl
from jax.experimental.pallas import tpu as pltpu
from jax.sharding import PartitionSpec as P

PRECISE = lax.Precision.HIGHEST
MESH = pl.DeviceIdType.MESH
LANES = 128
MIB = 1 << 20


def one_hot(ids, width, out_type):
    return (ids[..., None] == jnp.arange(width, dtype=jnp.int32)).astype(out_type)


def loss_grad(logits, targets, active, factor):
    probabilities = jax.nn.softmax(logits, axis=-1)
    picked = one_hot(targets, logits.shape[-1], jnp.float32)
    return ((probabilities - picked) * (active * factor)[:, None]).astype(jnp.bfloat16)


def peers_of(place, count):
    if count == 4:
        return [place + 1 - 2 * lax.rem(place, 2), lax.rem(place + 2, 4), 3 - place]
    if count == 2:
        return [1 - place]
    assert count == 1
    return []


def greet(peers):
    barrier = pltpu.get_barrier_semaphore()
    for peer in peers:
        pl.semaphore_signal(barrier, inc=1, device_id={"shard": peer}, device_id_type=MESH)
    pl.semaphore_wait(barrier, len(peers))


def dot_plain(left, right):
    return jnp.dot(left, right, preferred_element_type=jnp.float32)


def dot_turned(left, right):
    return lax.dot_general(left, right, (((1,), (1,)), ((), ())), preferred_element_type=jnp.float32)


def forward_kernel(
    count,
    x_front,
    x_back,
    w_in,
    bias,
    w_hbm,
    full_front,
    full_back,
    acts_front,
    acts_back,
    cell_front,
    cell_back,
    weights,
    load_sem,
    send_sem,
    recv_sem,
):
    place = lax.axis_index("shard")
    peers = peers_of(place, count)
    units = weights.shape[3]
    length, half_len = full_front.shape[0], full_back.shape[0]
    loads = [pltpu.make_async_copy(w_hbm.at[m], weights.at[m], load_sem.at[m]) for m in range(2)]
    for load in loads:
        load.start()
    greet(peers)
    models = ((x_front, full_front, acts_front, cell_front), (x_back, full_back, acts_back, cell_back))

    def columns(owner):
        return pl.ds(pl.multiple_of(owner * units, units), units)

    def exchange(m, t, k):
        full = models[m][1]
        slot = lax.rem(t, 2)
        return pltpu.make_async_remote_copy(
            src_ref=full.at[t, :, columns(place)],
            dst_ref=full.at[t, :, columns(place)],
            send_sem=send_sem.at[m, slot, k],
            recv_sem=recv_sem.at[m, slot, k],
            device_id={"shard": peers[k]},
            device_id_type=MESH,
        )

    def finish(m, t, sums, memory, last):
        full, acts, cell = models[m][1:]
        in_gate = jax.nn.sigmoid(sums[0])
        forget = jax.nn.sigmoid(sums[1])
        candidate = jnp.tanh(sums[2])
        out_gate = jax.nn.sigmoid(sums[3])
        new_memory = in_gate * candidate if memory is None else forget * memory + in_gate * candidate
        full[t, :, columns(place)] = (out_gate * jnp.tanh(new_memory)).astype(jnp.bfloat16)
        for k in range(len(peers)):
            exchange(m, t, k).start()
        for g, value in enumerate((in_gate, forget, candidate, out_gate)):
            acts[t, g] = value
        cell[t] = new_memory

    def start_sums(m, t):
        x_t = models[m][0][t]
        return [bias[m, g] + dot_plain(x_t, w_in[m, g]) for g in range(4)]

    def add_chunk(m, t, owner, sums):
        part = models[m][1][t, :, columns(owner)]
        rows = columns(owner)
        return [sums[g] + dot_plain(part, weights[m, g, rows, :]) for g in range(4)]

    def advance(m, t):
        sums = add_chunk(m, t - 1, place, start_sums(m, t))
        for k in range(len(peers)):
            copy = exchange(m, t - 1, k)
            copy.wait_recv()
            sums = add_chunk(m, t - 1, peers[k], sums)
        for k in range(len(peers)):
            exchange(m, t - 1, k).wait_send()
        finish(m, t, sums, models[m][3][t - 1], False)

    finish(0, 0, start_sums(0, 0), None, False)
    finish(1, 0, start_sums(1, 0), None, False)
    for load in loads:
        load.wait()

    def both(t, carry):
        advance(0, t)
        advance(1, t)
        return carry

    def front_only(t, carry):
        advance(0, t)
        return carry

    lax.fori_loop(1, half_len, both, 0)
    lax.fori_loop(half_len, length, front_only, 0)
    for m, end in ((0, length), (1, half_len)):
        for k in range(len(peers)):
            copy = exchange(m, end - 1, k)
            copy.wait_send()
            copy.wait_recv()


def run_forward(count, x_front, x_back, w_in, bias, w_rec):
    length, rows = x_front.shape[:2]
    half_len = x_back.shape[0]
    units, shard_units = w_rec.shape[2:]
    vmem = pl.BlockSpec(memory_space=pltpu.VMEM)
    shape = jax.ShapeDtypeStruct
    return pl.pallas_call(
        functools.partial(forward_kernel, count),
        out_shape=(
            shape((length, rows, units), jnp.bfloat16),
            shape((half_len, rows, units), jnp.bfloat16),
            shape((length, 4, rows, shard_units), jnp.float32),
            shape((half_len, 4, rows, shard_units), jnp.float32),
            shape((length, rows, shard_units), jnp.float32),
            shape((half_len, rows, shard_units), jnp.float32),
        ),
        in_specs=[vmem] * 4 + [pl.BlockSpec(memory_space=pl.ANY)],
        out_specs=(vmem,) * 6,
        scratch_shapes=[
            pltpu.VMEM(w_rec.shape, jnp.bfloat16),
            pltpu.SemaphoreType.DMA((2,)),
            pltpu.SemaphoreType.DMA((2, 2, max(count - 1, 1))),
            pltpu.SemaphoreType.DMA((2, 2, max(count - 1, 1))),
        ],
        compiler_params=pltpu.CompilerParams(
            collective_id=0, has_side_effects=True, vmem_limit_bytes=56 * MIB
        ),
        name="recurrence_forward",
    )(x_front, x_back, w_in, bias, w_rec)


def backward_kernel(
    count,
    acts_front,
    acts_back,
    cell_front,
    cell_back,
    dec_front,
    dec_back,
    w_hbm,
    gates_front,
    gates_back,
    weights,
    outbox,
    inbox,
    own_part,
    cell_grad,
    load_sem,
    send_sem,
    recv_sem,
):
    place = lax.axis_index("shard")
    peers = peers_of(place, count)
    units = weights.shape[3]
    length, half_len = cell_front.shape[0], cell_back.shape[0]
    loads = [pltpu.make_async_copy(w_hbm.at[m], weights.at[m], load_sem.at[m]) for m in range(2)]
    for load in loads:
        load.start()
    greet(peers)
    models = (
        (acts_front, cell_front, dec_front, gates_front),
        (acts_back, cell_back, dec_back, gates_back),
    )

    def rows_of(owner):
        return pl.ds(pl.multiple_of(owner * units, units), units)

    def exchange(m, t, k):
        slot = lax.rem(t, 2)
        return pltpu.make_async_remote_copy(
            src_ref=outbox.at[m, slot, k],
            dst_ref=inbox.at[m, slot, k],
            send_sem=send_sem.at[m, slot, k],
            recv_sem=recv_sem.at[m, slot, k],
            device_id={"shard": peers[k]},
            device_id_type=MESH,
        )

    def gate_grads(m, t, grad_hidden, carried, prev_memory):
        acts, cell, dec, gates = models[m]
        in_gate, forget, candidate, out_gate = (acts[t, g] for g in range(4))
        squashed = jnp.tanh(cell[t])
        grad_memory = grad_hidden * out_gate * (1.0 - squashed * squashed)
        if carried is not None:
            grad_memory = carried + grad_memory
        cell_grad[m] = grad_memory * forget
        forget_part = jnp.zeros_like(grad_memory)
        if prev_memory is not None:
            forget_part = grad_memory * prev_memory * forget * (1.0 - forget)
        values = (
            grad_memory * candidate * in_gate * (1.0 - in_gate),
            forget_part,
            grad_memory * in_gate * (1.0 - candidate * candidate),
            grad_hidden * squashed * out_gate * (1.0 - out_gate),
        )
        narrow = [value.astype(jnp.bfloat16) for value in values]
        for g in range(4):
            gates[t, :, g * units : (g + 1) * units] = narrow[g]
        return narrow

    def product(m, narrow, owner):
        total = None
        for g in range(4):
            part = dot_turned(narrow[g], weights[m, g, rows_of(owner), :])
            total = part if total is None else total + part
        return total

    def send_products(m, t, narrow):
        for k in reversed(range(len(peers))):
            outbox[m, lax.rem(t, 2), k] = product(m, narrow, peers[k])
            exchange(m, t, k).start()
        own_part[m] = product(m, narrow, place)

    def incoming(m, t):
        total = models[m][2][t - 1] + own_part[m]
        for k in range(len(peers)):
            exchange(m, t, k).wait_recv()
            total = total + inbox[m, lax.rem(t, 2), k]
        for k in range(len(peers)):
            exchange(m, t, k).wait_send()
        return total

    def retreat(m, t):
        total = incoming(m, t + 1)
        narrow = gate_grads(m, t, total, cell_grad[m], models[m][1][t - 1])
        send_products(m, t, narrow)

    for m, end in ((0, length), (1, half_len)):
        t = end - 1
        narrow = gate_grads(m, t, models[m][2][t], None, models[m][1][t - 1])
        loads[m].wait()
        send_products(m, t, narrow)

    def both(step, carry):
        retreat(0, length - 1 - step)
        retreat(1, half_len - 1 - step)
        return carry

    def front_only(step, carry):
        retreat(0, length - 1 - step)
        return carry

    lax.fori_loop(1, half_len - 1, both, 0)
    retreat(0, length - half_len)
    gate_grads(1, 0, incoming(1, 1), cell_grad[1], None)
    lax.fori_loop(half_len, length - 1, front_only, 0)
    gate_grads(0, 0, incoming(0, 1), cell_grad[0], None)


def run_backward(count, acts, cells, decs, w_rec):
    length, rows, shard_units = cells[0].shape
    half_len = cells[1].shape[0]
    vmem = pl.BlockSpec(memory_space=pltpu.VMEM)
    shape = jax.ShapeDtypeStruct
    box = (2, 2, max(count - 1, 1), rows, shard_units)
    return pl.pallas_call(
        functools.partial(backward_kernel, count),
        out_shape=(
            shape((length, rows, 4 * shard_units), jnp.bfloat16),
            shape((half_len, rows, 4 * shard_units), jnp.bfloat16),
        ),
        in_specs=[vmem] * 6 + [pl.BlockSpec(memory_space=pl.ANY)],
        out_specs=(vmem,) * 2,
        scratch_shapes=[
            pltpu.VMEM(w_rec.shape, jnp.bfloat16),
            pltpu.VMEM(box, jnp.float32),
            pltpu.VMEM(box, jnp.float32),
            pltpu.VMEM((2, rows, shard_units), jnp.float32),
            pltpu.VMEM((2, rows, shard_units), jnp.float32),
            pltpu.SemaphoreType.DMA((2,)),
            pltpu.SemaphoreType.DMA(box[:3]),
            pltpu.SemaphoreType.DMA(box[:3]),
        ],
        compiler_params=pltpu.CompilerParams(
            collective_id=1, has_side_effects=True, vmem_limit_bytes=56 * MIB
        ),
        name="recurrence_backward",
    )(*acts, *cells, *decs, w_rec)


def shifted(values):
    return jnp.concatenate([jnp.zeros_like(values[:1]), values[:-1]], axis=0)


def shards(char_ids, prefix, embedding, w_in, w_rec, gate_bias, w_out, b_out):
    seq_dev, length = char_ids.shape
    half_len = length // 2
    vocab_size, embed = embedding.shape[1:]
    shard_units = w_rec.shape[3]
    count = lax.axis_size("shard")
    factor = 1.0 / math.sqrt(lax.axis_size("rep") * count * seq_dev * length)
    ids_and_prefix = jnp.concatenate([char_ids, prefix[:, None]], axis=1)
    gathered = lax.all_gather(ids_and_prefix, "shard", axis=0, tiled=True)
    group_chars, group_prefix = gathered[:, :length], gathered[:, length]
    full_out = lax.all_gather(w_out, "shard", axis=1, tiled=True)
    group_size = group_chars.shape[0]
    front_in = group_chars.T
    front_target = jnp.concatenate([group_chars[:, 1:], group_chars[:, :1]], axis=1).T
    timeline = jnp.arange(length, dtype=jnp.int32)[:, None]
    front_active = jnp.broadcast_to(
        (timeline < length - 1).astype(jnp.float32), (length, group_size)
    )
    reverse_steps = jnp.arange(half_len, dtype=jnp.int32)[:, None]

    def back_pick(offset):
        spot = jnp.maximum(group_prefix[None, :] - offset - reverse_steps, 0)
        chosen = one_hot(spot, length, jnp.int32) * group_chars[None]
        return jnp.sum(chosen, axis=-1)

    back_in = back_pick(1)
    back_target = back_pick(2)
    back_active = (reverse_steps <= group_prefix[None, :] - 2).astype(jnp.float32)
    depth = -(-embed // LANES) * LANES
    table = jnp.pad(embedding, ((0, 0), (0, 0), (0, depth - embed)))
    inputs = jnp.pad(w_in, ((0, 0), (0, 0), (0, depth - embed), (0, 0)))

    def look_up(ids, m):
        return jnp.einsum(
            "tbv,ve->tbe",
            one_hot(ids, vocab_size, jnp.bfloat16),
            table[m],
            preferred_element_type=jnp.float32,
        ).astype(jnp.bfloat16)

    front_x, back_x = look_up(front_in, 0), look_up(back_in, 1)
    bias_wide = gate_bias.astype(jnp.float32)[:, :, None, :]
    full_front, full_back, acts_front, acts_back, cell_front, cell_back = run_forward(
        count, front_x, back_x, inputs, bias_wide, w_rec
    )
    first_unit = lax.axis_index("shard") * shard_units

    def decode(full, m, target, active):
        rows = full.reshape(-1, full.shape[-1])
        logits = jnp.dot(rows, full_out[m], preferred_element_type=jnp.float32) + b_out[m].astype(
            jnp.float32
        )
        grad = loss_grad(logits, target.reshape(-1), active.reshape(-1), factor)
        dec = jnp.einsum("rv,kv->rk", grad, w_out[m], preferred_element_type=jnp.float32)
        own = lax.dynamic_slice_in_dim(rows, first_unit, shard_units, axis=1)
        out_grad = jnp.einsum("rk,rv->kv", own, grad, preferred_element_type=jnp.float32)
        bout = jnp.sum(grad, axis=0, dtype=jnp.float32)
        return dec.reshape(full.shape[0], group_size, shard_units), out_grad, bout

    front_dec, front_out_grad, front_bout = decode(full_front, 0, front_target, front_active)
    back_dec, back_out_grad, back_bout = decode(full_back, 1, back_target, back_active)
    out_sum, bout_sum = lax.psum(
        (jnp.stack([front_out_grad, back_out_grad]), jnp.stack([front_bout, back_bout])), "rep"
    )
    front_grads, back_grads = run_backward(
        count, (acts_front, acts_back), (cell_front, cell_back), (front_dec, back_dec), w_rec
    )
    front_grads = front_grads.reshape(length, group_size, 4, shard_units)
    back_grads = back_grads.reshape(half_len, group_size, 4, shard_units)
    prev_front, prev_back = shifted(full_front), shifted(full_back)
    front_rec_grad = jnp.einsum(
        "tbk,tbgn->gkn", prev_front, front_grads, preferred_element_type=jnp.float32
    )
    back_rec_grad = jnp.einsum(
        "tbk,tbgn->gkn", prev_back, back_grads, preferred_element_type=jnp.float32
    )
    rec_grad = lax.psum_scatter(
        jnp.stack([front_rec_grad, back_rec_grad]), "rep", scatter_dimension=2, tiled=True
    )
    front_x, back_x = front_x[..., :embed], back_x[..., :embed]
    in_grad = jnp.stack(
        [
            jnp.einsum("tbe,tbgn->gen", front_x, front_grads, preferred_element_type=jnp.float32),
            jnp.einsum("tbe,tbgn->gen", back_x, back_grads, preferred_element_type=jnp.float32),
        ]
    )
    bias_grad = jnp.stack(
        [
            jnp.sum(front_grads, axis=(0, 1), dtype=jnp.float32),
            jnp.sum(back_grads, axis=(0, 1), dtype=jnp.float32),
        ]
    )
    front_dx = jnp.einsum("tbgn,gen->tbe", front_grads, w_in[0], preferred_element_type=jnp.float32)
    back_dx = jnp.einsum("tbgn,gen->tbe", back_grads, w_in[1], preferred_element_type=jnp.float32)
    embed_grad = jnp.stack(
        [
            jnp.einsum(
                "tbv,tbe->ve",
                one_hot(front_in, vocab_size, jnp.float32),
                front_dx,
                precision=PRECISE,
            ),
            jnp.einsum(
                "tbv,tbe->ve", one_hot(back_in, vocab_size, jnp.float32), back_dx, precision=PRECISE
            ),
        ]
    )
    in_sum, bias_sum = lax.psum((in_grad, bias_grad), "rep")
    embed_sum = lax.psum(embed_grad, ("rep", "shard"))
    return (embed_sum, in_sum, rec_grad, bias_sum, out_sum, bout_sum)


def solution(mesh):
    in_specs = (
        P(("rep", "shard"), None),
        P(("rep", "shard")),
        P(),
        P(None, None, None, "shard"),
        P(None, None, None, "shard"),
        P(None, None, "shard"),
        P(None, "shard", None),
        P(),
    )
    out_specs = (
        P(),
        P(None, None, None, "shard"),
        P(None, None, "rep", "shard"),
        P(None, None, "shard"),
        P(None, "shard", None),
        P(),
    )
    return jax.shard_map(shards, mesh=mesh, in_specs=in_specs, out_specs=out_specs, check_vma=False)
```

```python
import functools
import math
import types

import jax
import jax.numpy as jnp
from jax import lax
from jax.experimental import pallas as pl
from jax.experimental.pallas import tpu as pltpu
from jax.sharding import PartitionSpec as P

PRECISE = lax.Precision.HIGHEST
MESH = pl.DeviceIdType.MESH
LANES = 128
MIB = 1 << 20
B16 = jnp.bfloat16
F32 = jnp.float32
VMEM = pl.BlockSpec(memory_space=pltpu.VMEM)
ANYWHERE = pl.BlockSpec(memory_space=pl.ANY)


def one_hot(ids, width, out_type):
    return (ids[..., None] == jnp.arange(width, dtype=jnp.int32)).astype(out_type)


def loss_grad(logits, targets, active, factor):
    probabilities = jax.nn.softmax(logits, axis=-1)
    picked = one_hot(targets, logits.shape[-1], F32)
    return ((probabilities - picked) * (active * factor)[:, None]).astype(B16)


def peers_of(place, count):
    if count == 4:
        return [place + 1 - 2 * lax.rem(place, 2), lax.rem(place + 2, 4), 3 - place]
    if count == 2:
        return [1 - place]
    assert count == 1
    return []


def others_of(group, groups):
    return [lax.rem(group + j, groups) for j in range(1, groups)]


def greet(peers, others):
    barrier = pltpu.get_barrier_semaphore()
    for peer in peers:
        pl.semaphore_signal(barrier, inc=1, device_id={"shard": peer}, device_id_type=MESH)
    for other in others:
        pl.semaphore_signal(barrier, inc=1, device_id={"rep": other}, device_id_type=MESH)
    pl.semaphore_wait(barrier, len(peers) + len(others))


def span(index, size):
    return pl.ds(pl.multiple_of(index * size, size), size)


def dot(left, right):
    return jnp.dot(left, right, preferred_element_type=F32)


def dot_last(left, right):
    return lax.dot_general(left, right, (((1,), (1,)), ((), ())), preferred_element_type=F32)


def dot_first(left, right):
    return lax.dot_general(left, right, (((0,), (0,)), ((), ())), preferred_element_type=F32)


def column_of(ids, spot):
    lane = lax.broadcasted_iota(jnp.int32, ids.shape, 1)
    return jnp.sum(jnp.where(lane == spot, ids, 0), axis=1, keepdims=True)


def marks(column, width):
    lane = lax.broadcasted_iota(jnp.int32, (column.shape[0], width), 1)
    return (lane == column).astype(F32).astype(B16)


def id_column(ids, ends, m, t):
    return column_of(ids, t) if m == 0 else column_of(ids, jnp.maximum(ends - 1 - t, 0))


def split_three(value):
    first = value.astype(B16)
    rest = value - first.astype(F32)
    second = rest.astype(B16)
    return first, second, (rest - second.astype(F32)).astype(B16)


def call(body, name, ins, outs, scratch, collective_id, cost):
    names = [key for key, _, _ in ins] + [key for key, _, _, _ in outs] + [key for key, _ in scratch]

    def kernel(*refs):
        body(types.SimpleNamespace(**dict(zip(names, refs))))

    results = pl.pallas_call(
        kernel,
        out_shape=tuple(jax.ShapeDtypeStruct(shape, kind) for _, shape, kind, _ in outs),
        in_specs=[spec for _, _, spec in ins],
        out_specs=tuple(spec for _, _, _, spec in outs),
        scratch_shapes=[kind for _, kind in scratch],
        compiler_params=pltpu.CompilerParams(
            collective_id=collective_id, has_side_effects=True, vmem_limit_bytes=60 * MIB
        ),
        cost_estimate=pl.CostEstimate(flops=cost, bytes_accessed=50 * MIB, transcendentals=0),
        name=name,
    )(*[value for _, value, _ in ins])
    return types.SimpleNamespace(**dict(zip([key for key, _, _, _ in outs], results)))


def forward_body(count, groups, stream, length, r):
    place = lax.axis_index("shard")
    group = lax.axis_index("rep")
    peers = peers_of(place, count)
    others = others_of(group, groups) if stream else []
    units = r.weights.shape[3]
    half_len = length // 2
    seq_dev = r.own_ids.shape[0]
    loads = [pltpu.make_async_copy(r.w_rec.at[m], r.weights.at[m], r.load_sem.at[m]) for m in range(2)]
    for load in loads:
        load.start()
    r.id_blocks[group, place, :seq_dev] = r.own_ids[...]
    greet(peers, others)

    def id_copy(k):
        block = r.id_blocks.at[group, place]
        return pltpu.make_async_remote_copy(
            src_ref=block,
            dst_ref=block,
            send_sem=r.id_send.at[k],
            recv_sem=r.id_recv.at[k],
            device_id={"shard": peers[k]},
            device_id_type=MESH,
        )

    def id_spread(j, source):
        return pltpu.make_async_remote_copy(
            src_ref=r.id_blocks.at[group],
            dst_ref=r.id_blocks.at[source],
            send_sem=r.ids_send.at[j],
            recv_sem=r.ids_recv.at[j],
            device_id={"rep": others[j]},
            device_id_type=MESH,
        )

    for k in range(len(peers)):
        id_copy(k).start()
    fulls = (r.full_front, r.full_back)
    acts = (r.acts_front, r.acts_back)
    cells = (r.cell_front, r.cell_back)
    if stream:
        pasts = (r.past_front, r.past_back)
        wide = r.past_front.shape[3]
        r.blank[...] = jnp.zeros_like(r.blank)
        blanks = [pltpu.make_async_copy(r.blank, pasts[m].at[0], r.past_local.at[m]) for m in range(2)]
        for copy in blanks:
            copy.start()

    def spread(m, t):
        if not stream:
            return
        for j, other in enumerate(others):
            pltpu.make_async_remote_copy(
                src_ref=fulls[m].at[t, :, span(other // 2, wide)],
                dst_ref=pasts[m].at[t + 1, group],
                send_sem=r.past_send.at[m, j],
                recv_sem=r.past_recv.at[m, j],
                device_id={"rep": other},
                device_id_type=MESH,
            ).start()
        pltpu.make_async_copy(
            fulls[m].at[t, :, span(group // 2, wide)], pasts[m].at[t + 1, group], r.past_local.at[m]
        ).start()

    def finish_spread(m, steps):
        if not stream:
            return
        for j, other in enumerate(others):
            whole = pltpu.make_async_remote_copy(
                src_ref=pasts[m].at[pl.ds(1, steps), 0],
                dst_ref=pasts[m].at[pl.ds(1, steps), 0],
                send_sem=r.past_send.at[m, j],
                recv_sem=r.past_recv.at[m, j],
                device_id={"rep": other},
                device_id_type=MESH,
            )
            whole.wait_send()
            whole.wait_recv()
        mine = pasts[m].at[pl.ds(1, steps), 0]
        pltpu.make_async_copy(mine, mine, r.past_local.at[m]).wait()

    def exchange(m, t, k):
        slot = lax.rem(t, 2)
        own = fulls[m].at[t, :, span(place, units)]
        return pltpu.make_async_remote_copy(
            src_ref=own,
            dst_ref=own,
            send_sem=r.send_sem.at[m, slot, k],
            recv_sem=r.recv_sem.at[m, slot, k],
            device_id={"shard": peers[k]},
            device_id_type=MESH,
        )

    def finish(m, t, sums, memory):
        in_gate = jax.nn.sigmoid(sums[0])
        forget = jax.nn.sigmoid(sums[1])
        candidate = jnp.tanh(sums[2])
        out_gate = jax.nn.sigmoid(sums[3])
        new_memory = in_gate * candidate if memory is None else forget * memory + in_gate * candidate
        fulls[m][t, :, span(place, units)] = (out_gate * jnp.tanh(new_memory)).astype(B16)
        for k in reversed(range(len(peers))):
            exchange(m, t, k).start()
        for g, value in enumerate((in_gate, forget, candidate, out_gate)):
            acts[m][t, g] = value
        cells[m][t] = new_memory

    def start_sums(m, t):
        ids, ends = r.group_ids[...], r.group_ids[:, length : length + 1]
        spots = marks(id_column(ids, ends, m, t), r.table.shape[1])
        x_t = dot(spots, r.table[m]).astype(B16)
        return [r.bias[m, g : g + 1] + dot(x_t, r.w_in[m, g]) for g in range(4)]

    def add_chunk(m, t, owner, sums):
        part = fulls[m][t, :, span(owner, units)]
        return [sums[g] + dot(part, r.weights[m, g, span(owner, units), :]) for g in range(4)]

    def advance(m, t):
        sums = add_chunk(m, t - 1, place, start_sums(m, t))
        for k in range(len(peers)):
            exchange(m, t - 1, k).wait_recv()
            sums = add_chunk(m, t - 1, peers[k], sums)
        for k in range(len(peers)):
            exchange(m, t - 1, k).wait_send()
        finish(m, t, sums, cells[m][t - 1])
        spread(m, t - 1)

    def turn_copy(slot, m, g, p):
        return pltpu.make_async_copy(
            r.turned.at[slot],
            r.w_turned.at[m, span(g, units), span(p, units)],
            r.turn_sem.at[slot],
        )

    blocks = 8 * count

    def turn(block, slot):
        m, g, p = block // (4 * count), lax.rem(block // count, 4), lax.rem(block, count)

        @pl.when(block < blocks)
        def _():
            @pl.when(block >= 2)
            def _():
                turn_copy(slot, 0, 0, 0).wait()

            r.turned[slot] = r.weights[m, g, span(p, units), :].T
            turn_copy(slot, m, g, p).start()

    for k in range(len(peers)):
        id_copy(k).wait_send()
        id_copy(k).wait_recv()
    for s in range(count):
        r.group_ids[s * seq_dev : (s + 1) * seq_dev] = r.id_blocks[group, s, :seq_dev]
    for j in range(len(others)):
        id_spread(j, group).start()
    if stream:
        for copy in blanks:
            copy.wait()
    finish(0, 0, start_sums(0, 0), None)
    finish(1, 0, start_sums(1, 0), None)
    for load in loads:
        load.wait()

    def both(t, carry):
        advance(0, t)
        advance(1, t)
        return carry

    def front_only(t, carry):
        advance(0, t)
        turn(2 * (t - half_len), 0)
        turn(2 * (t - half_len) + 1, 1)
        return carry

    assert blocks <= 2 * (length - half_len)
    lax.fori_loop(1, half_len, both, 0)
    lax.fori_loop(half_len, length, front_only, 0)
    for m, end in ((0, length), (1, half_len)):
        for k in range(len(peers)):
            copy = exchange(m, end - 1, k)
            copy.wait_send()
            copy.wait_recv()
    for slot in range(2):
        turn_copy(slot, 0, 0, 0).wait()
    finish_spread(0, length - 1)
    finish_spread(1, half_len - 1)
    for j in range(len(others)):
        copy = id_spread(j, group)
        copy.wait_send()
        copy.wait_recv()
    if stream:
        r.every_ids[...] = r.id_blocks[:, :, :seq_dev].reshape(r.every_ids.shape)


def run_forward(count, groups, stream, length, own_ids, table, w_in, bias, w_rec):
    half_len = length // 2
    units, shard_units = w_rec.shape[2:]
    seq_dev = own_ids.shape[0]
    rows = seq_dev * count
    dma = pltpu.SemaphoreType.DMA
    links = max(count - 1, 1)
    ins = [
        ("own_ids", own_ids, VMEM),
        ("table", table, VMEM),
        ("w_in", w_in, VMEM),
        ("bias", bias, VMEM),
        ("w_rec", w_rec, ANYWHERE),
    ]
    outs = [
        ("full_front", (length, rows, units), B16, VMEM),
        ("full_back", (half_len, rows, units), B16, VMEM),
        ("acts_front", (length, 4, rows, shard_units), F32, VMEM),
        ("acts_back", (half_len, 4, rows, shard_units), F32, VMEM),
        ("cell_front", (length, rows, shard_units), F32, VMEM),
        ("cell_back", (half_len, rows, shard_units), F32, VMEM),
        ("group_ids", (rows, LANES), jnp.int32, VMEM),
        ("w_turned", (2, 4 * shard_units, units), B16, ANYWHERE),
    ]
    scratch = [
        ("weights", pltpu.VMEM(w_rec.shape, B16)),
        ("turned", pltpu.VMEM((2, shard_units, shard_units), B16)),
        ("id_blocks", pltpu.VMEM((groups, count, max(8, seq_dev), LANES), jnp.int32)),
        ("load_sem", dma((2,))),
        ("turn_sem", dma((2,))),
        ("send_sem", dma((2, 2, links))),
        ("recv_sem", dma((2, 2, links))),
        ("id_send", dma((links,))),
        ("id_recv", dma((links,))),
    ]
    if stream:
        wide = units // (groups // 2)
        outs += [
            ("past_front", (length, groups, rows, wide), B16, ANYWHERE),
            ("past_back", (half_len, groups, rows, wide), B16, ANYWHERE),
            ("every_ids", (groups * rows, LANES), jnp.int32, VMEM),
        ]
        scratch += [
            ("blank", pltpu.VMEM((groups, rows, wide), B16)),
            ("past_send", dma((2, groups - 1))),
            ("past_recv", dma((2, groups - 1))),
            ("past_local", dma((2,))),
            ("ids_send", dma((groups - 1,))),
            ("ids_recv", dma((groups - 1,))),
        ]
    body = functools.partial(forward_body, count, groups, stream, length)
    return call(body, "recurrence_forward", ins, outs, scratch, 0, 10**11)


def backward_body(count, groups, stream, r):
    place = lax.axis_index("shard")
    group = lax.axis_index("rep")
    core = lax.rem(group, 2)
    peers = peers_of(place, count)
    others = others_of(group, groups) if stream else []
    units = r.cell_front.shape[2]
    length, half_len = r.cell_front.shape[0], r.cell_back.shape[0]
    loads = [pltpu.make_async_copy(r.w_turned.at[m], r.weights.at[m], r.load_sem.at[m]) for m in range(2)]
    for load in loads:
        load.start()
    acts = (r.acts_front, r.acts_back)
    cells = (r.cell_front, r.cell_back)
    decs = (r.dec_front, r.dec_back)
    gates = (r.gates_front, r.gates_back)
    ends = (length, half_len)
    if stream:
        r.sums[...] = jnp.zeros_like(r.sums)
        r.rec_sums[...] = jnp.zeros_like(r.rec_sums)
        wides = (r.wide_front, r.wide_back)
        pasts = (r.past_front, r.past_back)
    greet(peers, others)

    def wide_copy(m, t, j):
        other = others[j]
        return pltpu.make_async_remote_copy(
            src_ref=gates[m].at[t, :, span(lax.rem(other, 2), 2 * units)],
            dst_ref=wides[m].at[t, group],
            send_sem=r.wide_send.at[m, j],
            recv_sem=r.wide_recv.at[m, t // 2],
            device_id={"rep": other},
            device_id_type=MESH,
        )

    def spread(m, t):
        if not stream:
            return
        for j in range(len(others)):
            wide_copy(m, t, j).start()
        pltpu.make_async_copy(
            gates[m].at[t, :, span(core, 2 * units)], wides[m].at[t, group], r.wide_local.at[m, t // 2]
        ).start()

    def arrive(m, pair):
        far = wides[m].at[pl.ds(2 * pair, 2), pl.ds(0, groups - 1)]
        pltpu.make_async_remote_copy(
            src_ref=far,
            dst_ref=far,
            send_sem=r.wide_send.at[m, 0],
            recv_sem=r.wide_recv.at[m, pair],
            device_id={"rep": others[0]},
            device_id_type=MESH,
        ).wait_recv()
        near = wides[m].at[pl.ds(2 * pair, 2), 0]
        pltpu.make_async_copy(near, near, r.wide_local.at[m, pair]).wait()

    def fetches(m, pair):
        slot = lax.rem(pair, 2)
        return (
            pltpu.make_async_copy(
                wides[m].at[pl.ds(2 * pair, 2)], r.wide_slot.at[m, slot], r.fetch_sem.at[m, slot, 0]
            ),
            pltpu.make_async_copy(
                pasts[m].at[pl.ds(2 * pair, 2)], r.past_slot.at[m, slot], r.fetch_sem.at[m, slot, 1]
            ),
        )

    def fetch(m, pair):
        arrive(m, pair)
        for copy in fetches(m, pair):
            copy.start()

    def accumulate(m, pair):
        slot = lax.rem(pair, 2)
        for copy in fetches(m, pair):
            copy.wait()
        dz = r.wide_slot[m, slot].reshape(-1, 2 * units)
        past = r.past_slot[m, slot].reshape(dz.shape[0], -1)
        r.rec_sums[m] += dot_first(past, dz)
        ids, stops = r.every_ids[...], r.every_ids[:, length : length + 1]
        spots = [marks(id_column(ids, stops, m, 2 * pair + i), r.sums.shape[1]) for i in range(2)]
        r.sums[m] += dot_first(jnp.concatenate(spots, axis=0), dz)

    def exchange(m, t, k):
        slot = lax.rem(t, 2)
        return pltpu.make_async_remote_copy(
            src_ref=r.outbox.at[m, slot, k],
            dst_ref=r.inbox.at[m, slot, k],
            send_sem=r.send_sem.at[m, slot, k],
            recv_sem=r.recv_sem.at[m, slot, k],
            device_id={"shard": peers[k]},
            device_id_type=MESH,
        )

    def gate_grads(m, t, grad_hidden, carried, prev_memory):
        in_gate, forget, candidate, out_gate = (acts[m][t, g] for g in range(4))
        squashed = jnp.tanh(cells[m][t])
        grad_memory = grad_hidden * out_gate * (1.0 - squashed * squashed)
        if carried is not None:
            grad_memory = carried + grad_memory
        r.cell_grad[m] = grad_memory * forget
        forget_part = jnp.zeros_like(grad_memory)
        if prev_memory is not None:
            forget_part = grad_memory * prev_memory * forget * (1.0 - forget)
        values = (
            grad_memory * candidate * in_gate * (1.0 - in_gate),
            forget_part,
            grad_memory * in_gate * (1.0 - candidate * candidate),
            grad_hidden * squashed * out_gate * (1.0 - out_gate),
        )
        for g, value in enumerate(values):
            gates[m][t, :, g * units : (g + 1) * units] = value.astype(B16)

    def product(m, t, owner):
        return dot(gates[m][t], r.weights[m, :, span(owner, units)])

    def send_products(m, t):
        for k in reversed(range(len(peers))):
            r.outbox[m, lax.rem(t, 2), k] = product(m, t, peers[k])
            exchange(m, t, k).start()
        r.own_part[m] = product(m, t, place)
        spread(m, t)

    def incoming(m, t):
        total = decs[m][t - 1] + r.own_part[m]
        for k in range(len(peers)):
            exchange(m, t, k).wait_recv()
            total = total + r.inbox[m, lax.rem(t, 2), k]
        for k in range(len(peers)):
            exchange(m, t, k).wait_send()
        return total

    def retreat(m, t):
        gate_grads(m, t, incoming(m, t + 1), r.cell_grad[m], cells[m][t - 1])
        send_products(m, t)

    def first(m):
        t = ends[m] - 1
        gate_grads(m, t, decs[m][t], None, cells[m][t - 1])
        loads[m].wait()
        send_products(m, t)

    def last(m):
        gate_grads(m, 0, incoming(m, 1), r.cell_grad[m], None)
        spread(m, 0)

    def lagged(work, m, step):
        if not stream:
            return
        pairs = ends[m] // 2

        @pl.when(jnp.logical_and(step >= 2, step < pairs + 2))
        def _():
            work(m, pairs + 1 - step)

    first(0)
    first(1)
    retreat(0, length - 2)
    retreat(1, half_len - 2)

    def both(step, carry):
        retreat(0, length - 1 - 2 * step)
        lagged(fetch, 0, step)
        retreat(1, half_len - 1 - 2 * step)
        lagged(fetch, 1, step)
        retreat(0, length - 2 - 2 * step)
        lagged(accumulate, 0, step)
        retreat(1, half_len - 2 - 2 * step)
        lagged(accumulate, 1, step)
        return carry

    def front_only(step, carry):
        retreat(0, length - 1 - 2 * step)
        lagged(fetch, 0, step)
        lagged(fetch, 1, step)
        retreat(0, length - 2 - 2 * step)
        lagged(accumulate, 0, step)
        lagged(accumulate, 1, step)
        return carry

    assert half_len % 2 == 0 and length == 2 * half_len
    turns = half_len // 2
    lax.fori_loop(1, turns - 1, both, 0)
    retreat(0, length - 1 - 2 * (turns - 1))
    lagged(fetch, 0, turns - 1)
    retreat(1, 1)
    lagged(fetch, 1, turns - 1)
    retreat(0, length - 2 * turns)
    lagged(accumulate, 0, turns - 1)
    last(1)
    lagged(accumulate, 1, turns - 1)
    lax.fori_loop(turns, 2 * turns - 1, front_only, 0)
    retreat(0, 1)
    lagged(fetch, 0, 2 * turns - 1)
    last(0)
    lagged(accumulate, 0, 2 * turns - 1)
    if not stream:
        return
    lagged(fetch, 0, 2 * turns)
    lagged(accumulate, 0, 2 * turns)
    lagged(fetch, 0, 2 * turns + 1)
    lagged(accumulate, 0, 2 * turns + 1)
    for m in range(2):
        for j, other in enumerate(others):
            part = wides[m].at[:, 0]
            pltpu.make_async_remote_copy(
                src_ref=part,
                dst_ref=part,
                send_sem=r.wide_send.at[m, j],
                recv_sem=r.wide_recv.at[m, 0],
                device_id={"rep": other},
                device_id_type=MESH,
            ).wait_send()
    sibling = group + 1 - 2 * core
    depth = r.rec_grad.shape[2]

    def swap(m, g, which, src, dst, sem):
        return (
            pltpu.make_async_remote_copy(
                src_ref=src(m, g, 1 - core),
                dst_ref=dst.at[m, 2 * core + g],
                send_sem=r.swap_send.at[which, m, g],
                recv_sem=r.swap_recv.at[which, m, g],
                device_id={"rep": sibling},
                device_id_type=MESH,
            ),
            pltpu.make_async_copy(
                src(m, g, core), dst.at[m, 2 * core + g], r.swap_local.at[which, m, g]
            ),
        )

    def rec_part(m, g, owner):
        return r.rec_sums.at[m, span(owner, depth), pl.ds(g * units, units)]

    def in_part(m, g, owner):
        return r.in_sums.at[m, g]

    swaps = []
    for m in range(2):
        for g in range(2):
            swaps += swap(m, g, 0, rec_part, r.rec_grad, None)
    for copy in swaps:
        copy.start()
    for m in range(2):
        embed_part = None
        in_sum = None
        for part in split_three(r.sums[m]):
            in_term = dot_first(r.table[m], part)
            embed_term = sum(
                dot_last(part[:, g * units : (g + 1) * units], r.w_pair[m, g]) for g in range(2)
            )
            in_sum = in_term if in_sum is None else in_sum + in_term
            embed_part = embed_term if embed_part is None else embed_part + embed_term
        for g in range(2):
            r.in_sums[m, g] = in_sum[:, g * units : (g + 1) * units]
        r.embed_part[m] = embed_part
    more = []
    for m in range(2):
        for g in range(2):
            more += swap(m, g, 1, in_part, r.in_grad, None)
    for copy in more:
        copy.start()
    rows = r.embed_half.shape[1]
    piece = rows // count

    def embed_swap(source, target, which, owner):
        return pltpu.make_async_remote_copy(
            src_ref=source.at[:, span(owner, rows)],
            dst_ref=target,
            send_sem=r.embed_send.at[which],
            recv_sem=r.embed_recv.at[which],
            device_id={"rep": sibling},
            device_id_type=MESH,
        )

    copy = embed_swap(r.embed_part, r.embed_half, 0, 1 - core)
    copy.start()
    copy.wait()
    r.embed_half[...] += r.embed_part[:, span(core, rows)]

    def embed_reduce(k):
        return pltpu.make_async_remote_copy(
            src_ref=r.embed_half.at[:, span(peers[k], piece)],
            dst_ref=r.embed_inbox.at[k],
            send_sem=r.reduce_send.at[k],
            recv_sem=r.reduce_recv.at[k],
            device_id={"shard": peers[k]},
            device_id_type=MESH,
        )

    def embed_gather(k):
        own = r.embed_full.at[:, pl.ds(pl.multiple_of(core * rows + place * piece, 8), piece)]
        return pltpu.make_async_remote_copy(
            src_ref=own,
            dst_ref=own,
            send_sem=r.gather_send.at[k],
            recv_sem=r.gather_recv.at[k],
            device_id={"shard": peers[k]},
            device_id_type=MESH,
        )

    for k in reversed(range(len(peers))):
        embed_reduce(k).start()
    total = r.embed_half[:, span(place, piece)]
    for k in range(len(peers)):
        embed_reduce(k).wait()
        total = total + r.embed_inbox[k]
    r.embed_full[:, pl.ds(pl.multiple_of(core * rows + place * piece, 8), piece)] = total
    for k in reversed(range(len(peers))):
        embed_gather(k).start()
    for k in range(len(peers)):
        embed_gather(k).wait()
    copy = pltpu.make_async_remote_copy(
        src_ref=r.embed_full.at[:, span(core, rows)],
        dst_ref=r.embed_full.at[:, span(core, rows)],
        send_sem=r.embed_send.at[1],
        recv_sem=r.embed_recv.at[1],
        device_id={"rep": sibling},
        device_id_type=MESH,
    )
    copy.start()
    copy.wait()
    for copy in swaps + more:
        copy.wait()


def run_backward(count, groups, stream, ran, decs, table, w_pair):
    length, rows, shard_units = ran.cell_front.shape
    half_len = ran.cell_back.shape[0]
    units = ran.w_turned.shape[2]
    links = max(count - 1, 1)
    dma = pltpu.SemaphoreType.DMA
    box = (2, 2, links, rows, shard_units)
    ins = [
        ("acts_front", ran.acts_front, VMEM),
        ("acts_back", ran.acts_back, VMEM),
        ("cell_front", ran.cell_front, VMEM),
        ("cell_back", ran.cell_back, VMEM),
        ("dec_front", decs[0], VMEM),
        ("dec_back", decs[1], VMEM),
        ("w_turned", ran.w_turned, ANYWHERE),
    ]
    gates = [
        ("gates_front", (length, rows, 4 * shard_units)),
        ("gates_back", (half_len, rows, 4 * shard_units)),
    ]
    scratch = [
        ("weights", pltpu.VMEM(ran.w_turned.shape, B16)),
        ("outbox", pltpu.VMEM(box, F32)),
        ("inbox", pltpu.VMEM(box, F32)),
        ("own_part", pltpu.VMEM((2, rows, shard_units), F32)),
        ("cell_grad", pltpu.VMEM((2, rows, shard_units), F32)),
        ("load_sem", dma((2,))),
        ("send_sem", dma(box[:3])),
        ("recv_sem", dma(box[:3])),
    ]
    if stream:
        wide = ran.past_front.shape[3]
        vocab, depth = table.shape[1:]
        reduced = -(-vocab // (16 * count)) * 8 * count
        padded = 2 * reduced
        table = jnp.pad(table, ((0, 0), (0, padded - vocab), (0, 0)))
        ins += [
            ("past_front", ran.past_front, ANYWHERE),
            ("past_back", ran.past_back, ANYWHERE),
            ("every_ids", ran.every_ids, VMEM),
            ("table", table, VMEM),
            ("w_pair", w_pair, VMEM),
        ]
        outs = [
            ("wide_front", (length, groups, rows, 2 * shard_units), B16, ANYWHERE),
            ("wide_back", (half_len, groups, rows, 2 * shard_units), B16, ANYWHERE),
            ("rec_grad", (2, 4, wide // 2, shard_units), F32, ANYWHERE),
            ("in_grad", (2, 4, depth, shard_units), F32, ANYWHERE),
            ("embed_full", (2, padded, depth), F32, VMEM),
        ]
        scratch += [(key, pltpu.VMEM(shape, B16)) for key, shape in gates]
        scratch += [
            ("sums", pltpu.VMEM((2, padded, 2 * shard_units), F32)),
            ("rec_sums", pltpu.VMEM((2, wide, 2 * shard_units), F32)),
            ("in_sums", pltpu.VMEM((2, 2, depth, shard_units), F32)),
            ("embed_part", pltpu.VMEM((2, padded, depth), F32)),
            ("embed_half", pltpu.VMEM((2, reduced, depth), F32)),
            ("embed_inbox", pltpu.VMEM((links, 2, reduced // count, depth), F32)),
            ("wide_slot", pltpu.VMEM((2, 2, 2, groups, rows, 2 * shard_units), B16)),
            ("past_slot", pltpu.VMEM((2, 2, 2, groups, rows, wide), B16)),
            ("wide_send", dma((2, groups - 1))),
            ("wide_recv", dma((2, length // 2))),
            ("wide_local", dma((2, length // 2))),
            ("fetch_sem", dma((2, 2, 2))),
            ("swap_send", dma((2, 2, 2))),
            ("swap_recv", dma((2, 2, 2))),
            ("swap_local", dma((2, 2, 2))),
            ("embed_send", dma((2,))),
            ("embed_recv", dma((2,))),
            ("reduce_send", dma((links,))),
            ("reduce_recv", dma((links,))),
            ("gather_send", dma((links,))),
            ("gather_recv", dma((links,))),
        ]
    else:
        outs = [(key, shape, B16, VMEM) for key, shape in gates]
    body = functools.partial(backward_body, count, groups, stream)
    return call(body, "recurrence_backward", ins, outs, scratch, 1, 10**11)


def shifted(values):
    return jnp.concatenate([jnp.zeros_like(values[:1]), values[:-1]], axis=0)


def reduced_grads(ran, gates, embedding, w_in, ids, group_size):
    embed = embedding.shape[2]

    def per_model(full, grads, ids, m):
        grads = grads.reshape(grads.shape[0], group_size, 4, -1)
        rec = jnp.einsum("tbk,tbgn->gkn", shifted(full), grads, preferred_element_type=F32)
        spots = one_hot(ids, embedding.shape[1], B16)
        x = jnp.einsum("tbv,ve->tbe", spots, embedding[m], preferred_element_type=F32).astype(B16)
        in_grad = jnp.einsum("tbe,tbgn->gen", x, grads, preferred_element_type=F32)
        bias = jnp.sum(grads, axis=(0, 1), dtype=F32)
        dx = jnp.einsum("tbgn,gen->tbe", grads, w_in[m], preferred_element_type=F32)
        embed_grad = jnp.einsum("tbv,tbe->ve", spots.astype(F32), dx, precision=PRECISE)
        return rec, in_grad, bias, embed_grad

    parts = (
        per_model(ran.full_front, gates.gates_front, ids[0], 0),
        per_model(ran.full_back, gates.gates_back, ids[1], 1),
    )
    rec, in_grad, bias, embed_grad = (jnp.stack(values) for values in zip(*parts))
    rec_grad = lax.psum_scatter(rec, "rep", scatter_dimension=2, tiled=True)
    in_sum, bias_sum = lax.psum((in_grad, bias), "rep")
    embed_sum = lax.psum(embed_grad, ("rep", "shard"))
    return embed_sum, in_sum, rec_grad, bias_sum


def shards(char_ids, prefix, embedding, w_in, w_rec, gate_bias, w_out, b_out):
    seq_dev, length = char_ids.shape
    half_len = length // 2
    vocab_size, embed = embedding.shape[1:]
    shard_units = w_rec.shape[3]
    count, groups = lax.axis_size("shard"), lax.axis_size("rep")
    stream = groups == 8
    group_size = seq_dev * count
    factor = 1.0 / math.sqrt(groups * count * seq_dev * length)
    own_ids = jnp.concatenate([char_ids, prefix[:, None]], axis=1)
    own_ids = jnp.pad(own_ids, ((0, 0), (0, LANES - length - 1)))
    full_out = lax.all_gather(w_out, "shard", axis=1, tiled=True)
    depth = -(-(embed + 1) // LANES) * LANES
    padded = -(-vocab_size // LANES) * LANES
    table = jnp.pad(embedding, ((0, 0), (0, 0), (0, 1)), constant_values=1)
    table = jnp.pad(table, ((0, 0), (0, padded - vocab_size), (0, depth - embed - 1)))
    inputs = jnp.pad(w_in, ((0, 0), (0, 0), (0, depth - embed), (0, 0)))
    ran = run_forward(
        count, groups, stream, length, own_ids, table, inputs, gate_bias.astype(F32), w_rec
    )
    group_chars, group_prefix = ran.group_ids[:, :length], ran.group_ids[:, length]
    front_in = group_chars.T
    front_target = jnp.concatenate([group_chars[:, 1:], group_chars[:, :1]], axis=1).T
    timeline = jnp.arange(length, dtype=jnp.int32)[:, None]
    front_active = jnp.broadcast_to((timeline < length - 1).astype(F32), (length, group_size))
    reverse_steps = jnp.arange(half_len, dtype=jnp.int32)[:, None]

    def back_pick(offset):
        spot = jnp.maximum(group_prefix[None, :] - offset - reverse_steps, 0)
        chosen = one_hot(spot, length, jnp.int32) * group_chars[None]
        return jnp.sum(chosen, axis=-1)

    back_target = back_pick(2)
    back_active = (reverse_steps <= group_prefix[None, :] - 2).astype(F32)
    first_unit = lax.axis_index("shard") * shard_units

    def decode(full, m, target, active):
        rows = full.reshape(-1, full.shape[-1])
        logits = dot(rows, full_out[m]) + b_out[m].astype(F32)
        grad = loss_grad(logits, target.reshape(-1), active.reshape(-1), factor)
        dec = dot_last(grad, w_out[m])
        own = lax.dynamic_slice_in_dim(rows, first_unit, shard_units, axis=1)
        out_grad = dot_first(own, grad)
        bout = jnp.sum(grad, axis=0, dtype=F32)
        return dec.reshape(full.shape[0], group_size, shard_units), out_grad, bout

    front_dec, front_out_grad, front_bout = decode(ran.full_front, 0, front_target, front_active)
    back_dec, back_out_grad, back_bout = decode(ran.full_back, 1, back_target, back_active)
    out_and_bout = jnp.stack(
        [
            jnp.concatenate([front_out_grad, front_bout[None]], axis=0),
            jnp.concatenate([back_out_grad, back_bout[None]], axis=0),
        ]
    )
    out_and_bout = lax.psum(out_and_bout, "rep")
    out_sum, bout_sum = out_and_bout[:, :shard_units], out_and_bout[:, shard_units]
    core = lax.rem(lax.axis_index("rep"), 2)
    w_pair = lax.dynamic_slice_in_dim(inputs, 2 * core, 2, axis=1)
    done = run_backward(
        count, groups, stream, ran, (front_dec, back_dec), table[:, :vocab_size], w_pair
    )
    if stream:
        in_sum, bias_sum = done.in_grad[:, :, :embed], done.in_grad[:, :, embed]
        embed_sum = done.embed_full[:, :vocab_size, :embed]
        rec_grad = done.rec_grad
    else:
        embed_sum, in_sum, rec_grad, bias_sum = reduced_grads(
            ran, done, embedding, w_in, (front_in, back_pick(1)), group_size
        )
    return (embed_sum, in_sum, rec_grad, bias_sum, out_sum, bout_sum)


def solution(mesh):
    in_specs = (
        P(("rep", "shard"), None),
        P(("rep", "shard")),
        P(),
        P(None, None, None, "shard"),
        P(None, None, None, "shard"),
        P(None, None, "shard"),
        P(None, "shard", None),
        P(),
    )
    out_specs = (
        P(),
        P(None, None, None, "shard"),
        P(None, None, "rep", "shard"),
        P(None, None, "shard"),
        P(None, "shard", None),
        P(),
    )
    return jax.shard_map(shards, mesh=mesh, in_specs=in_specs, out_specs=out_specs, check_vma=False)
```

```python
import functools
import math
import types

import jax
import jax.numpy as jnp
from jax import lax
from jax.experimental import pallas as pl
from jax.experimental.pallas import tpu as pltpu
from jax.sharding import PartitionSpec as P

PRECISE = lax.Precision.HIGHEST
MESH = pl.DeviceIdType.MESH
LANES = 128
MIB = 1 << 20
B16 = jnp.bfloat16
F32 = jnp.float32
VMEM = pl.BlockSpec(memory_space=pltpu.VMEM)
ANYWHERE = pl.BlockSpec(memory_space=pl.ANY)


def one_hot(ids, width, out_type):
    return (ids[..., None] == jnp.arange(width, dtype=jnp.int32)).astype(out_type)


def loss_grad(logits, targets, active, factor):
    probabilities = jax.nn.softmax(logits, axis=-1)
    picked = one_hot(targets, logits.shape[-1], F32)
    return ((probabilities - picked) * (active * factor)[:, None]).astype(B16)


def peers_of(place, count):
    if count == 4:
        return [place + 1 - 2 * lax.rem(place, 2), lax.rem(place + 2, 4), 3 - place]
    if count == 2:
        return [1 - place]
    assert count == 1
    return []


def others_of(group, groups):
    return [lax.rem(group + j, groups) for j in range(1, groups)]


def greet(peers, others):
    barrier = pltpu.get_barrier_semaphore()
    for peer in peers:
        pl.semaphore_signal(barrier, inc=1, device_id={"shard": peer}, device_id_type=MESH)
    for other in others:
        pl.semaphore_signal(barrier, inc=1, device_id={"rep": other}, device_id_type=MESH)
    pl.semaphore_wait(barrier, len(peers) + len(others))


def span(index, size):
    return pl.ds(pl.multiple_of(index * size, size), size)


def dot(left, right):
    return jnp.dot(left, right, preferred_element_type=F32)


def dot_last(left, right):
    return lax.dot_general(left, right, (((1,), (1,)), ((), ())), preferred_element_type=F32)


def dot_first(left, right):
    return lax.dot_general(left, right, (((0,), (0,)), ((), ())), preferred_element_type=F32)


def column_of(ids, spot):
    lane = lax.broadcasted_iota(jnp.int32, ids.shape, 1)
    return jnp.sum(jnp.where(lane == spot, ids, 0), axis=1, keepdims=True)


def marks(column, width):
    lane = lax.broadcasted_iota(jnp.int32, (column.shape[0], width), 1)
    return (lane == column).astype(F32).astype(B16)


def id_column(ids, ends, m, t):
    return column_of(ids, t) if m == 0 else column_of(ids, jnp.maximum(ends - 1 - t, 0))


def split_three(value):
    first = value.astype(B16)
    rest = value - first.astype(F32)
    second = rest.astype(B16)
    return first, second, (rest - second.astype(F32)).astype(B16)


def call(body, name, ins, outs, scratch, collective_id, cost):
    names = [key for key, _, _ in ins] + [key for key, _, _, _ in outs] + [key for key, _ in scratch]

    def kernel(*refs):
        body(types.SimpleNamespace(**dict(zip(names, refs))))

    results = pl.pallas_call(
        kernel,
        out_shape=tuple(jax.ShapeDtypeStruct(shape, kind) for _, shape, kind, _ in outs),
        in_specs=[spec for _, _, spec in ins],
        out_specs=tuple(spec for _, _, _, spec in outs),
        scratch_shapes=[kind for _, kind in scratch],
        compiler_params=pltpu.CompilerParams(
            collective_id=collective_id, has_side_effects=True, vmem_limit_bytes=60 * MIB
        ),
        cost_estimate=pl.CostEstimate(flops=cost, bytes_accessed=50 * MIB, transcendentals=0),
        name=name,
    )(*[value for _, value, _ in ins])
    return types.SimpleNamespace(**dict(zip([key for key, _, _, _ in outs], results)))


def forward_body(count, groups, stream, length, r):
    place = lax.axis_index("shard")
    group = lax.axis_index("rep")
    peers = peers_of(place, count)
    others = others_of(group, groups) if stream else []
    units = r.weights.shape[3]
    half_len = length // 2
    seq_dev = r.own_ids.shape[0]
    loads = [pltpu.make_async_copy(r.w_rec.at[m], r.weights.at[m], r.load_sem.at[m]) for m in range(2)]
    for load in loads:
        load.start()
    r.id_blocks[group, place, :seq_dev] = r.own_ids[...]
    greet(peers, others)

    def id_copy(k):
        block = r.id_blocks.at[group, place]
        return pltpu.make_async_remote_copy(
            src_ref=block,
            dst_ref=block,
            send_sem=r.id_send.at[k],
            recv_sem=r.id_recv.at[k],
            device_id={"shard": peers[k]},
            device_id_type=MESH,
        )

    def id_spread(j, source):
        return pltpu.make_async_remote_copy(
            src_ref=r.id_blocks.at[group],
            dst_ref=r.id_blocks.at[source],
            send_sem=r.ids_send.at[j],
            recv_sem=r.ids_recv.at[j],
            device_id={"rep": others[j]},
            device_id_type=MESH,
        )

    for k in range(len(peers)):
        id_copy(k).start()
    fulls = (r.full_front, r.full_back)
    acts = (r.acts_front, r.acts_back)
    cells = (r.cell_front, r.cell_back)
    if stream:
        pasts = (r.past_front, r.past_back)
        wide = r.past_front.shape[3]
        r.blank[...] = jnp.zeros_like(r.blank)
        blanks = [pltpu.make_async_copy(r.blank, pasts[m].at[0], r.past_local.at[m]) for m in range(2)]
        for copy in blanks:
            copy.start()

    def spread(m, t):
        if not stream:
            return
        for j, other in enumerate(others):
            pltpu.make_async_remote_copy(
                src_ref=fulls[m].at[t, :, span(other // 2, wide)],
                dst_ref=pasts[m].at[t + 1, group],
                send_sem=r.past_send.at[m, j],
                recv_sem=r.past_recv.at[m, j],
                device_id={"rep": other},
                device_id_type=MESH,
            ).start()
        pltpu.make_async_copy(
            fulls[m].at[t, :, span(group // 2, wide)], pasts[m].at[t + 1, group], r.past_local.at[m]
        ).start()

    def finish_spread(m, steps):
        if not stream:
            return
        for j, other in enumerate(others):
            whole = pltpu.make_async_remote_copy(
                src_ref=pasts[m].at[pl.ds(1, steps), 0],
                dst_ref=pasts[m].at[pl.ds(1, steps), 0],
                send_sem=r.past_send.at[m, j],
                recv_sem=r.past_recv.at[m, j],
                device_id={"rep": other},
                device_id_type=MESH,
            )
            whole.wait_send()
            whole.wait_recv()
        mine = pasts[m].at[pl.ds(1, steps), 0]
        pltpu.make_async_copy(mine, mine, r.past_local.at[m]).wait()

    def exchange(m, t, k):
        slot = lax.rem(t, 2)
        own = fulls[m].at[t, :, span(place, units)]
        return pltpu.make_async_remote_copy(
            src_ref=own,
            dst_ref=own,
            send_sem=r.send_sem.at[m, slot, k],
            recv_sem=r.recv_sem.at[m, slot, k],
            device_id={"shard": peers[k]},
            device_id_type=MESH,
        )

    def finish(m, t, sums, memory):
        in_gate = jax.nn.sigmoid(sums[0])
        forget = jax.nn.sigmoid(sums[1])
        candidate = jnp.tanh(sums[2])
        out_gate = jax.nn.sigmoid(sums[3])
        new_memory = in_gate * candidate if memory is None else forget * memory + in_gate * candidate
        fulls[m][t, :, span(place, units)] = (out_gate * jnp.tanh(new_memory)).astype(B16)
        for k in reversed(range(len(peers))):
            exchange(m, t, k).start()
        for g, value in enumerate((in_gate, forget, candidate, out_gate)):
            acts[m][t, g] = value
        cells[m][t] = new_memory

    def start_sums(m, t):
        ids, ends = r.group_ids[...], r.group_ids[:, length : length + 1]
        spots = marks(id_column(ids, ends, m, t), r.table.shape[1])
        x_t = dot(spots, r.table[m]).astype(B16)
        return [r.bias[m, g : g + 1] + dot(x_t, r.w_in[m, g]) for g in range(4)]

    def add_chunk(m, t, owner, sums):
        part = fulls[m][t, :, span(owner, units)]
        return [sums[g] + dot(part, r.weights[m, g, span(owner, units), :]) for g in range(4)]

    def advance(m, t):
        sums = add_chunk(m, t - 1, place, start_sums(m, t))
        for k in range(len(peers)):
            exchange(m, t - 1, k).wait_recv()
            sums = add_chunk(m, t - 1, peers[k], sums)
        for k in range(len(peers)):
            exchange(m, t - 1, k).wait_send()
        finish(m, t, sums, cells[m][t - 1])
        spread(m, t - 1)

    def turn_copy(slot, m, g, p):
        return pltpu.make_async_copy(
            r.turned.at[slot],
            r.w_turned.at[m, span(g, units), span(p, units)],
            r.turn_sem.at[slot],
        )

    blocks = 8 * count

    def turn(block, slot):
        m, g, p = block // (4 * count), lax.rem(block // count, 4), lax.rem(block, count)

        @pl.when(block < blocks)
        def _():
            @pl.when(block >= 2)
            def _():
                turn_copy(slot, 0, 0, 0).wait()

            r.turned[slot] = r.weights[m, g, span(p, units), :].T
            turn_copy(slot, m, g, p).start()

    for k in range(len(peers)):
        id_copy(k).wait_send()
        id_copy(k).wait_recv()
    for s in range(count):
        r.group_ids[s * seq_dev : (s + 1) * seq_dev] = r.id_blocks[group, s, :seq_dev]
    for j in range(len(others)):
        id_spread(j, group).start()
    if stream:
        for copy in blanks:
            copy.wait()
    finish(0, 0, start_sums(0, 0), None)
    finish(1, 0, start_sums(1, 0), None)
    for load in loads:
        load.wait()

    def both(t, carry):
        advance(0, t)
        advance(1, t)
        return carry

    def front_only(t, carry):
        advance(0, t)
        turn(2 * (t - half_len), 0)
        turn(2 * (t - half_len) + 1, 1)
        return carry

    assert blocks <= 2 * (length - half_len)
    lax.fori_loop(1, half_len, both, 0)
    lax.fori_loop(half_len, length, front_only, 0)
    for m, end in ((0, length), (1, half_len)):
        for k in range(len(peers)):
            copy = exchange(m, end - 1, k)
            copy.wait_send()
            copy.wait_recv()
    for slot in range(2):
        turn_copy(slot, 0, 0, 0).wait()
    finish_spread(0, length - 1)
    finish_spread(1, half_len - 1)
    for j in range(len(others)):
        copy = id_spread(j, group)
        copy.wait_send()
        copy.wait_recv()
    if stream:
        r.every_ids[...] = r.id_blocks[:, :, :seq_dev].reshape(r.every_ids.shape)


def run_forward(count, groups, stream, length, own_ids, table, w_in, bias, w_rec):
    half_len = length // 2
    units, shard_units = w_rec.shape[2:]
    seq_dev = own_ids.shape[0]
    rows = seq_dev * count
    dma = pltpu.SemaphoreType.DMA
    links = max(count - 1, 1)
    ins = [
        ("own_ids", own_ids, VMEM),
        ("table", table, VMEM),
        ("w_in", w_in, VMEM),
        ("bias", bias, VMEM),
        ("w_rec", w_rec, ANYWHERE),
    ]
    outs = [
        ("full_front", (length, rows, units), B16, VMEM),
        ("full_back", (half_len, rows, units), B16, VMEM),
        ("acts_front", (length, 4, rows, shard_units), F32, VMEM),
        ("acts_back", (half_len, 4, rows, shard_units), F32, VMEM),
        ("cell_front", (length, rows, shard_units), F32, VMEM),
        ("cell_back", (half_len, rows, shard_units), F32, VMEM),
        ("group_ids", (rows, LANES), jnp.int32, VMEM),
        ("w_turned", (2, 4 * shard_units, units), B16, ANYWHERE),
    ]
    scratch = [
        ("weights", pltpu.VMEM(w_rec.shape, B16)),
        ("turned", pltpu.VMEM((2, shard_units, shard_units), B16)),
        ("id_blocks", pltpu.VMEM((groups, count, max(8, seq_dev), LANES), jnp.int32)),
        ("load_sem", dma((2,))),
        ("turn_sem", dma((2,))),
        ("send_sem", dma((2, 2, links))),
        ("recv_sem", dma((2, 2, links))),
        ("id_send", dma((links,))),
        ("id_recv", dma((links,))),
    ]
    if stream:
        wide = units // (groups // 2)
        outs += [
            ("past_front", (length, groups, rows, wide), B16, ANYWHERE),
            ("past_back", (half_len, groups, rows, wide), B16, ANYWHERE),
            ("every_ids", (groups * rows, LANES), jnp.int32, VMEM),
        ]
        scratch += [
            ("blank", pltpu.VMEM((groups, rows, wide), B16)),
            ("past_send", dma((2, groups - 1))),
            ("past_recv", dma((2, groups - 1))),
            ("past_local", dma((2,))),
            ("ids_send", dma((groups - 1,))),
            ("ids_recv", dma((groups - 1,))),
        ]
    body = functools.partial(forward_body, count, groups, stream, length)
    return call(body, "recurrence_forward", ins, outs, scratch, 0, 10**11)


def backward_body(count, groups, stream, r):
    place = lax.axis_index("shard")
    group = lax.axis_index("rep")
    core = lax.rem(group, 2)
    peers = peers_of(place, count)
    others = others_of(group, groups) if stream else []
    units = r.cell_front.shape[2]
    length, half_len = r.cell_front.shape[0], r.cell_back.shape[0]
    loads = [pltpu.make_async_copy(r.w_turned.at[m], r.weights.at[m], r.load_sem.at[m]) for m in range(2)]
    for load in loads:
        load.start()
    acts = (r.acts_front, r.acts_back)
    cells = (r.cell_front, r.cell_back)
    decs = (r.dec_front, r.dec_back)
    gates = (r.gates_front, r.gates_back)
    ends = (length, half_len)
    if stream:
        r.sums[...] = jnp.zeros_like(r.sums)
        r.rec_sums[...] = jnp.zeros_like(r.rec_sums)
        wides = (r.wide_front, r.wide_back)
        pasts = (r.past_front, r.past_back)
    greet(peers, others)

    def wide_copy(m, t, j):
        other = others[j]
        return pltpu.make_async_remote_copy(
            src_ref=gates[m].at[t, :, span(lax.rem(other, 2), 2 * units)],
            dst_ref=wides[m].at[t, group],
            send_sem=r.wide_send.at[m, j],
            recv_sem=r.wide_recv.at[m, t // 2],
            device_id={"rep": other},
            device_id_type=MESH,
        )

    def spread(m, t):
        if not stream:
            return
        for j in range(len(others)):
            wide_copy(m, t, j).start()
        pltpu.make_async_copy(
            gates[m].at[t, :, span(core, 2 * units)], wides[m].at[t, group], r.wide_local.at[m, t // 2]
        ).start()

    def arrive(m, pair):
        far = wides[m].at[pl.ds(2 * pair, 2), pl.ds(0, groups - 1)]
        pltpu.make_async_remote_copy(
            src_ref=far,
            dst_ref=far,
            send_sem=r.wide_send.at[m, 0],
            recv_sem=r.wide_recv.at[m, pair],
            device_id={"rep": others[0]},
            device_id_type=MESH,
        ).wait_recv()
        near = wides[m].at[pl.ds(2 * pair, 2), 0]
        pltpu.make_async_copy(near, near, r.wide_local.at[m, pair]).wait()

    def fetches(m, pair):
        slot = lax.rem(pair, 2)
        return (
            pltpu.make_async_copy(
                wides[m].at[pl.ds(2 * pair, 2)], r.wide_slot.at[m, slot], r.fetch_sem.at[m, slot, 0]
            ),
            pltpu.make_async_copy(
                pasts[m].at[pl.ds(2 * pair, 2)], r.past_slot.at[m, slot], r.fetch_sem.at[m, slot, 1]
            ),
        )

    def fetch(m, pair):
        arrive(m, pair)
        for copy in fetches(m, pair):
            copy.start()

    def accumulate(m, pair):
        slot = lax.rem(pair, 2)
        for copy in fetches(m, pair):
            copy.wait()
        dz = r.wide_slot[m, slot].reshape(-1, 2 * units)
        past = r.past_slot[m, slot].reshape(dz.shape[0], -1)
        r.rec_sums[m] += dot_first(past, dz)
        ids, stops = r.every_ids[...], r.every_ids[:, length : length + 1]
        spots = [marks(id_column(ids, stops, m, 2 * pair + i), r.sums.shape[1]) for i in range(2)]
        r.sums[m] += dot_first(jnp.concatenate(spots, axis=0), dz)

    def box(side, m, t, k):
        slot = lax.rem(t, 2)
        if k == 0:
            return (r.outbox if side == 0 else r.inbox).at[m, slot]
        return (r.outbox_far if side == 0 else r.inbox_far).at[m, slot, k - 1]

    def exchange(m, t, k):
        slot = lax.rem(t, 2)
        return pltpu.make_async_remote_copy(
            src_ref=box(0, m, t, k),
            dst_ref=box(1, m, t, k),
            send_sem=r.send_sem.at[m, slot, k],
            recv_sem=r.recv_sem.at[m, slot, k],
            device_id={"shard": peers[k]},
            device_id_type=MESH,
        )

    def gate_grads(m, t, grad_hidden, carried, prev_memory):
        in_gate, forget, candidate, out_gate = (acts[m][t, g] for g in range(4))
        squashed = jnp.tanh(cells[m][t])
        grad_memory = grad_hidden * out_gate * (1.0 - squashed * squashed)
        if carried is not None:
            grad_memory = carried + grad_memory
        r.cell_grad[m] = grad_memory * forget
        forget_part = jnp.zeros_like(grad_memory)
        if prev_memory is not None:
            forget_part = grad_memory * prev_memory * forget * (1.0 - forget)
        values = (
            grad_memory * candidate * in_gate * (1.0 - in_gate),
            forget_part,
            grad_memory * in_gate * (1.0 - candidate * candidate),
            grad_hidden * squashed * out_gate * (1.0 - out_gate),
        )
        for g, value in enumerate(values):
            gates[m][t, :, g * units : (g + 1) * units] = value.astype(B16)

    def product(m, t, owner):
        return dot(gates[m][t], r.weights[m, :, span(owner, units)])

    def send_products(m, t):
        for k in reversed(range(len(peers))):
            target = box(0, m, t, k)
            target[...] = product(m, t, peers[k]).astype(target.dtype)
            exchange(m, t, k).start()
        r.own_part[m] = product(m, t, place)
        spread(m, t)

    def incoming(m, t):
        total = decs[m][t - 1] + r.own_part[m]
        for k in range(len(peers)):
            exchange(m, t, k).wait_recv()
            total = total + box(1, m, t, k)[...].astype(F32)
        return total

    def sent(m, t):
        for k in range(len(peers)):
            exchange(m, t, k).wait_send()

    def retreat(m, t):
        gate_grads(m, t, incoming(m, t + 1), r.cell_grad[m], cells[m][t - 1])
        send_products(m, t)
        sent(m, t + 1)

    def first(m):
        t = ends[m] - 1
        gate_grads(m, t, decs[m][t], None, cells[m][t - 1])
        loads[m].wait()
        send_products(m, t)

    def last(m):
        gate_grads(m, 0, incoming(m, 1), r.cell_grad[m], None)
        spread(m, 0)
        sent(m, 1)

    def lagged(work, m, step):
        if not stream:
            return
        if m == 0:
            pl.when(step >= 2)(lambda: work(0, length // 2 + 1 - step))
        else:
            ready = jnp.logical_and(step >= 3, lax.rem(step, 2) == 1)
            pl.when(ready)(lambda: work(1, half_len // 2 - 1 - (step - 3) // 2))

    assert half_len % 2 == 0 and length == 2 * half_len
    final = half_len - 1
    first(0)
    first(1)
    retreat(0, length - 2)

    def turn(step, carry):
        retreat(0, length - 1 - 2 * step)
        lagged(fetch, 0, step)
        lagged(fetch, 1, step)
        retreat(1, half_len - 1 - step)
        retreat(0, length - 2 - 2 * step)
        lagged(accumulate, 0, step)
        lagged(accumulate, 1, step)
        return carry

    lax.fori_loop(1, final, turn, 0)
    retreat(0, 1)
    lagged(fetch, 0, final)
    lagged(fetch, 1, final)
    last(1)
    last(0)
    if not stream:
        return
    fetch(0, 1)
    accumulate(0, 2)
    accumulate(1, 1)
    accumulate(0, 1)
    fetch(1, 0)
    fetch(0, 0)
    accumulate(1, 0)
    accumulate(0, 0)
    for m in range(2):
        for j, other in enumerate(others):
            part = wides[m].at[:, 0]
            pltpu.make_async_remote_copy(
                src_ref=part,
                dst_ref=part,
                send_sem=r.wide_send.at[m, j],
                recv_sem=r.wide_recv.at[m, 0],
                device_id={"rep": other},
                device_id_type=MESH,
            ).wait_send()
    sibling = group + 1 - 2 * core
    depth = r.rec_grad.shape[2]

    def swap(m, g, which, src, dst, sem):
        return (
            pltpu.make_async_remote_copy(
                src_ref=src(m, g, 1 - core),
                dst_ref=dst.at[m, 2 * core + g],
                send_sem=r.swap_send.at[which, m, g],
                recv_sem=r.swap_recv.at[which, m, g],
                device_id={"rep": sibling},
                device_id_type=MESH,
            ),
            pltpu.make_async_copy(
                src(m, g, core), dst.at[m, 2 * core + g], r.swap_local.at[which, m, g]
            ),
        )

    def rec_part(m, g, owner):
        return r.rec_sums.at[m, span(owner, depth), pl.ds(g * units, units)]

    def in_part(m, g, owner):
        return r.in_sums.at[m, g]

    swaps = []
    for m in range(2):
        for g in range(2):
            swaps += swap(m, g, 0, rec_part, r.rec_grad, None)
    for copy in swaps:
        copy.start()
    for m in range(2):
        embed_part = None
        in_sum = None
        for part in split_three(r.sums[m]):
            in_term = dot_first(r.table[m], part)
            embed_term = sum(
                dot_last(part[:, g * units : (g + 1) * units], r.w_pair[m, g]) for g in range(2)
            )
            in_sum = in_term if in_sum is None else in_sum + in_term
            embed_part = embed_term if embed_part is None else embed_part + embed_term
        for g in range(2):
            r.in_sums[m, g] = in_sum[:, g * units : (g + 1) * units]
        r.embed_part[m] = embed_part
    more = []
    for m in range(2):
        for g in range(2):
            more += swap(m, g, 1, in_part, r.in_grad, None)
    for copy in more:
        copy.start()
    rows = r.embed_half.shape[1]
    piece = rows // count

    def embed_swap(source, target, which, owner):
        return pltpu.make_async_remote_copy(
            src_ref=source.at[:, span(owner, rows)],
            dst_ref=target,
            send_sem=r.embed_send.at[which],
            recv_sem=r.embed_recv.at[which],
            device_id={"rep": sibling},
            device_id_type=MESH,
        )

    copy = embed_swap(r.embed_part, r.embed_half, 0, 1 - core)
    copy.start()
    copy.wait()
    r.embed_half[...] += r.embed_part[:, span(core, rows)]

    def embed_reduce(k):
        return pltpu.make_async_remote_copy(
            src_ref=r.embed_half.at[:, span(peers[k], piece)],
            dst_ref=r.embed_inbox.at[k],
            send_sem=r.reduce_send.at[k],
            recv_sem=r.reduce_recv.at[k],
            device_id={"shard": peers[k]},
            device_id_type=MESH,
        )

    def embed_gather(k):
        own = r.embed_full.at[:, pl.ds(pl.multiple_of(core * rows + place * piece, 8), piece)]
        return pltpu.make_async_remote_copy(
            src_ref=own,
            dst_ref=own,
            send_sem=r.gather_send.at[k],
            recv_sem=r.gather_recv.at[k],
            device_id={"shard": peers[k]},
            device_id_type=MESH,
        )

    for k in reversed(range(len(peers))):
        embed_reduce(k).start()
    total = r.embed_half[:, span(place, piece)]
    for k in range(len(peers)):
        embed_reduce(k).wait()
        total = total + r.embed_inbox[k]
    r.embed_full[:, pl.ds(pl.multiple_of(core * rows + place * piece, 8), piece)] = total
    for k in reversed(range(len(peers))):
        embed_gather(k).start()
    for k in range(len(peers)):
        embed_gather(k).wait()
    copy = pltpu.make_async_remote_copy(
        src_ref=r.embed_full.at[:, span(core, rows)],
        dst_ref=r.embed_full.at[:, span(core, rows)],
        send_sem=r.embed_send.at[1],
        recv_sem=r.embed_recv.at[1],
        device_id={"rep": sibling},
        device_id_type=MESH,
    )
    copy.start()
    copy.wait()
    for copy in swaps + more:
        copy.wait()


def run_backward(count, groups, stream, ran, decs, table, w_pair):
    length, rows, shard_units = ran.cell_front.shape
    half_len = ran.cell_back.shape[0]
    units = ran.w_turned.shape[2]
    links = max(count - 1, 1)
    dma = pltpu.SemaphoreType.DMA
    box = (2, 2, rows, shard_units)
    far_box = (2, 2, max(links - 1, 1), rows, shard_units)
    ins = [
        ("acts_front", ran.acts_front, VMEM),
        ("acts_back", ran.acts_back, VMEM),
        ("cell_front", ran.cell_front, VMEM),
        ("cell_back", ran.cell_back, VMEM),
        ("dec_front", decs[0], VMEM),
        ("dec_back", decs[1], VMEM),
        ("w_turned", ran.w_turned, ANYWHERE),
    ]
    gates = [
        ("gates_front", (length, rows, 4 * shard_units)),
        ("gates_back", (half_len, rows, 4 * shard_units)),
    ]
    scratch = [
        ("weights", pltpu.VMEM(ran.w_turned.shape, B16)),
        ("outbox", pltpu.VMEM(box, F32)),
        ("inbox", pltpu.VMEM(box, F32)),
        ("outbox_far", pltpu.VMEM(far_box, B16)),
        ("inbox_far", pltpu.VMEM(far_box, B16)),
        ("own_part", pltpu.VMEM((2, rows, shard_units), F32)),
        ("cell_grad", pltpu.VMEM((2, rows, shard_units), F32)),
        ("load_sem", dma((2,))),
        ("send_sem", dma((2, 2, links))),
        ("recv_sem", dma((2, 2, links))),
    ]
    if stream:
        wide = ran.past_front.shape[3]
        vocab, depth = table.shape[1:]
        reduced = -(-vocab // (16 * count)) * 8 * count
        padded = 2 * reduced
        table = jnp.pad(table, ((0, 0), (0, padded - vocab), (0, 0)))
        ins += [
            ("past_front", ran.past_front, ANYWHERE),
            ("past_back", ran.past_back, ANYWHERE),
            ("every_ids", ran.every_ids, VMEM),
            ("table", table, VMEM),
            ("w_pair", w_pair, VMEM),
        ]
        outs = [
            ("wide_front", (length, groups, rows, 2 * shard_units), B16, ANYWHERE),
            ("wide_back", (half_len, groups, rows, 2 * shard_units), B16, ANYWHERE),
            ("rec_grad", (2, 4, wide // 2, shard_units), F32, ANYWHERE),
            ("in_grad", (2, 4, depth, shard_units), F32, ANYWHERE),
            ("embed_full", (2, padded, depth), F32, VMEM),
        ]
        scratch += [(key, pltpu.VMEM(shape, B16)) for key, shape in gates]
        scratch += [
            ("sums", pltpu.VMEM((2, padded, 2 * shard_units), F32)),
            ("rec_sums", pltpu.VMEM((2, wide, 2 * shard_units), F32)),
            ("in_sums", pltpu.VMEM((2, 2, depth, shard_units), F32)),
            ("embed_part", pltpu.VMEM((2, padded, depth), F32)),
            ("embed_half", pltpu.VMEM((2, reduced, depth), F32)),
            ("embed_inbox", pltpu.VMEM((links, 2, reduced // count, depth), F32)),
            ("wide_slot", pltpu.VMEM((2, 2, 2, groups, rows, 2 * shard_units), B16)),
            ("past_slot", pltpu.VMEM((2, 2, 2, groups, rows, wide), B16)),
            ("wide_send", dma((2, groups - 1))),
            ("wide_recv", dma((2, length // 2))),
            ("wide_local", dma((2, length // 2))),
            ("fetch_sem", dma((2, 2, 2))),
            ("swap_send", dma((2, 2, 2))),
            ("swap_recv", dma((2, 2, 2))),
            ("swap_local", dma((2, 2, 2))),
            ("embed_send", dma((2,))),
            ("embed_recv", dma((2,))),
            ("reduce_send", dma((links,))),
            ("reduce_recv", dma((links,))),
            ("gather_send", dma((links,))),
            ("gather_recv", dma((links,))),
        ]
    else:
        outs = [(key, shape, B16, VMEM) for key, shape in gates]
    body = functools.partial(backward_body, count, groups, stream)
    return call(body, "recurrence_backward", ins, outs, scratch, 1, 10**11)


def shifted(values):
    return jnp.concatenate([jnp.zeros_like(values[:1]), values[:-1]], axis=0)


def reduced_grads(ran, gates, embedding, w_in, ids, group_size):
    embed = embedding.shape[2]

    def per_model(full, grads, ids, m):
        grads = grads.reshape(grads.shape[0], group_size, 4, -1)
        rec = jnp.einsum("tbk,tbgn->gkn", shifted(full), grads, preferred_element_type=F32)
        spots = one_hot(ids, embedding.shape[1], B16)
        x = jnp.einsum("tbv,ve->tbe", spots, embedding[m], preferred_element_type=F32).astype(B16)
        in_grad = jnp.einsum("tbe,tbgn->gen", x, grads, preferred_element_type=F32)
        bias = jnp.sum(grads, axis=(0, 1), dtype=F32)
        dx = jnp.einsum("tbgn,gen->tbe", grads, w_in[m], preferred_element_type=F32)
        embed_grad = jnp.einsum("tbv,tbe->ve", spots.astype(F32), dx, precision=PRECISE)
        return rec, in_grad, bias, embed_grad

    parts = (
        per_model(ran.full_front, gates.gates_front, ids[0], 0),
        per_model(ran.full_back, gates.gates_back, ids[1], 1),
    )
    rec, in_grad, bias, embed_grad = (jnp.stack(values) for values in zip(*parts))
    rec_grad = lax.psum_scatter(rec, "rep", scatter_dimension=2, tiled=True)
    in_sum, bias_sum = lax.psum((in_grad, bias), "rep")
    embed_sum = lax.psum(embed_grad, ("rep", "shard"))
    return embed_sum, in_sum, rec_grad, bias_sum


def shards(char_ids, prefix, embedding, w_in, w_rec, gate_bias, w_out, b_out):
    seq_dev, length = char_ids.shape
    half_len = length // 2
    vocab_size, embed = embedding.shape[1:]
    shard_units = w_rec.shape[3]
    count, groups = lax.axis_size("shard"), lax.axis_size("rep")
    stream = groups == 8
    group_size = seq_dev * count
    factor = 1.0 / math.sqrt(groups * count * seq_dev * length)
    own_ids = jnp.concatenate([char_ids, prefix[:, None]], axis=1)
    own_ids = jnp.pad(own_ids, ((0, 0), (0, LANES - length - 1)))
    full_out = lax.all_gather(w_out, "shard", axis=1, tiled=True)
    depth = -(-(embed + 1) // LANES) * LANES
    padded = -(-vocab_size // LANES) * LANES
    table = jnp.pad(embedding, ((0, 0), (0, 0), (0, 1)), constant_values=1)
    table = jnp.pad(table, ((0, 0), (0, padded - vocab_size), (0, depth - embed - 1)))
    inputs = jnp.pad(w_in, ((0, 0), (0, 0), (0, depth - embed), (0, 0)))
    ran = run_forward(
        count, groups, stream, length, own_ids, table, inputs, gate_bias.astype(F32), w_rec
    )
    group_chars, group_prefix = ran.group_ids[:, :length], ran.group_ids[:, length]
    front_in = group_chars.T
    front_target = jnp.concatenate([group_chars[:, 1:], group_chars[:, :1]], axis=1).T
    timeline = jnp.arange(length, dtype=jnp.int32)[:, None]
    front_active = jnp.broadcast_to((timeline < length - 1).astype(F32), (length, group_size))
    reverse_steps = jnp.arange(half_len, dtype=jnp.int32)[:, None]

    def back_pick(offset):
        spot = jnp.maximum(group_prefix[None, :] - offset - reverse_steps, 0)
        chosen = one_hot(spot, length, jnp.int32) * group_chars[None]
        return jnp.sum(chosen, axis=-1)

    back_target = back_pick(2)
    back_active = (reverse_steps <= group_prefix[None, :] - 2).astype(F32)
    first_unit = lax.axis_index("shard") * shard_units

    def decode(full, m, target, active):
        rows = full.reshape(-1, full.shape[-1])
        logits = dot(rows, full_out[m]) + b_out[m].astype(F32)
        grad = loss_grad(logits, target.reshape(-1), active.reshape(-1), factor)
        dec = dot_last(grad, w_out[m])
        own = lax.dynamic_slice_in_dim(rows, first_unit, shard_units, axis=1)
        out_grad = dot_first(own, grad)
        bout = jnp.sum(grad, axis=0, dtype=F32)
        return dec.reshape(full.shape[0], group_size, shard_units), out_grad, bout

    front_dec, front_out_grad, front_bout = decode(ran.full_front, 0, front_target, front_active)
    back_dec, back_out_grad, back_bout = decode(ran.full_back, 1, back_target, back_active)
    out_and_bout = jnp.stack(
        [
            jnp.concatenate([front_out_grad, front_bout[None]], axis=0),
            jnp.concatenate([back_out_grad, back_bout[None]], axis=0),
        ]
    )
    out_and_bout = lax.psum(out_and_bout, "rep")
    out_sum, bout_sum = out_and_bout[:, :shard_units], out_and_bout[:, shard_units]
    core = lax.rem(lax.axis_index("rep"), 2)
    w_pair = lax.dynamic_slice_in_dim(inputs, 2 * core, 2, axis=1)
    done = run_backward(
        count, groups, stream, ran, (front_dec, back_dec), table[:, :vocab_size], w_pair
    )
    if stream:
        in_sum, bias_sum = done.in_grad[:, :, :embed], done.in_grad[:, :, embed]
        embed_sum = done.embed_full[:, :vocab_size, :embed]
        rec_grad = done.rec_grad
    else:
        embed_sum, in_sum, rec_grad, bias_sum = reduced_grads(
            ran, done, embedding, w_in, (front_in, back_pick(1)), group_size
        )
    return (embed_sum, in_sum, rec_grad, bias_sum, out_sum, bout_sum)


def solution(mesh):
    in_specs = (
        P(("rep", "shard"), None),
        P(("rep", "shard")),
        P(),
        P(None, None, None, "shard"),
        P(None, None, None, "shard"),
        P(None, None, "shard"),
        P(None, "shard", None),
        P(),
    )
    out_specs = (
        P(),
        P(None, None, None, "shard"),
        P(None, None, "rep", "shard"),
        P(None, None, "shard"),
        P(None, "shard", None),
        P(),
    )
    return jax.shard_map(shards, mesh=mesh, in_specs=in_specs, out_specs=out_specs, check_vma=False)
```

```python
import functools
import math
import types

import jax
import jax.numpy as jnp
from jax import lax
from jax.experimental import pallas as pl
from jax.experimental.pallas import tpu as pltpu
from jax.sharding import PartitionSpec as P

PRECISE = lax.Precision.HIGHEST
MESH = pl.DeviceIdType.MESH
LANES = 128
MIB = 1 << 20
B16 = jnp.bfloat16
F32 = jnp.float32
VMEM = pl.BlockSpec(memory_space=pltpu.VMEM)
ANYWHERE = pl.BlockSpec(memory_space=pl.ANY)


def one_hot(ids, width, out_type):
    return (ids[..., None] == jnp.arange(width, dtype=jnp.int32)).astype(out_type)


def loss_grad(logits, targets, active, factor):
    probabilities = jax.nn.softmax(logits, axis=-1)
    picked = one_hot(targets, logits.shape[-1], F32)
    return ((probabilities - picked) * (active * factor)[:, None]).astype(B16)


def peers_of(place, count):
    if count == 4:
        return [place + 1 - 2 * lax.rem(place, 2), lax.rem(place + 2, 4), 3 - place]
    if count == 2:
        return [1 - place]
    assert count == 1
    return []


def others_of(group, groups):
    return [lax.rem(group + j, groups) for j in range(1, groups)]


def greet(peers, others):
    barrier = pltpu.get_barrier_semaphore()
    for peer in peers:
        pl.semaphore_signal(barrier, inc=1, device_id={"shard": peer}, device_id_type=MESH)
    for other in others:
        pl.semaphore_signal(barrier, inc=1, device_id={"rep": other}, device_id_type=MESH)
    pl.semaphore_wait(barrier, len(peers) + len(others))


def span(index, size):
    return pl.ds(pl.multiple_of(index * size, size), size)


def dot(left, right):
    return jnp.dot(left, right, preferred_element_type=F32)


def dot_last(left, right):
    return lax.dot_general(left, right, (((1,), (1,)), ((), ())), preferred_element_type=F32)


def dot_first(left, right):
    return lax.dot_general(left, right, (((0,), (0,)), ((), ())), preferred_element_type=F32)


def column_of(ids, spot):
    lane = lax.broadcasted_iota(jnp.int32, ids.shape, 1)
    return jnp.sum(jnp.where(lane == spot, ids, 0), axis=1, keepdims=True)


def marks(column, width):
    lane = lax.broadcasted_iota(jnp.int32, (column.shape[0], width), 1)
    return (lane == column).astype(F32).astype(B16)


def id_column(ids, ends, m, t):
    return column_of(ids, t) if m == 0 else column_of(ids, jnp.maximum(ends - 1 - t, 0))


def split_three(value):
    first = value.astype(B16)
    rest = value - first.astype(F32)
    second = rest.astype(B16)
    return first, second, (rest - second.astype(F32)).astype(B16)


def call(body, name, ins, outs, scratch, collective_id, cost):
    names = [*ins, *outs, *scratch]

    def kernel(*refs):
        body(types.SimpleNamespace(**dict(zip(names, refs))))

    results = pl.pallas_call(
        kernel,
        out_shape=tuple(jax.ShapeDtypeStruct(shape, kind) for shape, kind, _ in outs.values()),
        in_specs=[spec for _, spec in ins.values()],
        out_specs=tuple(spec for _, _, spec in outs.values()),
        scratch_shapes=list(scratch.values()),
        compiler_params=pltpu.CompilerParams(
            collective_id=collective_id, has_side_effects=True, vmem_limit_bytes=62 * MIB
        ),
        cost_estimate=pl.CostEstimate(flops=cost, bytes_accessed=50 * MIB, transcendentals=0),
        name=name,
    )(*[value for value, _ in ins.values()])
    return types.SimpleNamespace(**dict(zip(outs, results)))


def forward_body(count, length, r):
    place = lax.axis_index("shard")
    peers = peers_of(place, count)
    units = r.weights.shape[3]
    half_len = length // 2
    seq_dev = r.own_ids.shape[0]
    loads = [pltpu.make_async_copy(r.w_rec.at[m], r.weights.at[m], r.load_sem.at[m]) for m in range(2)]
    for load in loads:
        load.start()
    r.id_blocks[place, :seq_dev] = r.own_ids[...]
    greet(peers, [])

    def id_copy(k):
        block = r.id_blocks.at[place]
        return pltpu.make_async_remote_copy(
            src_ref=block,
            dst_ref=block,
            send_sem=r.id_send.at[k],
            recv_sem=r.id_recv.at[k],
            device_id={"shard": peers[k]},
            device_id_type=MESH,
        )

    for k in range(len(peers)):
        id_copy(k).start()
    fulls = (r.full_front, r.full_back)
    acts = (r.acts_front, r.acts_back)
    cells = (r.cell_front, r.cell_back)
    def exchange(m, t, k):
        slot = lax.rem(t, 2)
        own = fulls[m].at[t, :, span(place, units)]
        return pltpu.make_async_remote_copy(
            src_ref=own,
            dst_ref=own,
            send_sem=r.send_sem.at[m, slot, k],
            recv_sem=r.recv_sem.at[m, slot, k],
            device_id={"shard": peers[k]},
            device_id_type=MESH,
        )

    def finish(m, t, sums, memory):
        in_gate = jax.nn.sigmoid(sums[0])
        forget = jax.nn.sigmoid(sums[1])
        candidate = jnp.tanh(sums[2])
        out_gate = jax.nn.sigmoid(sums[3])
        new_memory = in_gate * candidate if memory is None else forget * memory + in_gate * candidate
        fulls[m][t, :, span(place, units)] = (out_gate * jnp.tanh(new_memory)).astype(B16)
        for k in reversed(range(len(peers))):
            exchange(m, t, k).start()
        for g, value in enumerate((in_gate, forget, candidate, out_gate)):
            acts[m][t, g] = value
        cells[m][t] = new_memory

    def start_sums(m, t):
        ids, ends = r.group_ids[...], r.group_ids[:, length : length + 1]
        spots = marks(id_column(ids, ends, m, t), r.table.shape[1])
        x_t = dot(spots, r.table[m]).astype(B16)
        return [r.bias[m, g : g + 1] + dot(x_t, r.w_in[m, g]) for g in range(4)]

    def add_chunk(m, t, owner, sums):
        part = fulls[m][t, :, span(owner, units)]
        return [sums[g] + dot(part, r.weights[m, g, span(owner, units), :]) for g in range(4)]

    def advance(m, t):
        sums = add_chunk(m, t - 1, place, start_sums(m, t))
        for k in range(len(peers)):
            exchange(m, t - 1, k).wait_recv()
            sums = add_chunk(m, t - 1, peers[k], sums)
        for k in range(len(peers)):
            exchange(m, t - 1, k).wait_send()
        finish(m, t, sums, cells[m][t - 1])

    def turn_copy(slot, m, g, p):
        return pltpu.make_async_copy(
            r.turned.at[slot],
            r.w_turned.at[m, span(g, units), span(p, units)],
            r.turn_sem.at[slot],
        )

    blocks = 8 * count

    def turn(block, slot):
        m, g, p = block // (4 * count), lax.rem(block // count, 4), lax.rem(block, count)

        @pl.when(block < blocks)
        def _():
            @pl.when(block >= 2)
            def _():
                turn_copy(slot, 0, 0, 0).wait()

            r.turned[slot] = r.weights[m, g, span(p, units), :].T
            turn_copy(slot, m, g, p).start()

    for k in range(len(peers)):
        id_copy(k).wait_send()
        id_copy(k).wait_recv()
    for s in range(count):
        r.group_ids[s * seq_dev : (s + 1) * seq_dev] = r.id_blocks[s, :seq_dev]
    finish(0, 0, start_sums(0, 0), None)
    finish(1, 0, start_sums(1, 0), None)
    for load in loads:
        load.wait()

    def both(t, carry):
        advance(0, t)
        advance(1, t)
        return carry

    def front_only(t, carry):
        advance(0, t)
        turn(2 * (t - half_len), 0)
        turn(2 * (t - half_len) + 1, 1)
        return carry

    assert blocks <= 2 * (length - half_len)
    lax.fori_loop(1, half_len, both, 0)
    lax.fori_loop(half_len, length, front_only, 0)
    for m, end in ((0, length), (1, half_len)):
        for k in range(len(peers)):
            copy = exchange(m, end - 1, k)
            copy.wait_send()
            copy.wait_recv()
    for slot in range(2):
        turn_copy(slot, 0, 0, 0).wait()


def run_forward(count, length, own_ids, table, w_in, bias, w_rec):
    half_len = length // 2
    units, shard_units = w_rec.shape[2:]
    seq_dev = own_ids.shape[0]
    rows = seq_dev * count
    dma = pltpu.SemaphoreType.DMA
    links = max(count - 1, 1)
    ins = dict(
        own_ids=(own_ids, VMEM),
        table=(table, VMEM),
        w_in=(w_in, VMEM),
        bias=(bias, VMEM),
        w_rec=(w_rec, ANYWHERE),
    )
    outs = dict(
        full_front=((length, rows, units), B16, VMEM),
        full_back=((half_len, rows, units), B16, VMEM),
        acts_front=((length, 4, rows, shard_units), F32, VMEM),
        acts_back=((half_len, 4, rows, shard_units), F32, VMEM),
        cell_front=((length, rows, shard_units), F32, VMEM),
        cell_back=((half_len, rows, shard_units), F32, VMEM),
        group_ids=((rows, LANES), jnp.int32, VMEM),
        w_turned=((2, 4 * shard_units, units), B16, ANYWHERE),
    )
    scratch = dict(
        weights=(pltpu.VMEM(w_rec.shape, B16)),
        turned=(pltpu.VMEM((2, shard_units, shard_units), B16)),
        id_blocks=(pltpu.VMEM((count, max(8, seq_dev), LANES), jnp.int32)),
        load_sem=(dma((2,))),
        turn_sem=(dma((2,))),
        send_sem=(dma((2, 2, links))),
        recv_sem=(dma((2, 2, links))),
        id_send=(dma((links,))),
        id_recv=(dma((links,))),
    )
    body = functools.partial(forward_body, count, length)
    return call(body, "recurrence_forward", ins, outs, scratch, 0, 10**11)


def backward_body(count, r):
    place = lax.axis_index("shard")
    peers = peers_of(place, count)
    units = r.cell_front.shape[2]
    length, half_len = r.cell_front.shape[0], r.cell_back.shape[0]
    loads = [pltpu.make_async_copy(r.w_turned.at[m], r.weights.at[m], r.load_sem.at[m]) for m in range(2)]
    for load in loads:
        load.start()
    acts = (r.acts_front, r.acts_back)
    cells = (r.cell_front, r.cell_back)
    decs = (r.dec_front, r.dec_back)
    gates = (r.gates_front, r.gates_back)
    ends = (length, half_len)
    greet(peers, [])

    def box(side, m, t, k):
        slot = lax.rem(t, 2)
        if k == 0:
            return (r.outbox if side == 0 else r.inbox).at[m, slot]
        return (r.outbox_far if side == 0 else r.inbox_far).at[m, slot, k - 1]

    def exchange(m, t, k):
        slot = lax.rem(t, 2)
        return pltpu.make_async_remote_copy(
            src_ref=box(0, m, t, k),
            dst_ref=box(1, m, t, k),
            send_sem=r.send_sem.at[m, slot, k],
            recv_sem=r.recv_sem.at[m, slot, k],
            device_id={"shard": peers[k]},
            device_id_type=MESH,
        )

    def gate_grads(m, t, grad_hidden, carried, prev_memory):
        in_gate, forget, candidate, out_gate = (acts[m][t, g] for g in range(4))
        squashed = jnp.tanh(cells[m][t])
        grad_memory = grad_hidden * out_gate * (1.0 - squashed * squashed)
        if carried is not None:
            grad_memory = carried + grad_memory
        r.cell_grad[m] = grad_memory * forget
        forget_part = jnp.zeros_like(grad_memory)
        if prev_memory is not None:
            forget_part = grad_memory * prev_memory * forget * (1.0 - forget)
        values = (
            grad_memory * candidate * in_gate * (1.0 - in_gate),
            forget_part,
            grad_memory * in_gate * (1.0 - candidate * candidate),
            grad_hidden * squashed * out_gate * (1.0 - out_gate),
        )
        for g, value in enumerate(values):
            gates[m][t, :, g * units : (g + 1) * units] = value.astype(B16)

    def product(m, t, owner):
        return dot(gates[m][t], r.weights[m, :, span(owner, units)])

    def send_products(m, t):
        for k in reversed(range(len(peers))):
            target = box(0, m, t, k)
            target[...] = product(m, t, peers[k]).astype(target.dtype)
            exchange(m, t, k).start()
        r.own_part[m] = product(m, t, place)

    def incoming(m, t):
        total = decs[m][t - 1] + r.own_part[m]
        for k in range(len(peers)):
            exchange(m, t, k).wait_recv()
            total = total + box(1, m, t, k)[...].astype(F32)
        return total

    def sent(m, t):
        for k in range(len(peers)):
            exchange(m, t, k).wait_send()

    def retreat(m, t):
        gate_grads(m, t, incoming(m, t + 1), r.cell_grad[m], cells[m][t - 1])
        send_products(m, t)
        sent(m, t + 1)

    def first(m):
        t = ends[m] - 1
        gate_grads(m, t, decs[m][t], None, cells[m][t - 1])
        loads[m].wait()
        send_products(m, t)

    def last(m):
        gate_grads(m, 0, incoming(m, 1), r.cell_grad[m], None)
        sent(m, 1)

    assert half_len % 2 == 0 and length == 2 * half_len
    final = half_len - 1
    first(0)
    first(1)
    retreat(0, length - 2)

    def turn(step, carry):
        retreat(0, length - 1 - 2 * step)
        retreat(1, half_len - 1 - step)
        retreat(0, length - 2 - 2 * step)
        return carry

    lax.fori_loop(1, final, turn, 0)
    retreat(0, 1)
    last(1)
    last(0)


def run_backward(count, ran, decs):
    length, rows, shard_units = ran.cell_front.shape
    half_len = ran.cell_back.shape[0]
    units = ran.w_turned.shape[2]
    links = max(count - 1, 1)
    dma = pltpu.SemaphoreType.DMA
    box = (2, 2, rows, shard_units)
    far_box = (2, 2, max(links - 1, 1), rows, shard_units)
    ins = dict(
        acts_front=(ran.acts_front, VMEM),
        acts_back=(ran.acts_back, VMEM),
        cell_front=(ran.cell_front, VMEM),
        cell_back=(ran.cell_back, VMEM),
        dec_front=(decs[0], VMEM),
        dec_back=(decs[1], VMEM),
        w_turned=(ran.w_turned, ANYWHERE),
    )
    gates = dict(
        gates_front=(length, rows, 4 * shard_units),
        gates_back=(half_len, rows, 4 * shard_units),
    )
    scratch = dict(
        weights=(pltpu.VMEM(ran.w_turned.shape, B16)),
        outbox=(pltpu.VMEM(box, F32)),
        inbox=(pltpu.VMEM(box, F32)),
        outbox_far=(pltpu.VMEM(far_box, B16)),
        inbox_far=(pltpu.VMEM(far_box, B16)),
        own_part=(pltpu.VMEM((2, rows, shard_units), F32)),
        cell_grad=(pltpu.VMEM((2, rows, shard_units), F32)),
        load_sem=(dma((2,))),
        send_sem=(dma((2, 2, links))),
        recv_sem=(dma((2, 2, links))),
    )
    outs = {key: (shape, B16, VMEM) for key, shape in gates.items()}
    body = functools.partial(backward_body, count)
    return call(body, "recurrence_backward", ins, outs, scratch, 1, 10**11)


def step_body(count, groups, factor, r):
    place = lax.axis_index("shard")
    group = lax.axis_index("rep")
    core = lax.rem(group, 2)
    sibling = group + 1 - 2 * core
    peers = peers_of(place, count)
    others = others_of(group, groups)
    units = r.weights.shape[3]
    length, half_len = r.full_front.shape[0], r.full_back.shape[0]
    ends = (length, half_len)
    rows = r.group_ids.shape[0]
    seq_dev = r.chars.shape[0]
    vocab, _, embed = r.embedding.shape
    wide = r.past_front.shape[3]
    fulls = (r.full_front, r.full_back)
    acts = (r.acts_front, r.acts_back)
    cells = (r.cell_front, r.cell_back)
    logit_grads = (r.logits_front, r.logits_back)
    pasts = (r.past_front, r.past_back)
    wides = (r.wide_front, r.wide_back)
    own_columns = span(place, units)

    inner = (place * (count - 1 - place)) // 2
    urgent = [
        (a + inner * (c - a), peers[a] + inner * (peers[c] - peers[a])) for a, c in ((2, 1), (1, 0), (0, 2))
    ]

    def to_peer(src, dst, send, recv, peer):
        return pltpu.make_async_remote_copy(
            src_ref=src,
            dst_ref=dst,
            send_sem=send,
            recv_sem=recv,
            device_id={"shard": peer},
            device_id_type=MESH,
        )

    def to_group(src, dst, send, recv, other):
        return pltpu.make_async_remote_copy(
            src_ref=src,
            dst_ref=dst,
            send_sem=send,
            recv_sem=recv,
            device_id={"rep": other},
            device_id_type=MESH,
        )

    loads = [pltpu.make_async_copy(r.w_rec.at[m], r.weights.at[m], r.load_sem.at[m]) for m in range(2)]
    for load in loads:
        load.start()
    barrier = pltpu.get_barrier_semaphore()
    for peer in peers:
        pl.semaphore_signal(barrier, inc=1, device_id={"shard": peer}, device_id_type=MESH)
    for other in others:
        pl.semaphore_signal(barrier, inc=1, device_id={"rep": other}, device_id_type=MESH)
    r.id_blocks[group, place, :seq_dev, :length] = r.chars[...]
    corner = (seq_dev, seq_dev)
    diagonal = lax.broadcasted_iota(jnp.int32, corner, 0) == lax.broadcasted_iota(jnp.int32, corner, 1)
    stops_across = jnp.broadcast_to(r.prefix[...], corner)
    r.id_blocks[group, place, :seq_dev, length : length + 1] = jnp.sum(
        jnp.where(diagonal, stops_across, 0), axis=1, keepdims=True
    )
    lane = lax.broadcasted_iota(jnp.int32, r.table.shape, 2)
    r.table[...] = jnp.where(lane == embed, 1.0, 0.0).astype(B16)
    r.inputs[...] = jnp.zeros_like(r.inputs)
    r.out_own[...] = jnp.zeros_like(r.out_own)
    for m in range(2):
        r.table[m, :vocab, :embed] = r.embedding[:, m, :]
        r.out_own[m, :vocab] = r.w_out[:, m, :]
        for g in range(4):
            r.inputs[m, g, :embed] = r.w_in[m, :, g, :]
    r.out_bias[...] = jnp.full_like(r.out_bias, -1e30)
    r.out_bias[:, :vocab] = r.b_out[...].astype(F32)
    share = units // groups
    for m in range(2):
        r.out_full[m, place] = r.out_own[m].T.reshape(groups, share, -1)
    r.blank[...] = jnp.zeros_like(r.blank)
    pl.semaphore_wait(barrier, len(peers) + len(others))

    def id_copy(k):
        block = r.id_blocks.at[group, place]
        return to_peer(block, block, r.id_send.at[k], r.id_recv.at[k], peers[k])

    def id_spread(j):
        block = r.id_blocks.at[group]
        return to_group(block, block, r.ids_send.at[j], r.ids_recv.at[j], others[j])

    for k in range(len(peers)):
        id_copy(k).start()
    blanks = [pltpu.make_async_copy(r.blank, pasts[m].at[0], r.past_local.at[m]) for m in range(2)]
    for copy in blanks:
        copy.start()
    r.in_sums[...] = jnp.zeros_like(r.in_sums)
    r.embed_part[...] = jnp.zeros_like(r.embed_part)
    r.rec_sums[...] = jnp.zeros_like(r.rec_sums)
    r.out_sums[...] = jnp.zeros_like(r.out_sums)

    def share_copy(n):
        k, m = len(peers) - 1 - n // 2, n % 2
        block = r.out_full.at[m, place, group]
        return to_peer(block, block, r.share_send.at[n], r.share_recv.at[n], peers[k])

    def share_spread(j, k):
        source = r.out_full.at[:, peers[k], group]
        other = lax.rem(group + 1 + j, groups)
        return to_group(source, source, r.all_send.at[j, k], r.all_recv.at[j, k], other)

    first_spread = 2 * len(peers) + 3

    def send_shares(t):
        for n in range(2 * len(peers)):
            pl.when(t == n + 1)(share_copy(n).start)

        @pl.when(t == first_spread - 1)
        def _():
            for n in range(2 * len(peers)):
                share_copy(n).wait()

        @pl.when(jnp.logical_and(t >= first_spread, t < first_spread + groups - 1))
        def _():
            for k in range(len(peers)):
                share_spread(t - first_spread, k).start()

    def spread_past(m, t):
        for j, other in enumerate(others):
            to_group(
                fulls[m].at[t, :, span(other // 2, wide)],
                pasts[m].at[t + 1, group],
                r.past_send.at[m, j],
                r.past_recv.at[m, j],
                other,
            ).start()
        pltpu.make_async_copy(
            fulls[m].at[t, :, span(group // 2, wide)], pasts[m].at[t + 1, group], r.past_local.at[m]
        ).start()

    def finish_past(m, steps):
        for j, other in enumerate(others):
            part = pasts[m].at[pl.ds(1, steps), 0]
            copy = to_group(part, part, r.past_send.at[m, j], r.past_recv.at[m, j], other)
            copy.wait_send()
            copy.wait_recv()
        mine = pasts[m].at[pl.ds(1, steps), 0]
        pltpu.make_async_copy(mine, mine, r.past_local.at[m]).wait()

    def exchange(m, t, k, peer):
        slot = lax.rem(t, 2)
        own = fulls[m].at[t, :, own_columns]
        return to_peer(own, own, r.hidden_send.at[m, slot, k], r.hidden_recv.at[m, slot, k], peer)

    def finish(m, t, sums, memory):
        in_gate = jax.nn.sigmoid(sums[0])
        forget = jax.nn.sigmoid(sums[1])
        candidate = jnp.tanh(sums[2])
        out_gate = jax.nn.sigmoid(sums[3])
        new_memory = in_gate * candidate if memory is None else forget * memory + in_gate * candidate
        fulls[m][t, :, own_columns] = (out_gate * jnp.tanh(new_memory)).astype(B16)
        for k, peer in urgent:
            exchange(m, t, k, peer).start()
        for g, value in enumerate((in_gate, forget, candidate, out_gate)):
            acts[m][t, g] = value
        cells[m][t] = new_memory

    def start_sums(m, t):
        ids, stops = r.group_ids[...], r.group_ids[:, length : length + 1]
        x_t = dot(marks(id_column(ids, stops, m, t), r.table.shape[1]), r.table[m]).astype(B16)
        return [
            r.gate_bias[m, g : g + 1, :].astype(F32) + dot(x_t, r.inputs[m, g]) for g in range(4)
        ]

    def add_chunk(m, t, owner, sums):
        part = fulls[m][t, :, span(owner, units)]
        return [sums[g] + dot(part, r.weights[m, g, span(owner, units), :]) for g in range(4)]

    def advance(m, t):
        sums = add_chunk(m, t - 1, place, start_sums(m, t))
        for k in range(len(peers)):
            exchange(m, t - 1, k, peers[k]).wait_recv()
            sums = add_chunk(m, t - 1, peers[k], sums)
        finish(m, t, sums, cells[m][t - 1])
        for k in range(len(peers)):
            exchange(m, t - 1, k, peers[k]).wait_send()
        spread_past(m, t - 1)

    def turn_block(m, g, p):
        r.weights[m, g, span(p, units), :] = r.weights[m, g, span(p, units), :].T

    stretch = 4

    def decode(m, chunk):
        t0 = stretch * chunk
        hidden = fulls[m][pl.ds(t0, stretch)].reshape(stretch * rows, count * units)
        logits = dot(hidden, r.out_full[m].reshape(count * units, -1)) + r.out_bias[m : m + 1, :]
        grown = jnp.exp(logits - jnp.max(logits, axis=1, keepdims=True))
        chances = grown / jnp.sum(grown, axis=1, keepdims=True)
        ids, stops = r.group_ids[...], r.group_ids[:, length : length + 1]
        targets, active = [], []
        for i in range(stretch):
            t = t0 + i
            if m == 0:
                targets.append(column_of(ids, lax.rem(t + 1, length)))
                live = jnp.full((rows, 1), t, jnp.int32) < length - 1
            else:
                targets.append(column_of(ids, jnp.maximum(stops - 2 - t, 0)))
                live = stops >= t + 2
            active.append(jnp.where(live, factor, 0.0).astype(F32))
        target, weight = jnp.concatenate(targets, axis=0), jnp.concatenate(active, axis=0)
        lane = lax.broadcasted_iota(jnp.int32, logits.shape, 1)
        picked = (lane == target).astype(F32)
        grad = ((chances - picked) * weight).astype(B16)
        logit_grads[m][pl.ds(t0, stretch)] = grad.reshape(stretch, rows, -1)
        own = fulls[m][pl.ds(t0, stretch), :, own_columns].reshape(stretch * rows, units)
        ones = jnp.ones((stretch * rows, LANES), B16)
        r.out_sums[m] += dot_first(grad, jnp.concatenate([own, ones], axis=1))

    piece = r.out_inbox.shape[2]

    def out_send(m, j):
        other = lax.rem(group + 1 + j, groups)
        return to_group(
            r.out_sums.at[m, span(other, piece)],
            r.out_inbox.at[m, j],
            r.out_send.at[m, j],
            r.out_recv.at[m, j],
            other,
        )

    def out_share(m, j):
        own = r.out_total.at[m, span(group, piece)]
        other = lax.rem(group + 1 + j, groups)
        return to_group(own, own, r.total_send.at[m, j], r.total_recv.at[m, j], other)

    def out_reduce(m):
        total = r.out_sums[m, span(group, piece)]
        for j in range(groups - 1):
            copy = out_send(m, j)
            copy.wait_send()
            copy.wait_recv()
        for j in range(groups - 1):
            total = total + r.out_inbox[m, j]
        r.out_total[m, span(group, piece)] = total

    def out_steps(m, n):
        pl.when(jnp.logical_and(n >= 0, n < groups - 1))(lambda: out_send(m, n).start())
        pl.when(n == groups)(lambda: out_reduce(m))
        ready = jnp.logical_and(n > groups, n < 2 * groups)
        pl.when(ready)(lambda: out_share(m, n - groups - 1).start())

    for k in range(len(peers)):
        id_copy(k).wait()
    for s in range(count):
        r.group_ids[s * seq_dev : (s + 1) * seq_dev] = r.id_blocks[group, s, :seq_dev]
    for j in range(len(others)):
        id_spread(j).start()
    for copy in blanks:
        copy.wait()
    for m in range(2):
        finish(m, 0, start_sums(m, 0), None)
    for load in loads:
        load.wait()

    def both(t, carry):
        advance(0, t)
        advance(1, t)
        send_shares(t)
        return carry

    back_chunks = half_len // stretch
    blocks = 4 * count
    assert half_len % stretch == 0 and length == 2 * half_len and half_len % 2 == 0
    assert first_spread + groups - 1 <= half_len and blocks <= half_len
    assert back_chunks + 2 * groups <= half_len

    def front_only(t, carry):
        advance(0, t)
        n = t - half_len
        pl.when(n < blocks)(lambda: turn_block(1, n // count, lax.rem(n, count)))
        pl.when(n < back_chunks)(lambda: decode(1, n))
        begun = n >= back_chunks
        early = jnp.logical_and(begun, stretch * (n - back_chunks + 1) <= t)
        late = jnp.logical_and(stretch * (n - back_chunks + 1) > t, lax.rem(t, stretch) == 0)
        pl.when(early)(lambda: decode(0, n - back_chunks))
        pl.when(jnp.logical_and(begun, late))(lambda: decode(0, t // stretch - 1))
        out_steps(1, n - back_chunks)
        return carry

    def settle(m):
        for k in range(len(peers)):
            exchange(m, ends[m] - 1, k, peers[k]).wait()

    lax.fori_loop(1, half_len, both, 0)
    settle(1)
    for j in range(groups - 1):
        for k in range(len(peers)):
            share_spread(j, k).wait()
    lax.fori_loop(half_len, length, front_only, 0)
    for g in range(4):
        for p in range(count):
            turn_block(0, g, p)
    settle(0)
    decode(0, length // stretch - 1)
    finish_past(0, length - 1)
    finish_past(1, half_len - 1)
    for j in range(len(others)):
        id_spread(j).wait()
    r.every_ids[...] = r.id_blocks[:, :, :seq_dev].reshape(r.every_ids.shape)

    gates = fulls

    def spread_gates(m, t):
        for j, other in enumerate(others):
            to_group(
                gates[m].at[t, :, span(lax.rem(other, 2), 2 * units)],
                wides[m].at[t, group],
                r.wide_send.at[m, j],
                r.wide_recv.at[m, t // 2],
                other,
            ).start()
        pltpu.make_async_copy(
            gates[m].at[t, :, span(core, 2 * units)], wides[m].at[t, group], r.wide_local.at[m, t // 2]
        ).start()

    def arrive(m, pair):
        far = wides[m].at[pl.ds(2 * pair, 2), pl.ds(0, groups - 1)]
        to_group(far, far, r.wide_send.at[m, 0], r.wide_recv.at[m, pair], others[0]).wait_recv()
        near = wides[m].at[pl.ds(2 * pair, 2), 0]
        pltpu.make_async_copy(near, near, r.wide_local.at[m, pair]).wait()

    def fetches(m, pair):
        slot = lax.rem(pair, 2)
        return (
            pltpu.make_async_copy(
                wides[m].at[pl.ds(2 * pair, 2)], r.wide_slot.at[m, slot], r.fetch_sem.at[m, slot, 0]
            ),
            pltpu.make_async_copy(
                pasts[m].at[pl.ds(2 * pair, 2)], r.past_slot.at[m, slot], r.fetch_sem.at[m, slot, 1]
            ),
        )

    def fetch(m, pair):
        arrive(m, pair)
        for copy in fetches(m, pair):
            copy.start()

    def accumulate(m, pair):
        slot = lax.rem(pair, 2)
        for copy in fetches(m, pair):
            copy.wait()
        dz = r.wide_slot[m, slot].reshape(-1, 2 * units)
        past = r.past_slot[m, slot].reshape(dz.shape[0], -1)
        r.rec_sums[m] += dot_first(past, dz)
        ids, stops = r.every_ids[...], r.every_ids[:, length : length + 1]
        spots = [marks(id_column(ids, stops, m, 2 * pair + i), r.table.shape[1]) for i in range(2)]
        spots = jnp.concatenate(spots, axis=0)
        r.in_sums[m] += dot_first(dot(spots, r.table[m]).astype(B16), dz)
        grad_x = None
        for g in range(2):
            term = dot_last(dz[:, g * units : (g + 1) * units], r.inputs[m, 2 * core + g])
            grad_x = term if grad_x is None else grad_x + term
        for part in split_three(grad_x):
            r.embed_part[m] += dot_first(spots, part)

    def give(m, t, k, peer):
        slot = lax.rem(t, 2)
        return to_peer(
            r.outbox.at[m, slot, k],
            r.inbox.at[m, slot, k],
            r.grad_send.at[m, slot, k],
            r.grad_recv.at[m, slot, k],
            peer,
        )

    def slopes(m, t, prev_memory):
        in_gate, forget, candidate, out_gate = (acts[m][t, g] for g in range(4))
        squashed = jnp.tanh(cells[m][t])
        forget_slope = jnp.zeros_like(forget)
        if prev_memory is not None:
            forget_slope = prev_memory * forget * (1.0 - forget)
        return (
            candidate * in_gate * (1.0 - in_gate),
            forget_slope,
            in_gate * (1.0 - candidate * candidate),
            squashed * out_gate * (1.0 - out_gate),
            out_gate * (1.0 - squashed * squashed),
            forget,
        )

    def gate_grads(m, t, slope, grad_hidden, carried):
        grad_memory = grad_hidden * slope[4]
        if carried is not None:
            grad_memory = carried + grad_memory
        values = [grad_memory * slope[g] for g in range(3)] + [grad_hidden * slope[3]]
        for g, value in enumerate(values):
            gates[m][t, :, g * units : (g + 1) * units] = value.astype(B16)
        r.cell_grad[m] = grad_memory * slope[5]

    def product(m, t, owner):
        total = None
        for g in range(4):
            part = dot(
                gates[m][t, :, g * units : (g + 1) * units], r.weights[m, g, span(owner, units), :]
            )
            total = part if total is None else total + part
        return total

    def from_decoder(m, t):
        return dot(logit_grads[m][t], r.out_own[m])

    def send_products(m, t):
        for k, peer in urgent:
            r.outbox[m, lax.rem(t, 2), k] = product(m, t, peer).astype(B16)
            give(m, t, k, peer).start()
        r.own_part[m] = product(m, t, place) + from_decoder(m, t - 1)
        spread_gates(m, t)

    def incoming(m, t):
        total = r.own_part[m]
        for k in range(len(peers)):
            give(m, t, k, peers[k]).wait_recv()
            total = total + r.inbox[m, lax.rem(t, 2), k].astype(F32)
        return total

    def sent(m, t):
        for k in range(len(peers)):
            give(m, t, k, peers[k]).wait_send()

    def retreat(m, t):
        slope = slopes(m, t, cells[m][t - 1])
        gate_grads(m, t, slope, incoming(m, t + 1), r.cell_grad[m])
        send_products(m, t)
        sent(m, t + 1)

    def first(m):
        t = ends[m] - 1
        gate_grads(m, t, slopes(m, t, cells[m][t - 1]), from_decoder(m, t), None)
        send_products(m, t)

    def last(m):
        slope = slopes(m, 0, None)
        gate_grads(m, 0, slope, incoming(m, 1), r.cell_grad[m])
        spread_gates(m, 0)
        sent(m, 1)

    def lagged(work, m, step):
        if m == 0:
            pl.when(step >= 2)(lambda: work(0, length // 2 + 1 - step))
        else:
            ready = jnp.logical_and(step >= 3, lax.rem(step, 2) == 1)
            pl.when(ready)(lambda: work(1, half_len // 2 - 1 - (step - 3) // 2))

    final = half_len - 1
    first(0)
    first(1)
    retreat(0, length - 2)

    def turn(step, carry):
        retreat(0, length - 1 - 2 * step)
        lagged(fetch, 0, step)
        lagged(fetch, 1, step)
        retreat(1, half_len - 1 - step)
        retreat(0, length - 2 - 2 * step)
        lagged(accumulate, 0, step)
        lagged(accumulate, 1, step)
        out_steps(0, step - 1)
        return carry

    lax.fori_loop(1, final, turn, 0)
    retreat(0, 1)
    lagged(fetch, 0, final)
    lagged(fetch, 1, final)
    last(1)
    last(0)
    fetch(0, 1)
    accumulate(0, 2)
    accumulate(1, 1)
    accumulate(0, 1)
    for m in range(2):
        for j in range(groups - 1):
            out_share(m, j).wait()
    for m in range(2):
        r.grad_out[:, m, :] = r.out_total[m, :vocab, :units]
        r.grad_bout[m : m + 1, :] = r.out_total[m, :, units:].T[:1, :vocab]
    fetch(1, 0)
    fetch(0, 0)
    accumulate(1, 0)
    accumulate(0, 0)

    depth = r.rec_grad.shape[2]
    kept = r.in_all.shape[2]

    def swap(m, g, i):
        source, target = (
            (r.rec_sums.at[m, span(1 - core, depth), pl.ds(g * units, units)], r.rec_grad),
            (r.in_sums.at[m, pl.ds(0, kept), pl.ds(g * units, units)], r.in_all),
        )[i]
        target = target.at[m, 2 * core + g]
        return to_group(source, target, r.swap_send.at[i, m, g], r.swap_recv.at[i, m, g], sibling)

    def keep(m, g):
        return pltpu.make_async_copy(
            r.rec_sums.at[m, span(core, depth), pl.ds(g * units, units)],
            r.rec_grad.at[m, 2 * core + g],
            r.keep_sem.at[m, g],
        )

    half = r.embed_half.shape[1]
    slice_rows = half // count
    pair_copy = to_group(
        r.embed_part.at[:, span(1 - core, half)],
        r.embed_half,
        r.embed_send.at[0],
        r.embed_recv.at[0],
        sibling,
    )
    cells_of = [(m, g) for m in range(2) for g in range(2)]
    for m, g in cells_of:
        swap(m, g, 1).start()
    pair_copy.start()
    for m, g in cells_of:
        swap(m, g, 0).start()
        keep(m, g).start()
        r.in_all[m, 2 * core + g] = r.in_sums[m, :kept, g * units : (g + 1) * units]
    pair_copy.wait()
    r.embed_half[...] += r.embed_part[:, span(core, half)]
    own_slice = r.embed_full.at[:, pl.ds(pl.multiple_of(core * half + place * slice_rows, 8), slice_rows)]

    def embed_reduce(k):
        return to_peer(
            r.embed_half.at[:, span(peers[k], slice_rows)],
            r.embed_inbox.at[k],
            r.reduce_send.at[k],
            r.reduce_recv.at[k],
            peers[k],
        )

    def embed_gather(k):
        return to_peer(own_slice, own_slice, r.gather_send.at[k], r.gather_recv.at[k], peers[k])

    for k in reversed(range(len(peers))):
        embed_reduce(k).start()
    total = r.embed_half[:, span(place, slice_rows)]
    for k in range(len(peers)):
        embed_reduce(k).wait()
        total = total + r.embed_inbox[k]
    own_slice[...] = total
    for k in reversed(range(len(peers))):
        embed_gather(k).start()
    for m, g in cells_of:
        swap(m, g, 1).wait()
    for m in range(2):
        for g in range(4):
            r.grad_in[m, :, g, :] = r.in_all[m, g, :embed]
    r.grad_bias[...] = r.in_all[:, :, embed, :]
    for m, g in cells_of:
        swap(m, g, 0).wait()
        keep(m, g).wait()
    for m in range(2):
        for j in range(groups - 1):
            part = wides[m].at[:, 0]
            to_group(part, part, r.wide_send.at[m, j], r.wide_recv.at[m, 0], others[j]).wait_send()
    for k in range(len(peers)):
        embed_gather(k).wait()
    whole_half = r.embed_full.at[:, span(core, half)]
    pair_copy = to_group(whole_half, whole_half, r.embed_send.at[1], r.embed_recv.at[1], sibling)
    pair_copy.start()
    pair_copy.wait()
    for m in range(2):
        r.grad_embed[:, m, :] = r.embed_full[m, :vocab, :embed]


def run_step(count, groups, factor, char_ids, prefix, embedding, w_in, w_rec, gate_bias, w_out, b_out):
    seq_dev, length = char_ids.shape
    half_len = length // 2
    units, shard_units = w_rec.shape[2:]
    vocab, embed = embedding.shape[1:]
    rows = seq_dev * count
    wide = units // (groups // 2)
    depth = -(-(embed + 1) // LANES) * LANES
    lanes = -(-vocab // LANES) * LANES
    reduced = -(-vocab // (16 * count)) * 8 * count
    padded = 2 * reduced
    piece = lanes // groups
    links = count - 1
    far = groups - 1
    dma = pltpu.SemaphoreType.DMA
    ins = dict(
        chars=(char_ids, VMEM),
        prefix=(prefix[None], VMEM),
        embedding=(embedding.transpose(1, 0, 2), VMEM),
        w_in=(w_in.transpose(0, 2, 1, 3), VMEM),
        gate_bias=(gate_bias, VMEM),
        w_out=(w_out.transpose(2, 0, 1), VMEM),
        b_out=(b_out, VMEM),
        w_rec=(w_rec, ANYWHERE),
    )
    outs = dict(
        grad_embed=((vocab, 2, embed), F32, VMEM),
        grad_in=((2, embed, 4, shard_units), F32, VMEM),
        rec_grad=((2, 4, wide // 2, shard_units), F32, ANYWHERE),
        grad_bias=((2, 4, shard_units), F32, VMEM),
        grad_out=((vocab, 2, shard_units), F32, VMEM),
        grad_bout=((2, vocab), F32, VMEM),
        past_front=((length, groups, rows, wide), B16, ANYWHERE),
        past_back=((half_len, groups, rows, wide), B16, ANYWHERE),
        wide_front=((length, groups, rows, 2 * shard_units), B16, ANYWHERE),
        wide_back=((half_len, groups, rows, 2 * shard_units), B16, ANYWHERE),
    )
    arrays = dict(
        weights=(w_rec.shape, B16),
        out_bias=((2, lanes), F32),
        out_full=((2, count, groups, shard_units // groups, lanes), B16),
        id_blocks=((groups, count, max(8, seq_dev), LANES), jnp.int32),
        group_ids=((rows, LANES), jnp.int32),
        every_ids=((groups * rows, LANES), jnp.int32),
        blank=((groups, rows, wide), B16),
        full_front=((length, rows, units), B16),
        full_back=((half_len, rows, units), B16),
        acts_front=((length, 4, rows, shard_units), F32),
        acts_back=((half_len, 4, rows, shard_units), F32),
        cell_front=((length, rows, shard_units), F32),
        cell_back=((half_len, rows, shard_units), F32),
        logits_front=((length, rows, lanes), B16),
        logits_back=((half_len, rows, lanes), B16),
        out_sums=((2, lanes, shard_units + LANES), F32),
        out_inbox=((2, far, piece, shard_units + LANES), F32),
        out_total=((2, lanes, shard_units + LANES), F32),
        outbox=((2, 2, links, rows, shard_units), B16),
        inbox=((2, 2, links, rows, shard_units), B16),
        own_part=((2, rows, shard_units), F32),
        cell_grad=((2, rows, shard_units), F32),
        rec_sums=((2, wide, 2 * shard_units), F32),
        in_sums=((2, depth, 2 * shard_units), F32),
        in_all=((2, 4, -(-(embed + 1) // 8) * 8, shard_units), F32),
        table=((2, padded, depth), B16),
        inputs=((2, 4, depth, shard_units), B16),
        out_own=((2, lanes, shard_units), B16),
        embed_part=((2, padded, depth), F32),
        embed_half=((2, reduced, depth), F32),
        embed_full=((2, padded, depth), F32),
        embed_inbox=((links, 2, reduced // count, depth), F32),
        wide_slot=((2, 2, 2, groups, rows, 2 * shard_units), B16),
        past_slot=((2, 2, 2, groups, rows, wide), B16),
    )
    semaphores = dict(
        load_sem=(2,),
        id_send=(links,),
        id_recv=(links,),
        ids_send=(far,),
        ids_recv=(far,),
        share_send=(2 * links,),
        share_recv=(2 * links,),
        all_send=(far, links),
        all_recv=(far, links),
        past_send=(2, far),
        past_recv=(2, far),
        past_local=(2,),
        hidden_send=(2, 2, links),
        hidden_recv=(2, 2, links),
        out_send=(2, far),
        out_recv=(2, far),
        total_send=(2, far),
        total_recv=(2, far),
        wide_send=(2, far),
        wide_recv=(2, length // 2),
        wide_local=(2, length // 2),
        fetch_sem=(2, 2, 2),
        grad_send=(2, 2, links),
        grad_recv=(2, 2, links),
        swap_send=(2, 2, 2),
        swap_recv=(2, 2, 2),
        keep_sem=(2, 2),
        embed_send=(2,),
        embed_recv=(2,),
        reduce_send=(links,),
        reduce_recv=(links,),
        gather_send=(links,),
        gather_recv=(links,),
    )
    scratch = {key: pltpu.VMEM(shape, kind) for key, (shape, kind) in arrays.items()}
    scratch |= {key: dma(shape) for key, shape in semaphores.items()}
    body = functools.partial(step_body, count, groups, factor)
    return call(body, "lstm_step", ins, outs, scratch, 2, 10**11)


def shifted(values):
    return jnp.concatenate([jnp.zeros_like(values[:1]), values[:-1]], axis=0)


def reduced_grads(ran, gates, embedding, w_in, ids, group_size):
    embed = embedding.shape[2]

    def per_model(full, grads, ids, m):
        grads = grads.reshape(grads.shape[0], group_size, 4, -1)
        rec = jnp.einsum("tbk,tbgn->gkn", shifted(full), grads, preferred_element_type=F32)
        spots = one_hot(ids, embedding.shape[1], B16)
        x = jnp.einsum("tbv,ve->tbe", spots, embedding[m], preferred_element_type=F32).astype(B16)
        in_grad = jnp.einsum("tbe,tbgn->gen", x, grads, preferred_element_type=F32)
        bias = jnp.sum(grads, axis=(0, 1), dtype=F32)
        dx = jnp.einsum("tbgn,gen->tbe", grads, w_in[m], preferred_element_type=F32)
        embed_grad = jnp.einsum("tbv,tbe->ve", spots.astype(F32), dx, precision=PRECISE)
        return rec, in_grad, bias, embed_grad

    parts = (
        per_model(ran.full_front, gates.gates_front, ids[0], 0),
        per_model(ran.full_back, gates.gates_back, ids[1], 1),
    )
    rec, in_grad, bias, embed_grad = (jnp.stack(values) for values in zip(*parts))
    rec_grad = lax.psum_scatter(rec, "rep", scatter_dimension=2, tiled=True)
    in_sum, bias_sum = lax.psum((in_grad, bias), "rep")
    embed_sum = lax.psum(embed_grad, ("rep", "shard"))
    return embed_sum, in_sum, rec_grad, bias_sum


def shards(char_ids, prefix, embedding, w_in, w_rec, gate_bias, w_out, b_out):
    seq_dev, length = char_ids.shape
    half_len = length // 2
    vocab_size, embed = embedding.shape[1:]
    shard_units = w_rec.shape[3]
    count, groups = lax.axis_size("shard"), lax.axis_size("rep")
    group_size = seq_dev * count
    factor = 1.0 / math.sqrt(groups * count * seq_dev * length)
    if groups == 8 and count == 4 and length == 48:
        done = run_step(
            count, groups, factor, char_ids, prefix, embedding, w_in, w_rec, gate_bias, w_out, b_out
        )
        return (
            done.grad_embed.transpose(1, 0, 2),
            done.grad_in.transpose(0, 2, 1, 3),
            done.rec_grad,
            done.grad_bias,
            done.grad_out.transpose(1, 2, 0),
            done.grad_bout,
        )
    own_ids = jnp.concatenate([char_ids, prefix[:, None]], axis=1)
    own_ids = jnp.pad(own_ids, ((0, 0), (0, LANES - length - 1)))
    full_out = lax.all_gather(w_out, "shard", axis=1, tiled=True)
    depth = -(-(embed + 1) // LANES) * LANES
    padded = -(-vocab_size // LANES) * LANES
    table = jnp.pad(embedding, ((0, 0), (0, 0), (0, 1)), constant_values=1)
    table = jnp.pad(table, ((0, 0), (0, padded - vocab_size), (0, depth - embed - 1)))
    inputs = jnp.pad(w_in, ((0, 0), (0, 0), (0, depth - embed), (0, 0)))
    ran = run_forward(count, length, own_ids, table, inputs, gate_bias.astype(F32), w_rec)
    group_chars, group_prefix = ran.group_ids[:, :length], ran.group_ids[:, length]
    front_in = group_chars.T
    front_target = jnp.concatenate([group_chars[:, 1:], group_chars[:, :1]], axis=1).T
    timeline = jnp.arange(length, dtype=jnp.int32)[:, None]
    front_active = jnp.broadcast_to((timeline < length - 1).astype(F32), (length, group_size))
    reverse_steps = jnp.arange(half_len, dtype=jnp.int32)[:, None]

    def back_pick(offset):
        spot = jnp.maximum(group_prefix[None, :] - offset - reverse_steps, 0)
        chosen = one_hot(spot, length, jnp.int32) * group_chars[None]
        return jnp.sum(chosen, axis=-1)

    back_target = back_pick(2)
    back_active = (reverse_steps <= group_prefix[None, :] - 2).astype(F32)
    first_unit = lax.axis_index("shard") * shard_units

    def decode(full, m, target, active):
        rows = full.reshape(-1, full.shape[-1])
        logits = dot(rows, full_out[m]) + b_out[m].astype(F32)
        grad = loss_grad(logits, target.reshape(-1), active.reshape(-1), factor)
        dec = dot_last(grad, w_out[m])
        own = lax.dynamic_slice_in_dim(rows, first_unit, shard_units, axis=1)
        out_grad = dot_first(own, grad)
        bout = jnp.sum(grad, axis=0, dtype=F32)
        return dec.reshape(full.shape[0], group_size, shard_units), out_grad, bout

    front_dec, front_out_grad, front_bout = decode(ran.full_front, 0, front_target, front_active)
    back_dec, back_out_grad, back_bout = decode(ran.full_back, 1, back_target, back_active)
    out_and_bout = jnp.stack(
        [
            jnp.concatenate([front_out_grad, front_bout[None]], axis=0),
            jnp.concatenate([back_out_grad, back_bout[None]], axis=0),
        ]
    )
    out_and_bout = lax.psum(out_and_bout, "rep")
    out_sum, bout_sum = out_and_bout[:, :shard_units], out_and_bout[:, shard_units]
    done = run_backward(count, ran, (front_dec, back_dec))
    embed_sum, in_sum, rec_grad, bias_sum = reduced_grads(
        ran, done, embedding, w_in, (front_in, back_pick(1)), group_size
    )
    return (embed_sum, in_sum, rec_grad, bias_sum, out_sum, bout_sum)


def solution(mesh):
    in_specs = (
        P(("rep", "shard"), None),
        P(("rep", "shard")),
        P(),
        P(None, None, None, "shard"),
        P(None, None, None, "shard"),
        P(None, None, "shard"),
        P(None, "shard", None),
        P(),
    )
    out_specs = (
        P(),
        P(None, None, None, "shard"),
        P(None, None, "rep", "shard"),
        P(None, None, "shard"),
        P(None, "shard", None),
        P(),
    )
    return jax.shard_map(shards, mesh=mesh, in_specs=in_specs, out_specs=out_specs, check_vma=False)
```

```python
import functools
import math
import types

import jax
import jax.numpy as jnp
from jax import lax
from jax.experimental import pallas as pl
from jax.experimental.pallas import tpu as pltpu
from jax.sharding import PartitionSpec as P

PRECISE = lax.Precision.HIGHEST
MESH = pl.DeviceIdType.MESH
LANES = 128
MIB = 1 << 20
B16 = jnp.bfloat16
F32 = jnp.float32
VMEM = pl.BlockSpec(memory_space=pltpu.VMEM)
ANYWHERE = pl.BlockSpec(memory_space=pl.ANY)


def one_hot(ids, width, out_type):
    return (ids[..., None] == jnp.arange(width, dtype=jnp.int32)).astype(out_type)


def loss_grad(logits, targets, active, factor):
    probabilities = jax.nn.softmax(logits, axis=-1)
    picked = one_hot(targets, logits.shape[-1], F32)
    return ((probabilities - picked) * (active * factor)[:, None]).astype(B16)


def peers_of(place, count):
    if count == 4:
        return [place + 1 - 2 * lax.rem(place, 2), lax.rem(place + 2, 4), 3 - place]
    if count == 2:
        return [1 - place]
    assert count == 1
    return []


def others_of(group, groups):
    return [lax.rem(group + j, groups) for j in range(1, groups)]


def greet(peers, others):
    barrier = pltpu.get_barrier_semaphore()
    for peer in peers:
        pl.semaphore_signal(barrier, inc=1, device_id={"shard": peer}, device_id_type=MESH)
    for other in others:
        pl.semaphore_signal(barrier, inc=1, device_id={"rep": other}, device_id_type=MESH)
    pl.semaphore_wait(barrier, len(peers) + len(others))


def span(index, size):
    return pl.ds(pl.multiple_of(index * size, size), size)


def dot(left, right):
    return jnp.dot(left, right, preferred_element_type=F32)


def dot_last(left, right):
    return lax.dot_general(left, right, (((1,), (1,)), ((), ())), preferred_element_type=F32)


def dot_first(left, right):
    return lax.dot_general(left, right, (((0,), (0,)), ((), ())), preferred_element_type=F32)


def column_of(ids, spot):
    lane = lax.broadcasted_iota(jnp.int32, ids.shape, 1)
    return jnp.sum(jnp.where(lane == spot, ids, 0), axis=1, keepdims=True)


def marks(column, width):
    lane = lax.broadcasted_iota(jnp.int32, (column.shape[0], width), 1)
    return (lane == column).astype(F32).astype(B16)


def id_column(ids, ends, m, t):
    return column_of(ids, t) if m == 0 else column_of(ids, jnp.maximum(ends - 1 - t, 0))


def split_three(value):
    first = value.astype(B16)
    rest = value - first.astype(F32)
    second = rest.astype(B16)
    return first, second, (rest - second.astype(F32)).astype(B16)


def call(body, name, ins, outs, scratch, collective_id, cost):
    names = [*ins, *outs, *scratch]

    def kernel(*refs):
        body(types.SimpleNamespace(**dict(zip(names, refs))))

    results = pl.pallas_call(
        kernel,
        out_shape=tuple(jax.ShapeDtypeStruct(shape, kind) for shape, kind, _ in outs.values()),
        in_specs=[spec for _, spec in ins.values()],
        out_specs=tuple(spec for _, _, spec in outs.values()),
        scratch_shapes=list(scratch.values()),
        compiler_params=pltpu.CompilerParams(
            collective_id=collective_id, has_side_effects=True, vmem_limit_bytes=62 * MIB
        ),
        cost_estimate=pl.CostEstimate(flops=cost, bytes_accessed=50 * MIB, transcendentals=0),
        name=name,
    )(*[value for value, _ in ins.values()])
    return types.SimpleNamespace(**dict(zip(outs, results)))


def forward_body(count, length, r):
    place = lax.axis_index("shard")
    peers = peers_of(place, count)
    units = r.weights.shape[3]
    half_len = length // 2
    seq_dev = r.own_ids.shape[0]
    loads = [pltpu.make_async_copy(r.w_rec.at[m], r.weights.at[m], r.load_sem.at[m]) for m in range(2)]
    for load in loads:
        load.start()
    r.id_blocks[place, :seq_dev] = r.own_ids[...]
    greet(peers, [])

    def id_copy(k):
        block = r.id_blocks.at[place]
        return pltpu.make_async_remote_copy(
            src_ref=block,
            dst_ref=block,
            send_sem=r.id_send.at[k],
            recv_sem=r.id_recv.at[k],
            device_id={"shard": peers[k]},
            device_id_type=MESH,
        )

    for k in range(len(peers)):
        id_copy(k).start()
    fulls = (r.full_front, r.full_back)
    acts = (r.acts_front, r.acts_back)
    cells = (r.cell_front, r.cell_back)
    def exchange(m, t, k):
        slot = lax.rem(t, 2)
        own = fulls[m].at[t, :, span(place, units)]
        return pltpu.make_async_remote_copy(
            src_ref=own,
            dst_ref=own,
            send_sem=r.send_sem.at[m, slot, k],
            recv_sem=r.recv_sem.at[m, slot, k],
            device_id={"shard": peers[k]},
            device_id_type=MESH,
        )

    def finish(m, t, sums, memory):
        in_gate = jax.nn.sigmoid(sums[0])
        forget = jax.nn.sigmoid(sums[1])
        candidate = jnp.tanh(sums[2])
        out_gate = jax.nn.sigmoid(sums[3])
        new_memory = in_gate * candidate if memory is None else forget * memory + in_gate * candidate
        fulls[m][t, :, span(place, units)] = (out_gate * jnp.tanh(new_memory)).astype(B16)
        for k in reversed(range(len(peers))):
            exchange(m, t, k).start()
        for g, value in enumerate((in_gate, forget, candidate, out_gate)):
            acts[m][t, g] = value
        cells[m][t] = new_memory

    def start_sums(m, t):
        ids, ends = r.group_ids[...], r.group_ids[:, length : length + 1]
        spots = marks(id_column(ids, ends, m, t), r.table.shape[1])
        x_t = dot(spots, r.table[m]).astype(B16)
        return [r.bias[m, g : g + 1] + dot(x_t, r.w_in[m, g]) for g in range(4)]

    def add_chunk(m, t, owner, sums):
        part = fulls[m][t, :, span(owner, units)]
        return [sums[g] + dot(part, r.weights[m, g, span(owner, units), :]) for g in range(4)]

    def advance(m, t):
        sums = add_chunk(m, t - 1, place, start_sums(m, t))
        for k in range(len(peers)):
            exchange(m, t - 1, k).wait_recv()
            sums = add_chunk(m, t - 1, peers[k], sums)
        for k in range(len(peers)):
            exchange(m, t - 1, k).wait_send()
        finish(m, t, sums, cells[m][t - 1])

    def turn_copy(slot, m, g, p):
        return pltpu.make_async_copy(
            r.turned.at[slot],
            r.w_turned.at[m, span(g, units), span(p, units)],
            r.turn_sem.at[slot],
        )

    blocks = 8 * count

    def turn(block, slot):
        m, g, p = block // (4 * count), lax.rem(block // count, 4), lax.rem(block, count)

        @pl.when(block < blocks)
        def _():
            @pl.when(block >= 2)
            def _():
                turn_copy(slot, 0, 0, 0).wait()

            r.turned[slot] = r.weights[m, g, span(p, units), :].T
            turn_copy(slot, m, g, p).start()

    for k in range(len(peers)):
        id_copy(k).wait_send()
        id_copy(k).wait_recv()
    for s in range(count):
        r.group_ids[s * seq_dev : (s + 1) * seq_dev] = r.id_blocks[s, :seq_dev]
    finish(0, 0, start_sums(0, 0), None)
    finish(1, 0, start_sums(1, 0), None)
    for load in loads:
        load.wait()

    def both(t, carry):
        advance(0, t)
        advance(1, t)
        return carry

    def front_only(t, carry):
        advance(0, t)
        turn(2 * (t - half_len), 0)
        turn(2 * (t - half_len) + 1, 1)
        return carry

    assert blocks <= 2 * (length - half_len)
    lax.fori_loop(1, half_len, both, 0)
    lax.fori_loop(half_len, length, front_only, 0)
    for m, end in ((0, length), (1, half_len)):
        for k in range(len(peers)):
            copy = exchange(m, end - 1, k)
            copy.wait_send()
            copy.wait_recv()
    for slot in range(2):
        turn_copy(slot, 0, 0, 0).wait()


def run_forward(count, length, own_ids, table, w_in, bias, w_rec):
    half_len = length // 2
    units, shard_units = w_rec.shape[2:]
    seq_dev = own_ids.shape[0]
    rows = seq_dev * count
    dma = pltpu.SemaphoreType.DMA
    links = max(count - 1, 1)
    ins = dict(
        own_ids=(own_ids, VMEM),
        table=(table, VMEM),
        w_in=(w_in, VMEM),
        bias=(bias, VMEM),
        w_rec=(w_rec, ANYWHERE),
    )
    outs = dict(
        full_front=((length, rows, units), B16, VMEM),
        full_back=((half_len, rows, units), B16, VMEM),
        acts_front=((length, 4, rows, shard_units), F32, VMEM),
        acts_back=((half_len, 4, rows, shard_units), F32, VMEM),
        cell_front=((length, rows, shard_units), F32, VMEM),
        cell_back=((half_len, rows, shard_units), F32, VMEM),
        group_ids=((rows, LANES), jnp.int32, VMEM),
        w_turned=((2, 4 * shard_units, units), B16, ANYWHERE),
    )
    scratch = dict(
        weights=(pltpu.VMEM(w_rec.shape, B16)),
        turned=(pltpu.VMEM((2, shard_units, shard_units), B16)),
        id_blocks=(pltpu.VMEM((count, max(8, seq_dev), LANES), jnp.int32)),
        load_sem=(dma((2,))),
        turn_sem=(dma((2,))),
        send_sem=(dma((2, 2, links))),
        recv_sem=(dma((2, 2, links))),
        id_send=(dma((links,))),
        id_recv=(dma((links,))),
    )
    body = functools.partial(forward_body, count, length)
    return call(body, "recurrence_forward", ins, outs, scratch, 0, 10**11)


def backward_body(count, r):
    place = lax.axis_index("shard")
    peers = peers_of(place, count)
    units = r.cell_front.shape[2]
    length, half_len = r.cell_front.shape[0], r.cell_back.shape[0]
    loads = [pltpu.make_async_copy(r.w_turned.at[m], r.weights.at[m], r.load_sem.at[m]) for m in range(2)]
    for load in loads:
        load.start()
    acts = (r.acts_front, r.acts_back)
    cells = (r.cell_front, r.cell_back)
    decs = (r.dec_front, r.dec_back)
    gates = (r.gates_front, r.gates_back)
    ends = (length, half_len)
    greet(peers, [])

    def box(side, m, t, k):
        slot = lax.rem(t, 2)
        if k == 0:
            return (r.outbox if side == 0 else r.inbox).at[m, slot]
        return (r.outbox_far if side == 0 else r.inbox_far).at[m, slot, k - 1]

    def exchange(m, t, k):
        slot = lax.rem(t, 2)
        return pltpu.make_async_remote_copy(
            src_ref=box(0, m, t, k),
            dst_ref=box(1, m, t, k),
            send_sem=r.send_sem.at[m, slot, k],
            recv_sem=r.recv_sem.at[m, slot, k],
            device_id={"shard": peers[k]},
            device_id_type=MESH,
        )

    def gate_grads(m, t, grad_hidden, carried, prev_memory):
        in_gate, forget, candidate, out_gate = (acts[m][t, g] for g in range(4))
        squashed = jnp.tanh(cells[m][t])
        grad_memory = grad_hidden * out_gate * (1.0 - squashed * squashed)
        if carried is not None:
            grad_memory = carried + grad_memory
        r.cell_grad[m] = grad_memory * forget
        forget_part = jnp.zeros_like(grad_memory)
        if prev_memory is not None:
            forget_part = grad_memory * prev_memory * forget * (1.0 - forget)
        values = (
            grad_memory * candidate * in_gate * (1.0 - in_gate),
            forget_part,
            grad_memory * in_gate * (1.0 - candidate * candidate),
            grad_hidden * squashed * out_gate * (1.0 - out_gate),
        )
        for g, value in enumerate(values):
            gates[m][t, :, g * units : (g + 1) * units] = value.astype(B16)

    def product(m, t, owner):
        return dot(gates[m][t], r.weights[m, :, span(owner, units)])

    def send_products(m, t):
        for k in reversed(range(len(peers))):
            target = box(0, m, t, k)
            target[...] = product(m, t, peers[k]).astype(target.dtype)
            exchange(m, t, k).start()
        r.own_part[m] = product(m, t, place)

    def incoming(m, t):
        total = decs[m][t - 1] + r.own_part[m]
        for k in range(len(peers)):
            exchange(m, t, k).wait_recv()
            total = total + box(1, m, t, k)[...].astype(F32)
        return total

    def sent(m, t):
        for k in range(len(peers)):
            exchange(m, t, k).wait_send()

    def retreat(m, t):
        gate_grads(m, t, incoming(m, t + 1), r.cell_grad[m], cells[m][t - 1])
        send_products(m, t)
        sent(m, t + 1)

    def first(m):
        t = ends[m] - 1
        gate_grads(m, t, decs[m][t], None, cells[m][t - 1])
        loads[m].wait()
        send_products(m, t)

    def last(m):
        gate_grads(m, 0, incoming(m, 1), r.cell_grad[m], None)
        sent(m, 1)

    assert half_len % 2 == 0 and length == 2 * half_len
    final = half_len - 1
    first(0)
    first(1)
    retreat(0, length - 2)

    def turn(step, carry):
        retreat(0, length - 1 - 2 * step)
        retreat(1, half_len - 1 - step)
        retreat(0, length - 2 - 2 * step)
        return carry

    lax.fori_loop(1, final, turn, 0)
    retreat(0, 1)
    last(1)
    last(0)


def run_backward(count, ran, decs):
    length, rows, shard_units = ran.cell_front.shape
    half_len = ran.cell_back.shape[0]
    units = ran.w_turned.shape[2]
    links = max(count - 1, 1)
    dma = pltpu.SemaphoreType.DMA
    box = (2, 2, rows, shard_units)
    far_box = (2, 2, max(links - 1, 1), rows, shard_units)
    ins = dict(
        acts_front=(ran.acts_front, VMEM),
        acts_back=(ran.acts_back, VMEM),
        cell_front=(ran.cell_front, VMEM),
        cell_back=(ran.cell_back, VMEM),
        dec_front=(decs[0], VMEM),
        dec_back=(decs[1], VMEM),
        w_turned=(ran.w_turned, ANYWHERE),
    )
    gates = dict(
        gates_front=(length, rows, 4 * shard_units),
        gates_back=(half_len, rows, 4 * shard_units),
    )
    scratch = dict(
        weights=(pltpu.VMEM(ran.w_turned.shape, B16)),
        outbox=(pltpu.VMEM(box, F32)),
        inbox=(pltpu.VMEM(box, F32)),
        outbox_far=(pltpu.VMEM(far_box, B16)),
        inbox_far=(pltpu.VMEM(far_box, B16)),
        own_part=(pltpu.VMEM((2, rows, shard_units), F32)),
        cell_grad=(pltpu.VMEM((2, rows, shard_units), F32)),
        load_sem=(dma((2,))),
        send_sem=(dma((2, 2, links))),
        recv_sem=(dma((2, 2, links))),
    )
    outs = {key: (shape, B16, VMEM) for key, shape in gates.items()}
    body = functools.partial(backward_body, count)
    return call(body, "recurrence_backward", ins, outs, scratch, 1, 10**11)


def step_body(count, groups, factor, r):
    place = lax.axis_index("shard")
    group = lax.axis_index("rep")
    core = lax.rem(group, 2)
    sibling = group + 1 - 2 * core
    peers = peers_of(place, count)
    others = others_of(group, groups)
    units = r.weights.shape[3]
    length, half_len = r.full_front.shape[0], r.full_back.shape[0]
    ends = (length, half_len)
    rows = r.group_ids.shape[0]
    seq_dev = r.chars.shape[0]
    vocab, _, embed = r.embedding.shape
    wide = r.past_front.shape[3]
    fulls = (r.full_front, r.full_back)
    acts = (r.acts_front, r.acts_back)
    cells = (r.cell_front, r.cell_back)
    logit_grads = (r.logits_front, r.logits_back)
    pasts = (r.past_front, r.past_back)
    wides = (r.wide_front, r.wide_back)
    own_columns = span(place, units)

    inner = (place * (count - 1 - place)) // 2
    urgent = [
        (a + inner * (c - a), peers[a] + inner * (peers[c] - peers[a])) for a, c in ((2, 1), (1, 0), (0, 2))
    ]

    def to_peer(src, dst, send, recv, peer):
        return pltpu.make_async_remote_copy(
            src_ref=src,
            dst_ref=dst,
            send_sem=send,
            recv_sem=recv,
            device_id={"shard": peer},
            device_id_type=MESH,
        )

    def to_group(src, dst, send, recv, other):
        return pltpu.make_async_remote_copy(
            src_ref=src,
            dst_ref=dst,
            send_sem=send,
            recv_sem=recv,
            device_id={"rep": other},
            device_id_type=MESH,
        )

    loads = [pltpu.make_async_copy(r.w_rec.at[m], r.weights.at[m], r.load_sem.at[m]) for m in range(2)]
    for load in loads:
        load.start()
    barrier = pltpu.get_barrier_semaphore()
    for peer in peers:
        pl.semaphore_signal(barrier, inc=1, device_id={"shard": peer}, device_id_type=MESH)
    for other in others:
        pl.semaphore_signal(barrier, inc=1, device_id={"rep": other}, device_id_type=MESH)
    r.id_blocks[group, place, :seq_dev, :length] = r.chars[...]
    corner = (seq_dev, seq_dev)
    diagonal = lax.broadcasted_iota(jnp.int32, corner, 0) == lax.broadcasted_iota(jnp.int32, corner, 1)
    stops_across = jnp.broadcast_to(r.prefix[...], corner)
    r.id_blocks[group, place, :seq_dev, length : length + 1] = jnp.sum(
        jnp.where(diagonal, stops_across, 0), axis=1, keepdims=True
    )
    pl.semaphore_wait(barrier, len(peers) + len(others))

    def id_copy(k):
        block = r.id_blocks.at[group, place]
        return to_peer(block, block, r.id_send.at[k], r.id_recv.at[k], peers[k])

    def id_spread(j):
        block = r.id_blocks.at[group]
        return to_group(block, block, r.ids_send.at[j], r.ids_recv.at[j], others[j])

    for k in range(len(peers)):
        id_copy(k).start()
    lane = lax.broadcasted_iota(jnp.int32, r.table.shape, 2)
    r.table[...] = jnp.where(lane == embed, 1.0, 0.0).astype(B16)
    r.inputs[...] = jnp.zeros_like(r.inputs)
    for m in range(2):
        r.table[m, :vocab, :embed] = r.embedding[:, m, :]
        for g in range(4):
            r.inputs[m, g, :embed] = r.w_in[m, :, g, :]

    blanks = [pltpu.make_async_copy(r.blank, pasts[m].at[0], r.past_local.at[m]) for m in range(2)]

    def prepare_decoder():
        r.out_own[...] = jnp.zeros_like(r.out_own)
        r.out_bias[...] = jnp.full_like(r.out_bias, -1e30)
        r.out_bias[:, :vocab] = r.b_out[...].astype(F32)
        for m in range(2):
            r.out_own[m, :vocab] = r.w_out[:, m, :]
            r.out_full[m, place] = r.out_own[m].T.reshape(groups, units // groups, -1)
        r.out_sums[...] = jnp.zeros_like(r.out_sums)

    def prepare_sums():
        r.in_sums[...] = jnp.zeros_like(r.in_sums)
        r.embed_part[...] = jnp.zeros_like(r.embed_part)
        r.rec_sums[...] = jnp.zeros_like(r.rec_sums)

    def share_copy(n):
        k, m = len(peers) - 1 - n // 2, n % 2
        block = r.out_full.at[m, place, group]
        return to_peer(block, block, r.share_send.at[n], r.share_recv.at[n], peers[k])

    def share_spread(j, k):
        source = r.out_full.at[:, peers[k], group]
        other = lax.rem(group + 1 + j, groups)
        return to_group(source, source, r.all_send.at[j, k], r.all_recv.at[j, k], other)

    first_spread = 2 * len(peers) + 3

    def send_shares(t):
        for n in range(2 * len(peers)):
            pl.when(t == n + 1)(share_copy(n).start)

        @pl.when(t == first_spread - 1)
        def _():
            for n in range(2 * len(peers)):
                share_copy(n).wait()

        @pl.when(jnp.logical_and(t >= first_spread, t < first_spread + groups - 1))
        def _():
            for k in range(len(peers)):
                share_spread(t - first_spread, k).start()

    def spread_past(m, t):
        for j, other in enumerate(others):
            to_group(
                fulls[m].at[t, :, span(other // 2, wide)],
                pasts[m].at[t + 1, group],
                r.past_send.at[m, j],
                r.past_recv.at[m, j],
                other,
            ).start()
        pltpu.make_async_copy(
            fulls[m].at[t, :, span(group // 2, wide)], pasts[m].at[t + 1, group], r.past_local.at[m]
        ).start()

    def finish_past(m, steps):
        for j, other in enumerate(others):
            part = pasts[m].at[pl.ds(1, steps), 0]
            copy = to_group(part, part, r.past_send.at[m, j], r.past_recv.at[m, j], other)
            copy.wait_send()
            copy.wait_recv()
        mine = pasts[m].at[pl.ds(1, steps), 0]
        pltpu.make_async_copy(mine, mine, r.past_local.at[m]).wait()

    def exchange(m, t, k, peer):
        slot = lax.rem(t, 2)
        own = fulls[m].at[t, :, own_columns]
        return to_peer(own, own, r.hidden_send.at[m, slot, k], r.hidden_recv.at[m, slot, k], peer)

    def finish(m, t, sums, memory):
        in_gate = jax.nn.sigmoid(sums[0])
        forget = jax.nn.sigmoid(sums[1])
        candidate = jnp.tanh(sums[2])
        out_gate = jax.nn.sigmoid(sums[3])
        new_memory = in_gate * candidate if memory is None else forget * memory + in_gate * candidate
        fulls[m][t, :, own_columns] = (out_gate * jnp.tanh(new_memory)).astype(B16)
        for k, peer in urgent:
            exchange(m, t, k, peer).start()
        for g, value in enumerate((in_gate, forget, candidate, out_gate)):
            acts[m][t, g] = value
        cells[m][t] = new_memory

    def start_sums(m, t):
        ids, stops = r.group_ids[...], r.group_ids[:, length : length + 1]
        x_t = dot(marks(id_column(ids, stops, m, t), r.table.shape[1]), r.table[m]).astype(B16)
        return [
            r.gate_bias[m, g : g + 1, :].astype(F32) + dot(x_t, r.inputs[m, g]) for g in range(4)
        ]

    def add_chunk(m, t, owner, sums):
        part = fulls[m][t, :, span(owner, units)]
        return [sums[g] + dot(part, r.weights[m, g, span(owner, units), :]) for g in range(4)]

    def advance(m, t):
        sums = add_chunk(m, t - 1, place, start_sums(m, t))
        for k in range(len(peers)):
            exchange(m, t - 1, k, peers[k]).wait_recv()
            sums = add_chunk(m, t - 1, peers[k], sums)
        finish(m, t, sums, cells[m][t - 1])
        for k in range(len(peers)):
            exchange(m, t - 1, k, peers[k]).wait_send()
        spread_past(m, t - 1)

    def turn_block(m, g, p):
        r.weights[m, g, span(p, units), :] = r.weights[m, g, span(p, units), :].T

    stretch = 4

    def decode(m, chunk):
        t0 = stretch * chunk
        hidden = fulls[m][pl.ds(t0, stretch)].reshape(stretch * rows, count * units)
        logits = dot(hidden, r.out_full[m].reshape(count * units, -1)) + r.out_bias[m : m + 1, :]
        grown = jnp.exp(logits - jnp.max(logits, axis=1, keepdims=True))
        chances = grown / jnp.sum(grown, axis=1, keepdims=True)
        ids, stops = r.group_ids[...], r.group_ids[:, length : length + 1]
        targets, active = [], []
        for i in range(stretch):
            t = t0 + i
            if m == 0:
                targets.append(column_of(ids, lax.rem(t + 1, length)))
                live = jnp.full((rows, 1), t, jnp.int32) < length - 1
            else:
                targets.append(column_of(ids, jnp.maximum(stops - 2 - t, 0)))
                live = stops >= t + 2
            active.append(jnp.where(live, factor, 0.0).astype(F32))
        target, weight = jnp.concatenate(targets, axis=0), jnp.concatenate(active, axis=0)
        lane = lax.broadcasted_iota(jnp.int32, logits.shape, 1)
        picked = (lane == target).astype(F32)
        grad = ((chances - picked) * weight).astype(B16)
        logit_grads[m][pl.ds(t0, stretch)] = grad.reshape(stretch, rows, -1)
        own = fulls[m][pl.ds(t0, stretch), :, own_columns].reshape(stretch * rows, units)
        ones = jnp.ones((stretch * rows, LANES), B16)
        r.out_sums[m] += dot_first(grad, jnp.concatenate([own, ones], axis=1))

    piece = r.out_inbox.shape[2]

    def out_send(m, j):
        other = lax.rem(group + 1 + j, groups)
        return to_group(
            r.out_sums.at[m, span(other, piece)],
            r.out_inbox.at[m, j],
            r.out_send.at[m, j],
            r.out_recv.at[m, j],
            other,
        )

    def out_share(m, j):
        own = r.out_total.at[m, span(group, piece)]
        other = lax.rem(group + 1 + j, groups)
        return to_group(own, own, r.total_send.at[m, j], r.total_recv.at[m, j], other)

    def out_reduce(m):
        total = r.out_sums[m, span(group, piece)]
        for j in range(groups - 1):
            copy = out_send(m, j)
            copy.wait_send()
            copy.wait_recv()
        for j in range(groups - 1):
            total = total + r.out_inbox[m, j]
        r.out_total[m, span(group, piece)] = total

    def out_steps(m, n):
        pl.when(jnp.logical_and(n >= 0, n < groups - 1))(lambda: out_send(m, n).start())
        pl.when(n == groups)(lambda: out_reduce(m))
        ready = jnp.logical_and(n > groups, n < 2 * groups)
        pl.when(ready)(lambda: out_share(m, n - groups - 1).start())

    gates = fulls

    def spread_gates(m, t):
        for j, other in enumerate(others):
            to_group(
                gates[m].at[t, :, span(lax.rem(other, 2), 2 * units)],
                wides[m].at[t, group],
                r.wide_send.at[m, j],
                r.wide_recv.at[m, t // 2],
                other,
            ).start()
        pltpu.make_async_copy(
            gates[m].at[t, :, span(core, 2 * units)], wides[m].at[t, group], r.wide_local.at[m, t // 2]
        ).start()

    def arrive(m, pair):
        far = wides[m].at[pl.ds(2 * pair, 2), pl.ds(0, groups - 1)]
        to_group(far, far, r.wide_send.at[m, 0], r.wide_recv.at[m, pair], others[0]).wait_recv()
        near = wides[m].at[pl.ds(2 * pair, 2), 0]
        pltpu.make_async_copy(near, near, r.wide_local.at[m, pair]).wait()

    def fetches(m, pair):
        slot = lax.rem(pair, 2)
        return (
            pltpu.make_async_copy(
                wides[m].at[pl.ds(2 * pair, 2)], r.wide_slot.at[m, slot], r.fetch_sem.at[m, slot, 0]
            ),
            pltpu.make_async_copy(
                pasts[m].at[pl.ds(2 * pair, 2)], r.past_slot.at[m, slot], r.fetch_sem.at[m, slot, 1]
            ),
        )

    def fetch(m, pair):
        arrive(m, pair)
        for copy in fetches(m, pair):
            copy.start()

    def accumulate(m, pair):
        slot = lax.rem(pair, 2)
        for copy in fetches(m, pair):
            copy.wait()
        dz = r.wide_slot[m, slot].reshape(-1, 2 * units)
        past = r.past_slot[m, slot].reshape(dz.shape[0], -1)
        r.rec_sums[m] += dot_first(past, dz)
        ids, stops = r.every_ids[...], r.every_ids[:, length : length + 1]
        spots = [marks(id_column(ids, stops, m, 2 * pair + i), r.table.shape[1]) for i in range(2)]
        spots = jnp.concatenate(spots, axis=0)
        r.in_sums[m] += dot_first(dot(spots, r.table[m]).astype(B16), dz)
        grad_x = None
        for g in range(2):
            term = dot_last(dz[:, g * units : (g + 1) * units], r.inputs[m, 2 * core + g])
            grad_x = term if grad_x is None else grad_x + term
        for part in split_three(grad_x):
            r.embed_part[m] += dot_first(spots, part)

    def give(m, t, k, peer):
        slot = lax.rem(t, 2)
        return to_peer(
            r.outbox.at[m, slot, k],
            r.inbox.at[m, slot, k],
            r.grad_send.at[m, slot, k],
            r.grad_recv.at[m, slot, k],
            peer,
        )

    def slopes(m, t, prev_memory):
        in_gate, forget, candidate, out_gate = (acts[m][t, g] for g in range(4))
        squashed = jnp.tanh(cells[m][t])
        forget_slope = jnp.zeros_like(forget)
        if prev_memory is not None:
            forget_slope = prev_memory * forget * (1.0 - forget)
        return (
            candidate * in_gate * (1.0 - in_gate),
            forget_slope,
            in_gate * (1.0 - candidate * candidate),
            squashed * out_gate * (1.0 - out_gate),
            out_gate * (1.0 - squashed * squashed),
            forget,
        )

    def gate_grads(m, t, slope, grad_hidden, carried):
        grad_memory = grad_hidden * slope[4]
        if carried is not None:
            grad_memory = carried + grad_memory
        values = [grad_memory * slope[g] for g in range(3)] + [grad_hidden * slope[3]]
        for g, value in enumerate(values):
            gates[m][t, :, g * units : (g + 1) * units] = value.astype(B16)
        r.cell_grad[m] = grad_memory * slope[5]

    def product(m, t, owner):
        total = None
        for g in range(4):
            part = dot(
                gates[m][t, :, g * units : (g + 1) * units], r.weights[m, g, span(owner, units), :]
            )
            total = part if total is None else total + part
        return total

    def from_decoder(m, t):
        return dot(logit_grads[m][t], r.out_own[m])

    def send_products(m, t):
        for k, peer in urgent:
            r.outbox[m, lax.rem(t, 2), k] = product(m, t, peer).astype(B16)
            give(m, t, k, peer).start()
        r.own_part[m] = product(m, t, place) + from_decoder(m, t - 1)
        spread_gates(m, t)

    def incoming(m, t):
        total = r.own_part[m]
        for k in range(len(peers)):
            give(m, t, k, peers[k]).wait_recv()
            total = total + r.inbox[m, lax.rem(t, 2), k].astype(F32)
        return total

    def sent(m, t):
        for k in range(len(peers)):
            give(m, t, k, peers[k]).wait_send()

    def retreat(m, t):
        slope = slopes(m, t, cells[m][t - 1])
        gate_grads(m, t, slope, incoming(m, t + 1), r.cell_grad[m])
        send_products(m, t)
        sent(m, t + 1)

    def first(m):
        t = ends[m] - 1
        gate_grads(m, t, slopes(m, t, cells[m][t - 1]), from_decoder(m, t), None)
        send_products(m, t)

    def last(m):
        slope = slopes(m, 0, None)
        gate_grads(m, 0, slope, incoming(m, 1), r.cell_grad[m])
        spread_gates(m, 0)
        sent(m, 1)

    depth = r.rec_grad.shape[2]
    kept = r.in_all.shape[2]

    def swap(m, g, i):
        source, target = (
            (r.rec_sums.at[m, span(1 - core, depth), pl.ds(g * units, units)], r.rec_grad),
            (r.in_sums.at[m, pl.ds(0, kept), pl.ds(g * units, units)], r.in_all),
        )[i]
        target = target.at[m, 2 * core + g]
        return to_group(source, target, r.swap_send.at[i, m, g], r.swap_recv.at[i, m, g], sibling)

    def keep(m, g):
        return pltpu.make_async_copy(
            r.rec_sums.at[m, span(core, depth), pl.ds(g * units, units)],
            r.rec_grad.at[m, 2 * core + g],
            r.keep_sem.at[m, g],
        )

    def start_swaps(m):
        for g in range(2):
            swap(m, g, 1).start()
        for g in range(2):
            swap(m, g, 0).start()
            keep(m, g).start()
            r.in_all[m, 2 * core + g] = r.in_sums[m, :kept, g * units : (g + 1) * units]

    def finish_inputs(m):
        for g in range(2):
            swap(m, g, 1).wait()
        for g in range(4):
            r.grad_in[m, :, g, :] = r.in_all[m, g, :embed]
        r.grad_bias[m] = r.in_all[m, :, embed, :]

    def finish_swaps(m):
        for g in range(2):
            swap(m, g, 0).wait()
            keep(m, g).wait()

    half = r.embed_half.shape[1]
    slice_rows = half // count

    def embed_pair(m):
        return to_group(
            r.embed_part.at[m, span(1 - core, half)],
            r.embed_half.at[m],
            r.embed_send.at[m, 0],
            r.embed_recv.at[m, 0],
            sibling,
        )

    def embed_reduce(m, k):
        return to_peer(
            r.embed_half.at[m, span(peers[k], slice_rows)],
            r.embed_inbox.at[m, k],
            r.reduce_send.at[m, k],
            r.reduce_recv.at[m, k],
            peers[k],
        )

    def own_slice(m):
        first_row = pl.multiple_of(core * half + place * slice_rows, 8)
        return r.embed_full.at[m, pl.ds(first_row, slice_rows)]

    def embed_gather(m, k):
        return to_peer(
            own_slice(m), own_slice(m), r.gather_send.at[m, k], r.gather_recv.at[m, k], peers[k]
        )

    def embed_return(m):
        whole = r.embed_full.at[m, span(core, half)]
        return to_group(whole, whole, r.embed_send.at[m, 1], r.embed_recv.at[m, 1], sibling)

    def embed_stage(m, stage):
        if stage == 0:
            embed_pair(m).start()
        elif stage == 1:
            embed_pair(m).wait()
            r.embed_half[m] += r.embed_part[m, span(core, half)]
            for k in reversed(range(len(peers))):
                embed_reduce(m, k).start()
        elif stage == 2:
            total = r.embed_half[m, span(place, slice_rows)]
            for k in range(len(peers)):
                embed_reduce(m, k).wait()
                total = total + r.embed_inbox[m, k]
            own_slice(m)[...] = total
            for k in reversed(range(len(peers))):
                embed_gather(m, k).start()
        elif stage == 3:
            for k in range(len(peers)):
                embed_gather(m, k).wait()
            embed_return(m).start()
        else:
            embed_return(m).wait()
            r.grad_embed[:, m, :] = r.embed_full[m, :vocab, :embed]

    for k in range(len(peers)):
        id_copy(k).wait()
    for s in range(count):
        r.group_ids[s * seq_dev : (s + 1) * seq_dev] = r.id_blocks[group, s, :seq_dev]
    for j in range(len(others)):
        id_spread(j).start()
    for m in range(2):
        finish(m, 0, start_sums(m, 0), None)
    r.blank[...] = jnp.zeros_like(r.blank)
    for copy in blanks:
        copy.start()
    prepare_decoder()
    for copy in blanks:
        copy.wait()
    for load in loads:
        load.wait()

    shared = first_spread + groups

    def both(t, carry):
        advance(0, t)
        advance(1, t)
        send_shares(t)
        pl.when(t == 2)(prepare_sums)

        @pl.when(t == shared)
        def _():
            for j in range(groups - 1):
                for k in range(len(peers)):
                    share_spread(j, k).wait()

        chunk = t - shared - 1
        pl.when(jnp.logical_and(chunk >= 0, stretch * (chunk + 1) <= t))(lambda: decode(0, chunk))
        return carry

    decoded = 0
    while stretch * (decoded + 1) <= shared + 1 + decoded and shared + 1 + decoded < half_len:
        decoded += 1

    def settle(m):
        for k in range(len(peers)):
            exchange(m, ends[m] - 1, k, peers[k]).wait()

    back_chunks = half_len // stretch
    blocks = 4 * count
    begin = 3
    back_pairs = half_len // 2
    front_pairs = length // 2
    assert half_len % stretch == 0 and length == 2 * half_len and half_len % 2 == 0
    assert first_spread + groups - 1 <= half_len
    assert back_chunks == 2 * begin and blocks <= 6 * begin and groups < half_len // 2

    def front_only(t, carry):
        advance(0, t)
        n = t - half_len

        @pl.when(n < begin)
        def _():
            for i in range(2):
                decode(1, back_chunks - 1 - 2 * n - i)
            for i in range(6):
                block = 6 * n + i
                pl.when(block < blocks)(lambda: turn_block(1, block // count, lax.rem(block, count)))

        @pl.when(n == begin)
        def _():
            finish_past(1, half_len - 1)
            first(1)

        pl.when(n > begin)(lambda: retreat(1, half_len - 1 - (n - begin)))
        begun = n >= begin
        chunk = n - begin + decoded
        early = jnp.logical_and(begun, stretch * (chunk + 1) <= t)
        late = jnp.logical_and(stretch * (chunk + 1) > t, lax.rem(t, stretch) == 0)
        pl.when(early)(lambda: decode(0, chunk))
        pl.when(jnp.logical_and(begun, late))(lambda: decode(0, t // stretch - 1))
        behind = n - begin - 5
        even = jnp.logical_and(behind >= 0, lax.rem(n - begin, 2) == 1)
        odd = jnp.logical_and(behind >= 1, lax.rem(n - begin, 2) == 0)
        pl.when(even)(lambda: fetch(1, back_pairs - 1 - behind // 2))
        pl.when(odd)(lambda: accumulate(1, back_pairs - 1 - behind // 2))
        return carry

    lax.fori_loop(1, half_len, both, 0)
    settle(1)
    for j in range(len(others)):
        id_spread(j).wait()
    r.every_ids[...] = r.id_blocks[:, :, :seq_dev].reshape(r.every_ids.shape)
    lax.fori_loop(half_len, length, front_only, 0)
    for g in range(4):
        for p in range(count):
            turn_block(0, g, p)
    settle(0)
    decode(0, length // stretch - 1)
    finish_past(0, length - 1)

    first(0)
    retreat(1, begin - 1)
    retreat(0, length - 2)
    retreat(1, begin - 2)
    fetched = (half_len - begin - 5) // 2
    left = back_pairs - fetched
    after = left + 2

    def turn(step, carry):
        retreat(0, length - 1 - 2 * step)
        pl.when(step == 1)(lambda: last(1))
        pl.when(step >= 3)(lambda: fetch(0, front_pairs + 2 - step))
        remaining = jnp.logical_and(step >= 2, step < left + 2)
        pl.when(remaining)(lambda: fetch(1, left + 1 - step))
        for stage in range(5):
            pl.when(step == after + stage)(lambda stage=stage: embed_stage(1, stage))
        pl.when(step == after)(lambda: start_swaps(1))
        pl.when(step == after + 2)(lambda: finish_inputs(1))
        retreat(0, length - 2 - 2 * step)
        pl.when(step >= 3)(lambda: accumulate(0, front_pairs + 2 - step))
        pl.when(remaining)(lambda: accumulate(1, left + 1 - step))
        out_steps(0, step - 1)
        out_steps(1, step - 1)
        return carry

    final = half_len - 1
    assert begin == 3 and after + 5 <= final
    lax.fori_loop(1, final, turn, 0)
    retreat(0, 1)
    fetch(0, 3)
    last(0)
    fetch(0, 2)
    accumulate(0, 3)
    accumulate(0, 2)
    fetch(0, 1)
    for m in range(2):
        for j in range(groups - 1):
            out_share(m, j).wait()
        r.grad_out[:, m, :] = r.out_total[m, :vocab, :units]
        r.grad_bout[m : m + 1, :] = r.out_total[m, :, units:].T[:1, :vocab]
    finish_swaps(1)
    accumulate(0, 1)
    fetch(0, 0)
    accumulate(0, 0)
    embed_stage(0, 0)
    start_swaps(0)
    embed_stage(0, 1)
    for m in range(2):
        for j in range(groups - 1):
            part = wides[m].at[:, 0]
            to_group(part, part, r.wide_send.at[m, j], r.wide_recv.at[m, 0], others[j]).wait_send()
    embed_stage(0, 2)
    finish_inputs(0)
    finish_swaps(0)
    embed_stage(0, 3)
    embed_stage(0, 4)


def run_step(count, groups, factor, char_ids, prefix, embedding, w_in, w_rec, gate_bias, w_out, b_out):
    seq_dev, length = char_ids.shape
    half_len = length // 2
    units, shard_units = w_rec.shape[2:]
    vocab, embed = embedding.shape[1:]
    rows = seq_dev * count
    wide = units // (groups // 2)
    depth = -(-(embed + 1) // LANES) * LANES
    lanes = -(-vocab // LANES) * LANES
    reduced = -(-vocab // (16 * count)) * 8 * count
    padded = 2 * reduced
    piece = lanes // groups
    links = count - 1
    far = groups - 1
    dma = pltpu.SemaphoreType.DMA
    ins = dict(
        chars=(char_ids, VMEM),
        prefix=(prefix[None], VMEM),
        embedding=(embedding.transpose(1, 0, 2), VMEM),
        w_in=(w_in.transpose(0, 2, 1, 3), VMEM),
        gate_bias=(gate_bias, VMEM),
        w_out=(w_out.transpose(2, 0, 1), VMEM),
        b_out=(b_out, VMEM),
        w_rec=(w_rec, ANYWHERE),
    )
    outs = dict(
        grad_embed=((vocab, 2, embed), F32, VMEM),
        grad_in=((2, embed, 4, shard_units), F32, VMEM),
        rec_grad=((2, 4, wide // 2, shard_units), F32, ANYWHERE),
        grad_bias=((2, 4, shard_units), F32, VMEM),
        grad_out=((vocab, 2, shard_units), F32, VMEM),
        grad_bout=((2, vocab), F32, VMEM),
        past_front=((length, groups, rows, wide), B16, ANYWHERE),
        past_back=((half_len, groups, rows, wide), B16, ANYWHERE),
        wide_front=((length, groups, rows, 2 * shard_units), B16, ANYWHERE),
        wide_back=((half_len, groups, rows, 2 * shard_units), B16, ANYWHERE),
    )
    arrays = dict(
        weights=(w_rec.shape, B16),
        out_bias=((2, lanes), F32),
        out_full=((2, count, groups, shard_units // groups, lanes), B16),
        id_blocks=((groups, count, max(8, seq_dev), LANES), jnp.int32),
        group_ids=((rows, LANES), jnp.int32),
        every_ids=((groups * rows, LANES), jnp.int32),
        blank=((groups, rows, wide), B16),
        full_front=((length, rows, units), B16),
        full_back=((half_len, rows, units), B16),
        acts_front=((length, 4, rows, shard_units), F32),
        acts_back=((half_len, 4, rows, shard_units), F32),
        cell_front=((length, rows, shard_units), F32),
        cell_back=((half_len, rows, shard_units), F32),
        logits_front=((length, rows, lanes), B16),
        logits_back=((half_len, rows, lanes), B16),
        out_sums=((2, lanes, shard_units + LANES), F32),
        out_inbox=((2, far, piece, shard_units + LANES), F32),
        out_total=((2, lanes, shard_units + LANES), F32),
        outbox=((2, 2, links, rows, shard_units), B16),
        inbox=((2, 2, links, rows, shard_units), B16),
        own_part=((2, rows, shard_units), F32),
        cell_grad=((2, rows, shard_units), F32),
        rec_sums=((2, wide, 2 * shard_units), F32),
        in_sums=((2, depth, 2 * shard_units), F32),
        in_all=((2, 4, -(-(embed + 1) // 8) * 8, shard_units), F32),
        table=((2, padded, depth), B16),
        inputs=((2, 4, depth, shard_units), B16),
        out_own=((2, lanes, shard_units), B16),
        embed_part=((2, padded, depth), F32),
        embed_half=((2, reduced, depth), F32),
        embed_full=((2, padded, depth), F32),
        embed_inbox=((2, links, reduced // count, depth), F32),
        wide_slot=((2, 2, 2, groups, rows, 2 * shard_units), B16),
        past_slot=((2, 2, 2, groups, rows, wide), B16),
    )
    semaphores = dict(
        load_sem=(2,),
        id_send=(links,),
        id_recv=(links,),
        ids_send=(far,),
        ids_recv=(far,),
        share_send=(2 * links,),
        share_recv=(2 * links,),
        all_send=(far, links),
        all_recv=(far, links),
        past_send=(2, far),
        past_recv=(2, far),
        past_local=(2,),
        hidden_send=(2, 2, links),
        hidden_recv=(2, 2, links),
        out_send=(2, far),
        out_recv=(2, far),
        total_send=(2, far),
        total_recv=(2, far),
        wide_send=(2, far),
        wide_recv=(2, length // 2),
        wide_local=(2, length // 2),
        fetch_sem=(2, 2, 2),
        grad_send=(2, 2, links),
        grad_recv=(2, 2, links),
        swap_send=(2, 2, 2),
        swap_recv=(2, 2, 2),
        keep_sem=(2, 2),
        embed_send=(2, 2),
        embed_recv=(2, 2),
        reduce_send=(2, links),
        reduce_recv=(2, links),
        gather_send=(2, links),
        gather_recv=(2, links),
    )
    scratch = {key: pltpu.VMEM(shape, kind) for key, (shape, kind) in arrays.items()}
    scratch |= {key: dma(shape) for key, shape in semaphores.items()}
    body = functools.partial(step_body, count, groups, factor)
    return call(body, "lstm_step", ins, outs, scratch, 2, 10**11)


def shifted(values):
    return jnp.concatenate([jnp.zeros_like(values[:1]), values[:-1]], axis=0)


def reduced_grads(ran, gates, embedding, w_in, ids, group_size):
    embed = embedding.shape[2]

    def per_model(full, grads, ids, m):
        grads = grads.reshape(grads.shape[0], group_size, 4, -1)
        rec = jnp.einsum("tbk,tbgn->gkn", shifted(full), grads, preferred_element_type=F32)
        spots = one_hot(ids, embedding.shape[1], B16)
        x = jnp.einsum("tbv,ve->tbe", spots, embedding[m], preferred_element_type=F32).astype(B16)
        in_grad = jnp.einsum("tbe,tbgn->gen", x, grads, preferred_element_type=F32)
        bias = jnp.sum(grads, axis=(0, 1), dtype=F32)
        dx = jnp.einsum("tbgn,gen->tbe", grads, w_in[m], preferred_element_type=F32)
        embed_grad = jnp.einsum("tbv,tbe->ve", spots.astype(F32), dx, precision=PRECISE)
        return rec, in_grad, bias, embed_grad

    parts = (
        per_model(ran.full_front, gates.gates_front, ids[0], 0),
        per_model(ran.full_back, gates.gates_back, ids[1], 1),
    )
    rec, in_grad, bias, embed_grad = (jnp.stack(values) for values in zip(*parts))
    rec_grad = lax.psum_scatter(rec, "rep", scatter_dimension=2, tiled=True)
    in_sum, bias_sum = lax.psum((in_grad, bias), "rep")
    embed_sum = lax.psum(embed_grad, ("rep", "shard"))
    return embed_sum, in_sum, rec_grad, bias_sum


def shards(char_ids, prefix, embedding, w_in, w_rec, gate_bias, w_out, b_out):
    seq_dev, length = char_ids.shape
    half_len = length // 2
    vocab_size, embed = embedding.shape[1:]
    shard_units = w_rec.shape[3]
    count, groups = lax.axis_size("shard"), lax.axis_size("rep")
    group_size = seq_dev * count
    factor = 1.0 / math.sqrt(groups * count * seq_dev * length)
    if groups == 8 and count == 4 and length == 48:
        done = run_step(
            count, groups, factor, char_ids, prefix, embedding, w_in, w_rec, gate_bias, w_out, b_out
        )
        return (
            done.grad_embed.transpose(1, 0, 2),
            done.grad_in.transpose(0, 2, 1, 3),
            done.rec_grad,
            done.grad_bias,
            done.grad_out.transpose(1, 2, 0),
            done.grad_bout,
        )
    own_ids = jnp.concatenate([char_ids, prefix[:, None]], axis=1)
    own_ids = jnp.pad(own_ids, ((0, 0), (0, LANES - length - 1)))
    full_out = lax.all_gather(w_out, "shard", axis=1, tiled=True)
    depth = -(-(embed + 1) // LANES) * LANES
    padded = -(-vocab_size // LANES) * LANES
    table = jnp.pad(embedding, ((0, 0), (0, 0), (0, 1)), constant_values=1)
    table = jnp.pad(table, ((0, 0), (0, padded - vocab_size), (0, depth - embed - 1)))
    inputs = jnp.pad(w_in, ((0, 0), (0, 0), (0, depth - embed), (0, 0)))
    ran = run_forward(count, length, own_ids, table, inputs, gate_bias.astype(F32), w_rec)
    group_chars, group_prefix = ran.group_ids[:, :length], ran.group_ids[:, length]
    front_in = group_chars.T
    front_target = jnp.concatenate([group_chars[:, 1:], group_chars[:, :1]], axis=1).T
    timeline = jnp.arange(length, dtype=jnp.int32)[:, None]
    front_active = jnp.broadcast_to((timeline < length - 1).astype(F32), (length, group_size))
    reverse_steps = jnp.arange(half_len, dtype=jnp.int32)[:, None]

    def back_pick(offset):
        spot = jnp.maximum(group_prefix[None, :] - offset - reverse_steps, 0)
        chosen = one_hot(spot, length, jnp.int32) * group_chars[None]
        return jnp.sum(chosen, axis=-1)

    back_target = back_pick(2)
    back_active = (reverse_steps <= group_prefix[None, :] - 2).astype(F32)
    first_unit = lax.axis_index("shard") * shard_units

    def decode(full, m, target, active):
        rows = full.reshape(-1, full.shape[-1])
        logits = dot(rows, full_out[m]) + b_out[m].astype(F32)
        grad = loss_grad(logits, target.reshape(-1), active.reshape(-1), factor)
        dec = dot_last(grad, w_out[m])
        own = lax.dynamic_slice_in_dim(rows, first_unit, shard_units, axis=1)
        out_grad = dot_first(own, grad)
        bout = jnp.sum(grad, axis=0, dtype=F32)
        return dec.reshape(full.shape[0], group_size, shard_units), out_grad, bout

    front_dec, front_out_grad, front_bout = decode(ran.full_front, 0, front_target, front_active)
    back_dec, back_out_grad, back_bout = decode(ran.full_back, 1, back_target, back_active)
    out_and_bout = jnp.stack(
        [
            jnp.concatenate([front_out_grad, front_bout[None]], axis=0),
            jnp.concatenate([back_out_grad, back_bout[None]], axis=0),
        ]
    )
    out_and_bout = lax.psum(out_and_bout, "rep")
    out_sum, bout_sum = out_and_bout[:, :shard_units], out_and_bout[:, shard_units]
    done = run_backward(count, ran, (front_dec, back_dec))
    embed_sum, in_sum, rec_grad, bias_sum = reduced_grads(
        ran, done, embedding, w_in, (front_in, back_pick(1)), group_size
    )
    return (embed_sum, in_sum, rec_grad, bias_sum, out_sum, bout_sum)


def solution(mesh):
    in_specs = (
        P(("rep", "shard"), None),
        P(("rep", "shard")),
        P(),
        P(None, None, None, "shard"),
        P(None, None, None, "shard"),
        P(None, None, "shard"),
        P(None, "shard", None),
        P(),
    )
    out_specs = (
        P(),
        P(None, None, None, "shard"),
        P(None, None, "rep", "shard"),
        P(None, None, "shard"),
        P(None, "shard", None),
        P(),
    )
    return jax.shard_map(shards, mesh=mesh, in_specs=in_specs, out_specs=out_specs, check_vma=False)
```

```python
import functools
import math
import types

import jax
import jax.numpy as jnp
from jax import lax
from jax.experimental import pallas as pl
from jax.experimental.pallas import tpu as pltpu
from jax.sharding import PartitionSpec as P

PRECISE = lax.Precision.HIGHEST
MESH = pl.DeviceIdType.MESH
LANES = 128
MIB = 1 << 20
B16 = jnp.bfloat16
F32 = jnp.float32
VMEM = pl.BlockSpec(memory_space=pltpu.VMEM)
ANYWHERE = pl.BlockSpec(memory_space=pl.ANY)


def one_hot(ids, width, out_type):
    return (ids[..., None] == jnp.arange(width, dtype=jnp.int32)).astype(out_type)


def loss_grad(logits, targets, active, factor):
    probabilities = jax.nn.softmax(logits, axis=-1)
    picked = one_hot(targets, logits.shape[-1], F32)
    return ((probabilities - picked) * (active * factor)[:, None]).astype(B16)


def peers_of(place, count):
    if count == 4:
        return [place + 1 - 2 * lax.rem(place, 2), lax.rem(place + 2, 4), 3 - place]
    if count == 2:
        return [1 - place]
    assert count == 1
    return []


def others_of(group, groups):
    return [lax.rem(group + j, groups) for j in range(1, groups)]


def greet(peers, others):
    barrier = pltpu.get_barrier_semaphore()
    for peer in peers:
        pl.semaphore_signal(barrier, inc=1, device_id={"shard": peer}, device_id_type=MESH)
    for other in others:
        pl.semaphore_signal(barrier, inc=1, device_id={"rep": other}, device_id_type=MESH)
    pl.semaphore_wait(barrier, len(peers) + len(others))


def span(index, size):
    return pl.ds(pl.multiple_of(index * size, size), size)


def dot(left, right):
    return jnp.dot(left, right, preferred_element_type=F32)


def dot_last(left, right):
    return lax.dot_general(left, right, (((1,), (1,)), ((), ())), preferred_element_type=F32)


def dot_first(left, right):
    return lax.dot_general(left, right, (((0,), (0,)), ((), ())), preferred_element_type=F32)


def column_of(ids, spot):
    lane = lax.broadcasted_iota(jnp.int32, ids.shape, 1)
    return jnp.sum(jnp.where(lane == spot, ids, 0), axis=1, keepdims=True)


def marks(column, width):
    lane = lax.broadcasted_iota(jnp.int32, (column.shape[0], width), 1)
    return (lane == column).astype(F32).astype(B16)


def id_column(ids, ends, m, t):
    return column_of(ids, t) if m == 0 else column_of(ids, jnp.maximum(ends - 1 - t, 0))


def split_three(value):
    first = value.astype(B16)
    rest = value - first.astype(F32)
    second = rest.astype(B16)
    return first, second, (rest - second.astype(F32)).astype(B16)


def call(body, name, ins, outs, scratch, collective_id, cost, resident=False):
    names = [*ins, *outs, *scratch]

    def result(shape, kind, spec):
        if resident and spec is VMEM:
            return pltpu.VMEM(shape, kind)
        return jax.ShapeDtypeStruct(shape, kind)

    def kernel(*refs):
        body(types.SimpleNamespace(**dict(zip(names, refs))))

    results = pl.pallas_call(
        kernel,
        out_shape=tuple(result(*out) for out in outs.values()),
        in_specs=[spec for _, spec in ins.values()],
        out_specs=tuple(spec for _, _, spec in outs.values()),
        scratch_shapes=list(scratch.values()),
        compiler_params=pltpu.CompilerParams(
            collective_id=collective_id,
            has_side_effects=True,
            vmem_limit_bytes=(59 if resident else 62) * MIB,
        ),
        cost_estimate=pl.CostEstimate(flops=cost, bytes_accessed=50 * MIB, transcendentals=0),
        name=name,
    )(*[value for value, _ in ins.values()])
    return types.SimpleNamespace(**dict(zip(outs, results)))


def forward_body(count, length, r):
    place = lax.axis_index("shard")
    peers = peers_of(place, count)
    units = r.weights.shape[3]
    half_len = length // 2
    seq_dev = r.own_ids.shape[0]
    loads = [pltpu.make_async_copy(r.w_rec.at[m], r.weights.at[m], r.load_sem.at[m]) for m in range(2)]
    for load in loads:
        load.start()
    r.id_blocks[place, :seq_dev] = r.own_ids[...]
    greet(peers, [])

    def id_copy(k):
        block = r.id_blocks.at[place]
        return pltpu.make_async_remote_copy(
            src_ref=block,
            dst_ref=block,
            send_sem=r.id_send.at[k],
            recv_sem=r.id_recv.at[k],
            device_id={"shard": peers[k]},
            device_id_type=MESH,
        )

    for k in range(len(peers)):
        id_copy(k).start()
    fulls = (r.full_front, r.full_back)
    acts = (r.acts_front, r.acts_back)
    cells = (r.cell_front, r.cell_back)
    def exchange(m, t, k):
        slot = lax.rem(t, 2)
        own = fulls[m].at[t, :, span(place, units)]
        return pltpu.make_async_remote_copy(
            src_ref=own,
            dst_ref=own,
            send_sem=r.send_sem.at[m, slot, k],
            recv_sem=r.recv_sem.at[m, slot, k],
            device_id={"shard": peers[k]},
            device_id_type=MESH,
        )

    def finish(m, t, sums, memory):
        in_gate = jax.nn.sigmoid(sums[0])
        forget = jax.nn.sigmoid(sums[1])
        candidate = jnp.tanh(sums[2])
        out_gate = jax.nn.sigmoid(sums[3])
        new_memory = in_gate * candidate if memory is None else forget * memory + in_gate * candidate
        fulls[m][t, :, span(place, units)] = (out_gate * jnp.tanh(new_memory)).astype(B16)
        for k in reversed(range(len(peers))):
            exchange(m, t, k).start()
        for g, value in enumerate((in_gate, forget, candidate, out_gate)):
            acts[m][t, g] = value
        cells[m][t] = new_memory

    def start_sums(m, t):
        ids, ends = r.group_ids[...], r.group_ids[:, length : length + 1]
        spots = marks(id_column(ids, ends, m, t), r.table.shape[1])
        x_t = dot(spots, r.table[m]).astype(B16)
        return [r.bias[m, g : g + 1] + dot(x_t, r.w_in[m, g]) for g in range(4)]

    def add_chunk(m, t, owner, sums):
        part = fulls[m][t, :, span(owner, units)]
        return [sums[g] + dot(part, r.weights[m, g, span(owner, units), :]) for g in range(4)]

    def advance(m, t):
        sums = add_chunk(m, t - 1, place, start_sums(m, t))
        for k in range(len(peers)):
            exchange(m, t - 1, k).wait_recv()
            sums = add_chunk(m, t - 1, peers[k], sums)
        for k in range(len(peers)):
            exchange(m, t - 1, k).wait_send()
        finish(m, t, sums, cells[m][t - 1])

    def turn_copy(slot, m, g, p):
        return pltpu.make_async_copy(
            r.turned.at[slot],
            r.w_turned.at[m, span(g, units), span(p, units)],
            r.turn_sem.at[slot],
        )

    blocks = 8 * count

    def turn(block, slot):
        m, g, p = block // (4 * count), lax.rem(block // count, 4), lax.rem(block, count)

        @pl.when(block < blocks)
        def _():
            @pl.when(block >= 2)
            def _():
                turn_copy(slot, 0, 0, 0).wait()

            r.turned[slot] = r.weights[m, g, span(p, units), :].T
            turn_copy(slot, m, g, p).start()

    for k in range(len(peers)):
        id_copy(k).wait_send()
        id_copy(k).wait_recv()
    for s in range(count):
        r.group_ids[s * seq_dev : (s + 1) * seq_dev] = r.id_blocks[s, :seq_dev]
    finish(0, 0, start_sums(0, 0), None)
    finish(1, 0, start_sums(1, 0), None)
    for load in loads:
        load.wait()

    def both(t, carry):
        advance(0, t)
        advance(1, t)
        return carry

    def front_only(t, carry):
        advance(0, t)
        turn(2 * (t - half_len), 0)
        turn(2 * (t - half_len) + 1, 1)
        return carry

    assert blocks <= 2 * (length - half_len)
    lax.fori_loop(1, half_len, both, 0)
    lax.fori_loop(half_len, length, front_only, 0)
    for m, end in ((0, length), (1, half_len)):
        for k in range(len(peers)):
            copy = exchange(m, end - 1, k)
            copy.wait_send()
            copy.wait_recv()
    for slot in range(2):
        turn_copy(slot, 0, 0, 0).wait()


def run_forward(count, length, own_ids, table, w_in, bias, w_rec):
    half_len = length // 2
    units, shard_units = w_rec.shape[2:]
    seq_dev = own_ids.shape[0]
    rows = seq_dev * count
    dma = pltpu.SemaphoreType.DMA
    links = max(count - 1, 1)
    ins = dict(
        own_ids=(own_ids, VMEM),
        table=(table, VMEM),
        w_in=(w_in, VMEM),
        bias=(bias, VMEM),
        w_rec=(w_rec, ANYWHERE),
    )
    outs = dict(
        full_front=((length, rows, units), B16, VMEM),
        full_back=((half_len, rows, units), B16, VMEM),
        acts_front=((length, 4, rows, shard_units), F32, VMEM),
        acts_back=((half_len, 4, rows, shard_units), F32, VMEM),
        cell_front=((length, rows, shard_units), F32, VMEM),
        cell_back=((half_len, rows, shard_units), F32, VMEM),
        group_ids=((rows, LANES), jnp.int32, VMEM),
        w_turned=((2, 4 * shard_units, units), B16, ANYWHERE),
    )
    scratch = dict(
        weights=(pltpu.VMEM(w_rec.shape, B16)),
        turned=(pltpu.VMEM((2, shard_units, shard_units), B16)),
        id_blocks=(pltpu.VMEM((count, max(8, seq_dev), LANES), jnp.int32)),
        load_sem=(dma((2,))),
        turn_sem=(dma((2,))),
        send_sem=(dma((2, 2, links))),
        recv_sem=(dma((2, 2, links))),
        id_send=(dma((links,))),
        id_recv=(dma((links,))),
    )
    body = functools.partial(forward_body, count, length)
    return call(body, "recurrence_forward", ins, outs, scratch, 0, 10**11)


def backward_body(count, r):
    place = lax.axis_index("shard")
    peers = peers_of(place, count)
    units = r.cell_front.shape[2]
    length, half_len = r.cell_front.shape[0], r.cell_back.shape[0]
    loads = [pltpu.make_async_copy(r.w_turned.at[m], r.weights.at[m], r.load_sem.at[m]) for m in range(2)]
    for load in loads:
        load.start()
    acts = (r.acts_front, r.acts_back)
    cells = (r.cell_front, r.cell_back)
    decs = (r.dec_front, r.dec_back)
    gates = (r.gates_front, r.gates_back)
    ends = (length, half_len)
    greet(peers, [])

    def box(side, m, t, k):
        slot = lax.rem(t, 2)
        if k == 0:
            return (r.outbox if side == 0 else r.inbox).at[m, slot]
        return (r.outbox_far if side == 0 else r.inbox_far).at[m, slot, k - 1]

    def exchange(m, t, k):
        slot = lax.rem(t, 2)
        return pltpu.make_async_remote_copy(
            src_ref=box(0, m, t, k),
            dst_ref=box(1, m, t, k),
            send_sem=r.send_sem.at[m, slot, k],
            recv_sem=r.recv_sem.at[m, slot, k],
            device_id={"shard": peers[k]},
            device_id_type=MESH,
        )

    def gate_grads(m, t, grad_hidden, carried, prev_memory):
        in_gate, forget, candidate, out_gate = (acts[m][t, g] for g in range(4))
        squashed = jnp.tanh(cells[m][t])
        grad_memory = grad_hidden * out_gate * (1.0 - squashed * squashed)
        if carried is not None:
            grad_memory = carried + grad_memory
        r.cell_grad[m] = grad_memory * forget
        forget_part = jnp.zeros_like(grad_memory)
        if prev_memory is not None:
            forget_part = grad_memory * prev_memory * forget * (1.0 - forget)
        values = (
            grad_memory * candidate * in_gate * (1.0 - in_gate),
            forget_part,
            grad_memory * in_gate * (1.0 - candidate * candidate),
            grad_hidden * squashed * out_gate * (1.0 - out_gate),
        )
        for g, value in enumerate(values):
            gates[m][t, :, g * units : (g + 1) * units] = value.astype(B16)

    def product(m, t, owner):
        return dot(gates[m][t], r.weights[m, :, span(owner, units)])

    def send_products(m, t):
        for k in reversed(range(len(peers))):
            target = box(0, m, t, k)
            target[...] = product(m, t, peers[k]).astype(target.dtype)
            exchange(m, t, k).start()
        r.own_part[m] = product(m, t, place)

    def incoming(m, t):
        total = decs[m][t - 1] + r.own_part[m]
        for k in range(len(peers)):
            exchange(m, t, k).wait_recv()
            total = total + box(1, m, t, k)[...].astype(F32)
        return total

    def sent(m, t):
        for k in range(len(peers)):
            exchange(m, t, k).wait_send()

    def retreat(m, t):
        gate_grads(m, t, incoming(m, t + 1), r.cell_grad[m], cells[m][t - 1])
        send_products(m, t)
        sent(m, t + 1)

    def first(m):
        t = ends[m] - 1
        gate_grads(m, t, decs[m][t], None, cells[m][t - 1])
        loads[m].wait()
        send_products(m, t)

    def last(m):
        gate_grads(m, 0, incoming(m, 1), r.cell_grad[m], None)
        sent(m, 1)

    assert half_len % 2 == 0 and length == 2 * half_len
    final = half_len - 1
    first(0)
    first(1)
    retreat(0, length - 2)

    def turn(step, carry):
        retreat(0, length - 1 - 2 * step)
        retreat(1, half_len - 1 - step)
        retreat(0, length - 2 - 2 * step)
        return carry

    lax.fori_loop(1, final, turn, 0)
    retreat(0, 1)
    last(1)
    last(0)


def run_backward(count, ran, decs):
    length, rows, shard_units = ran.cell_front.shape
    half_len = ran.cell_back.shape[0]
    units = ran.w_turned.shape[2]
    links = max(count - 1, 1)
    dma = pltpu.SemaphoreType.DMA
    box = (2, 2, rows, shard_units)
    far_box = (2, 2, max(links - 1, 1), rows, shard_units)
    ins = dict(
        acts_front=(ran.acts_front, VMEM),
        acts_back=(ran.acts_back, VMEM),
        cell_front=(ran.cell_front, VMEM),
        cell_back=(ran.cell_back, VMEM),
        dec_front=(decs[0], VMEM),
        dec_back=(decs[1], VMEM),
        w_turned=(ran.w_turned, ANYWHERE),
    )
    gates = dict(
        gates_front=(length, rows, 4 * shard_units),
        gates_back=(half_len, rows, 4 * shard_units),
    )
    scratch = dict(
        weights=(pltpu.VMEM(ran.w_turned.shape, B16)),
        outbox=(pltpu.VMEM(box, F32)),
        inbox=(pltpu.VMEM(box, F32)),
        outbox_far=(pltpu.VMEM(far_box, B16)),
        inbox_far=(pltpu.VMEM(far_box, B16)),
        own_part=(pltpu.VMEM((2, rows, shard_units), F32)),
        cell_grad=(pltpu.VMEM((2, rows, shard_units), F32)),
        load_sem=(dma((2,))),
        send_sem=(dma((2, 2, links))),
        recv_sem=(dma((2, 2, links))),
    )
    outs = {key: (shape, B16, VMEM) for key, shape in gates.items()}
    body = functools.partial(backward_body, count)
    return call(body, "recurrence_backward", ins, outs, scratch, 1, 10**11)


def step_body(count, groups, factor, r):
    place = lax.axis_index("shard")
    group = lax.axis_index("rep")
    core = lax.rem(group, 2)
    sibling = group + 1 - 2 * core
    peers = peers_of(place, count)
    others = others_of(group, groups)
    units = r.weights.shape[3]
    length, half_len = r.full_front.shape[0], r.full_back.shape[0]
    ends = (length, half_len)
    rows = r.group_ids.shape[0]
    seq_dev = r.chars.shape[0]
    vocab, _, embed = r.embedding.shape
    wide = r.past_front.shape[3]
    fulls = (r.full_front, r.full_back)
    acts = (r.acts_front, r.acts_back)
    cells = (r.cell_front, r.cell_back)
    logit_grads = (r.logits_front, r.logits_back)
    pasts = (r.past_front, r.past_back)
    wides = (r.wide_front, r.wide_back)
    own_columns = span(place, units)

    inner = (place * (count - 1 - place)) // 2
    urgent = [
        (a + inner * (c - a), peers[a] + inner * (peers[c] - peers[a])) for a, c in ((2, 1), (1, 0), (0, 2))
    ]

    def to_peer(src, dst, send, recv, peer):
        return pltpu.make_async_remote_copy(
            src_ref=src,
            dst_ref=dst,
            send_sem=send,
            recv_sem=recv,
            device_id={"shard": peer},
            device_id_type=MESH,
        )

    def to_group(src, dst, send, recv, other):
        return pltpu.make_async_remote_copy(
            src_ref=src,
            dst_ref=dst,
            send_sem=send,
            recv_sem=recv,
            device_id={"rep": other},
            device_id_type=MESH,
        )

    loads = [pltpu.make_async_copy(r.w_rec.at[m], r.weights.at[m], r.load_sem.at[m]) for m in range(2)]
    for load in loads:
        load.start()
    barrier = pltpu.get_barrier_semaphore()
    for peer in peers:
        pl.semaphore_signal(barrier, inc=1, device_id={"shard": peer}, device_id_type=MESH)
    for other in others:
        pl.semaphore_signal(barrier, inc=1, device_id={"rep": other}, device_id_type=MESH)
    r.id_blocks[group, place, :seq_dev, :length] = r.chars[...]
    corner = (seq_dev, seq_dev)
    diagonal = lax.broadcasted_iota(jnp.int32, corner, 0) == lax.broadcasted_iota(jnp.int32, corner, 1)
    stops_across = jnp.broadcast_to(r.prefix[...], corner)
    r.id_blocks[group, place, :seq_dev, length : length + 1] = jnp.sum(
        jnp.where(diagonal, stops_across, 0), axis=1, keepdims=True
    )
    pl.semaphore_wait(barrier, len(peers) + len(others))

    def id_copy(k):
        block = r.id_blocks.at[group, place]
        return to_peer(block, block, r.id_send.at[k], r.id_recv.at[k], peers[k])

    def id_spread(j):
        block = r.id_blocks.at[group]
        return to_group(block, block, r.ids_send.at[j], r.ids_recv.at[j], others[j])

    for k in range(len(peers)):
        id_copy(k).start()
    lane = lax.broadcasted_iota(jnp.int32, r.table.shape, 2)
    r.table[...] = jnp.where(lane == embed, 1.0, 0.0).astype(B16)
    r.inputs[...] = jnp.zeros_like(r.inputs)
    for m in range(2):
        r.table[m, :vocab, :embed] = r.embedding[:, m, :]
        for g in range(4):
            r.inputs[m, g, :embed] = r.w_in[m, :, g, :]

    blanks = [pltpu.make_async_copy(r.blank, pasts[m].at[0], r.past_local.at[m]) for m in range(2)]

    def prepare_decoder():
        r.out_own[...] = jnp.zeros_like(r.out_own)
        r.out_bias[...] = jnp.full_like(r.out_bias, -1e30)
        r.out_bias[:, :vocab] = r.b_out[...].astype(F32)
        for m in range(2):
            r.out_own[m, :vocab] = r.w_out[:, m, :]
            r.out_full[m, place] = r.out_own[m].T.reshape(groups, units // groups, -1)
        r.out_sums[...] = jnp.zeros_like(r.out_sums)

    def prepare_sums():
        r.in_sums[...] = jnp.zeros_like(r.in_sums)
        r.embed_part[...] = jnp.zeros_like(r.embed_part)
        r.rec_sums[...] = jnp.zeros_like(r.rec_sums)

    def share_copy(n):
        k, m = len(peers) - 1 - n // 2, n % 2
        block = r.out_full.at[m, place, group]
        return to_peer(block, block, r.share_send.at[n], r.share_recv.at[n], peers[k])

    def share_spread(j, k):
        source = r.out_full.at[:, peers[k], group]
        other = lax.rem(group + 1 + j, groups)
        return to_group(source, source, r.all_send.at[j, k], r.all_recv.at[j, k], other)

    first_spread = 2 * len(peers) + 3

    def send_shares(t):
        for n in range(2 * len(peers)):
            pl.when(t == n + 1)(share_copy(n).start)

        @pl.when(t == first_spread - 1)
        def _():
            for n in range(2 * len(peers)):
                share_copy(n).wait()

        @pl.when(jnp.logical_and(t >= first_spread, t < first_spread + groups - 1))
        def _():
            for k in range(len(peers)):
                share_spread(t - first_spread, k).start()

    def spread_past(m, t):
        for j, other in enumerate(others):
            to_group(
                fulls[m].at[t, :, span(other // 2, wide)],
                pasts[m].at[t + 1, group],
                r.past_send.at[m, j],
                r.past_recv.at[m, j],
                other,
            ).start()
        pltpu.make_async_copy(
            fulls[m].at[t, :, span(group // 2, wide)], pasts[m].at[t + 1, group], r.past_local.at[m]
        ).start()

    def finish_past(m, steps):
        for j, other in enumerate(others):
            part = pasts[m].at[pl.ds(1, steps), 0]
            copy = to_group(part, part, r.past_send.at[m, j], r.past_recv.at[m, j], other)
            copy.wait_send()
            copy.wait_recv()
        mine = pasts[m].at[pl.ds(1, steps), 0]
        pltpu.make_async_copy(mine, mine, r.past_local.at[m]).wait()

    def exchange(m, t, k, peer):
        slot = lax.rem(t, 2)
        own = fulls[m].at[t, :, own_columns]
        return to_peer(own, own, r.hidden_send.at[m, slot, k], r.hidden_recv.at[m, slot, k], peer)

    def finish(m, t, sums, memory):
        in_gate = jax.nn.sigmoid(sums[0])
        forget = jax.nn.sigmoid(sums[1])
        candidate = jnp.tanh(sums[2])
        out_gate = jax.nn.sigmoid(sums[3])
        new_memory = in_gate * candidate if memory is None else forget * memory + in_gate * candidate
        fulls[m][t, :, own_columns] = (out_gate * jnp.tanh(new_memory)).astype(B16)
        for k, peer in urgent:
            exchange(m, t, k, peer).start()
        for g, value in enumerate((in_gate, forget, candidate, out_gate)):
            acts[m][t, g] = value
        cells[m][t] = new_memory

    def start_sums(m, t):
        ids, stops = r.group_ids[...], r.group_ids[:, length : length + 1]
        x_t = dot(marks(id_column(ids, stops, m, t), r.table.shape[1]), r.table[m]).astype(B16)
        return [
            r.gate_bias[m, g : g + 1, :].astype(F32) + dot(x_t, r.inputs[m, g]) for g in range(4)
        ]

    def add_chunk(m, t, owner, sums):
        part = fulls[m][t, :, span(owner, units)]
        return [sums[g] + dot(part, r.weights[m, g, span(owner, units), :]) for g in range(4)]

    def advance(m, t):
        sums = add_chunk(m, t - 1, place, start_sums(m, t))
        for k in range(len(peers)):
            exchange(m, t - 1, k, peers[k]).wait_recv()
            sums = add_chunk(m, t - 1, peers[k], sums)
        finish(m, t, sums, cells[m][t - 1])
        for k in range(len(peers)):
            exchange(m, t - 1, k, peers[k]).wait_send()
        spread_past(m, t - 1)

    def turn_block(m, g, p):
        r.weights[m, g, span(p, units), :] = r.weights[m, g, span(p, units), :].T

    stretch = 4

    def decode(m, chunk):
        t0 = stretch * chunk
        hidden = fulls[m][pl.ds(t0, stretch)].reshape(stretch * rows, count * units)
        logits = dot(hidden, r.out_full[m].reshape(count * units, -1)) + r.out_bias[m : m + 1, :]
        grown = jnp.exp(logits - jnp.max(logits, axis=1, keepdims=True))
        chances = grown / jnp.sum(grown, axis=1, keepdims=True)
        ids, stops = r.group_ids[...], r.group_ids[:, length : length + 1]
        targets, active = [], []
        for i in range(stretch):
            t = t0 + i
            if m == 0:
                targets.append(column_of(ids, lax.rem(t + 1, length)))
                live = jnp.full((rows, 1), t, jnp.int32) < length - 1
            else:
                targets.append(column_of(ids, jnp.maximum(stops - 2 - t, 0)))
                live = stops >= t + 2
            active.append(jnp.where(live, factor, 0.0).astype(F32))
        target, weight = jnp.concatenate(targets, axis=0), jnp.concatenate(active, axis=0)
        lane = lax.broadcasted_iota(jnp.int32, logits.shape, 1)
        picked = (lane == target).astype(F32)
        grad = ((chances - picked) * weight).astype(B16)
        logit_grads[m][pl.ds(t0, stretch)] = grad.reshape(stretch, rows, -1)
        own = fulls[m][pl.ds(t0, stretch), :, own_columns].reshape(stretch * rows, units)
        ones = jnp.ones((stretch * rows, LANES), B16)
        r.out_sums[m] += dot_first(grad, jnp.concatenate([own, ones], axis=1))

    piece = r.out_inbox.shape[2]

    def out_send(m, j):
        other = lax.rem(group + 1 + j, groups)
        return to_group(
            r.out_sums.at[m, span(other, piece)],
            r.out_inbox.at[m, j],
            r.out_send.at[m, j],
            r.out_recv.at[m, j],
            other,
        )

    def out_share(m, j):
        own = r.out_total.at[m, span(group, piece)]
        other = lax.rem(group + 1 + j, groups)
        return to_group(own, own, r.total_send.at[m, j], r.total_recv.at[m, j], other)

    def out_reduce(m):
        total = r.out_sums[m, span(group, piece)]
        for j in range(groups - 1):
            copy = out_send(m, j)
            copy.wait_send()
            copy.wait_recv()
        for j in range(groups - 1):
            total = total + r.out_inbox[m, j]
        r.out_total[m, span(group, piece)] = total

    def out_steps(m, n):
        pl.when(jnp.logical_and(n >= 0, n < groups - 1))(lambda: out_send(m, n).start())
        pl.when(n == groups)(lambda: out_reduce(m))
        ready = jnp.logical_and(n > groups, n < 2 * groups)
        pl.when(ready)(lambda: out_share(m, n - groups - 1).start())

    gates = fulls

    def spread_gates(m, t):
        for j, other in enumerate(others):
            to_group(
                gates[m].at[t, :, span(lax.rem(other, 2), 2 * units)],
                wides[m].at[t, group],
                r.wide_send.at[m, j],
                r.wide_recv.at[m, t // 2],
                other,
            ).start()
        pltpu.make_async_copy(
            gates[m].at[t, :, span(core, 2 * units)], wides[m].at[t, group], r.wide_local.at[m, t // 2]
        ).start()

    def arrive(m, pair):
        far = wides[m].at[pl.ds(2 * pair, 2), pl.ds(0, groups - 1)]
        to_group(far, far, r.wide_send.at[m, 0], r.wide_recv.at[m, pair], others[0]).wait_recv()
        near = wides[m].at[pl.ds(2 * pair, 2), 0]
        pltpu.make_async_copy(near, near, r.wide_local.at[m, pair]).wait()

    def fetches(m, pair):
        slot = lax.rem(pair, 2)
        return (
            pltpu.make_async_copy(
                wides[m].at[pl.ds(2 * pair, 2)], r.wide_slot.at[m, slot], r.fetch_sem.at[m, slot, 0]
            ),
            pltpu.make_async_copy(
                pasts[m].at[pl.ds(2 * pair, 2)], r.past_slot.at[m, slot], r.fetch_sem.at[m, slot, 1]
            ),
        )

    def fetch(m, pair):
        arrive(m, pair)
        for copy in fetches(m, pair):
            copy.start()

    def accumulate(m, pair):
        slot = lax.rem(pair, 2)
        for copy in fetches(m, pair):
            copy.wait()
        dz = r.wide_slot[m, slot].reshape(-1, 2 * units)
        past = r.past_slot[m, slot].reshape(dz.shape[0], -1)
        r.rec_sums[m] += dot_first(past, dz)
        ids, stops = r.every_ids[...], r.every_ids[:, length : length + 1]
        spots = [marks(id_column(ids, stops, m, 2 * pair + i), r.table.shape[1]) for i in range(2)]
        spots = jnp.concatenate(spots, axis=0)
        r.in_sums[m] += dot_first(dot(spots, r.table[m]).astype(B16), dz)
        grad_x = None
        for g in range(2):
            term = dot_last(dz[:, g * units : (g + 1) * units], r.inputs[m, 2 * core + g])
            grad_x = term if grad_x is None else grad_x + term
        for part in split_three(grad_x):
            r.embed_part[m] += dot_first(spots, part)

    def give(m, t, k, peer):
        slot = lax.rem(t, 2)
        return to_peer(
            r.outbox.at[m, slot, k],
            r.inbox.at[m, slot, k],
            r.grad_send.at[m, slot, k],
            r.grad_recv.at[m, slot, k],
            peer,
        )

    def slopes(m, t, prev_memory):
        in_gate, forget, candidate, out_gate = (acts[m][t, g] for g in range(4))
        squashed = jnp.tanh(cells[m][t])
        forget_slope = jnp.zeros_like(forget)
        if prev_memory is not None:
            forget_slope = prev_memory * forget * (1.0 - forget)
        return (
            candidate * in_gate * (1.0 - in_gate),
            forget_slope,
            in_gate * (1.0 - candidate * candidate),
            squashed * out_gate * (1.0 - out_gate),
            out_gate * (1.0 - squashed * squashed),
            forget,
        )

    def gate_grads(m, t, slope, grad_hidden, carried):
        grad_memory = grad_hidden * slope[4]
        if carried is not None:
            grad_memory = carried + grad_memory
        values = [grad_memory * slope[g] for g in range(3)] + [grad_hidden * slope[3]]
        for g, value in enumerate(values):
            gates[m][t, :, g * units : (g + 1) * units] = value.astype(B16)
        r.cell_grad[m] = grad_memory * slope[5]

    def product(m, t, owner):
        total = None
        for g in range(4):
            part = dot(
                gates[m][t, :, g * units : (g + 1) * units], r.weights[m, g, span(owner, units), :]
            )
            total = part if total is None else total + part
        return total

    def from_decoder(m, t):
        return dot(logit_grads[m][t], r.out_own[m])

    def send_products(m, t):
        for k, peer in urgent:
            r.outbox[m, lax.rem(t, 2), k] = product(m, t, peer).astype(B16)
            give(m, t, k, peer).start()
        r.own_part[m] = product(m, t, place) + from_decoder(m, t - 1)
        spread_gates(m, t)

    def incoming(m, t):
        total = r.own_part[m]
        for k in range(len(peers)):
            give(m, t, k, peers[k]).wait_recv()
            total = total + r.inbox[m, lax.rem(t, 2), k].astype(F32)
        return total

    def sent(m, t):
        for k in range(len(peers)):
            give(m, t, k, peers[k]).wait_send()

    def retreat(m, t):
        slope = slopes(m, t, cells[m][t - 1])
        gate_grads(m, t, slope, incoming(m, t + 1), r.cell_grad[m])
        send_products(m, t)
        sent(m, t + 1)

    def first(m):
        t = ends[m] - 1
        gate_grads(m, t, slopes(m, t, cells[m][t - 1]), from_decoder(m, t), None)
        send_products(m, t)

    def last(m):
        slope = slopes(m, 0, None)
        gate_grads(m, 0, slope, incoming(m, 1), r.cell_grad[m])
        spread_gates(m, 0)
        sent(m, 1)

    depth = r.rec_grad.shape[2]
    kept = r.in_all.shape[2]

    def swap(m, g, i):
        source, target = (
            (r.rec_sums.at[m, span(1 - core, depth), pl.ds(g * units, units)], r.rec_grad),
            (r.in_sums.at[m, pl.ds(0, kept), pl.ds(g * units, units)], r.in_all),
        )[i]
        target = target.at[m, 2 * core + g]
        return to_group(source, target, r.swap_send.at[i, m, g], r.swap_recv.at[i, m, g], sibling)

    def keep(m, g):
        return pltpu.make_async_copy(
            r.rec_sums.at[m, span(core, depth), pl.ds(g * units, units)],
            r.rec_grad.at[m, 2 * core + g],
            r.keep_sem.at[m, g],
        )

    def start_swaps(m):
        for g in range(2):
            swap(m, g, 1).start()
        for g in range(2):
            swap(m, g, 0).start()
            keep(m, g).start()
            r.in_all[m, 2 * core + g] = r.in_sums[m, :kept, g * units : (g + 1) * units]

    def finish_inputs(m):
        for g in range(2):
            swap(m, g, 1).wait()
        for g in range(4):
            r.grad_in[m, :, g, :] = r.in_all[m, g, :embed]
        r.grad_bias[m] = r.in_all[m, :, embed, :]

    def finish_swaps(m):
        for g in range(2):
            swap(m, g, 0).wait()
            keep(m, g).wait()

    half = r.embed_half.shape[1]
    slice_rows = half // count

    def embed_pair(m):
        return to_group(
            r.embed_part.at[m, span(1 - core, half)],
            r.embed_half.at[m],
            r.embed_send.at[m, 0],
            r.embed_recv.at[m, 0],
            sibling,
        )

    def embed_reduce(m, k):
        return to_peer(
            r.embed_half.at[m, span(peers[k], slice_rows)],
            r.embed_inbox.at[m, k],
            r.reduce_send.at[m, k],
            r.reduce_recv.at[m, k],
            peers[k],
        )

    def own_slice(m):
        first_row = pl.multiple_of(core * half + place * slice_rows, 8)
        return r.embed_full.at[m, pl.ds(first_row, slice_rows)]

    def embed_gather(m, k):
        return to_peer(
            own_slice(m), own_slice(m), r.gather_send.at[m, k], r.gather_recv.at[m, k], peers[k]
        )

    def embed_return(m):
        whole = r.embed_full.at[m, span(core, half)]
        return to_group(whole, whole, r.embed_send.at[m, 1], r.embed_recv.at[m, 1], sibling)

    def embed_stage(m, stage):
        if stage == 0:
            embed_pair(m).start()
        elif stage == 1:
            embed_pair(m).wait()
            r.embed_half[m] += r.embed_part[m, span(core, half)]
            for k in reversed(range(len(peers))):
                embed_reduce(m, k).start()
        elif stage == 2:
            total = r.embed_half[m, span(place, slice_rows)]
            for k in range(len(peers)):
                embed_reduce(m, k).wait()
                total = total + r.embed_inbox[m, k]
            own_slice(m)[...] = total
            for k in reversed(range(len(peers))):
                embed_gather(m, k).start()
        elif stage == 3:
            for k in range(len(peers)):
                embed_gather(m, k).wait()
            embed_return(m).start()
        else:
            embed_return(m).wait()
            r.grad_embed[:, m, :] = r.embed_full[m, :vocab, :embed]

    for k in range(len(peers)):
        id_copy(k).wait()
    for s in range(count):
        r.group_ids[s * seq_dev : (s + 1) * seq_dev] = r.id_blocks[group, s, :seq_dev]
    for j in range(len(others)):
        id_spread(j).start()
    for m in range(2):
        finish(m, 0, start_sums(m, 0), None)
    r.blank[...] = jnp.zeros_like(r.blank)
    for copy in blanks:
        copy.start()
    prepare_decoder()
    for copy in blanks:
        copy.wait()
    for load in loads:
        load.wait()

    shared = first_spread + groups

    def both(t, carry):
        advance(0, t)
        advance(1, t)
        send_shares(t)
        pl.when(t == 2)(prepare_sums)

        @pl.when(t == shared)
        def _():
            for j in range(groups - 1):
                for k in range(len(peers)):
                    share_spread(j, k).wait()

        chunk = t - shared - 1
        pl.when(jnp.logical_and(chunk >= 0, stretch * (chunk + 1) <= t))(lambda: decode(0, chunk))
        return carry

    decoded = 0
    while stretch * (decoded + 1) <= shared + 1 + decoded and shared + 1 + decoded < half_len:
        decoded += 1

    def settle(m):
        for k in range(len(peers)):
            exchange(m, ends[m] - 1, k, peers[k]).wait()

    back_chunks = half_len // stretch
    blocks = 4 * count
    begin = 3
    back_pairs = half_len // 2
    front_pairs = length // 2
    assert half_len % stretch == 0 and length == 2 * half_len and half_len % 2 == 0
    assert first_spread + groups - 1 <= half_len
    assert back_chunks == 2 * begin and blocks <= 6 * begin and groups < half_len // 2

    def front_only(t, carry):
        advance(0, t)
        n = t - half_len

        @pl.when(n < begin)
        def _():
            for i in range(2):
                decode(1, back_chunks - 1 - 2 * n - i)
            for i in range(6):
                block = 6 * n + i
                pl.when(block < blocks)(lambda: turn_block(1, block // count, lax.rem(block, count)))

        @pl.when(n == begin)
        def _():
            finish_past(1, half_len - 1)
            first(1)

        pl.when(n > begin)(lambda: retreat(1, half_len - 1 - (n - begin)))
        begun = n >= begin
        chunk = n - begin + decoded
        early = jnp.logical_and(begun, stretch * (chunk + 1) <= t)
        late = jnp.logical_and(stretch * (chunk + 1) > t, lax.rem(t, stretch) == 0)
        pl.when(early)(lambda: decode(0, chunk))
        pl.when(jnp.logical_and(begun, late))(lambda: decode(0, t // stretch - 1))
        behind = n - begin - 5
        even = jnp.logical_and(behind >= 0, lax.rem(n - begin, 2) == 1)
        odd = jnp.logical_and(behind >= 1, lax.rem(n - begin, 2) == 0)
        pl.when(even)(lambda: fetch(1, back_pairs - 1 - behind // 2))
        pl.when(odd)(lambda: accumulate(1, back_pairs - 1 - behind // 2))
        return carry

    lax.fori_loop(1, half_len, both, 0)
    settle(1)
    for j in range(len(others)):
        id_spread(j).wait()
    r.every_ids[...] = r.id_blocks[:, :, :seq_dev].reshape(r.every_ids.shape)
    lax.fori_loop(half_len, length, front_only, 0)
    for g in range(4):
        for p in range(count):
            turn_block(0, g, p)
    settle(0)
    decode(0, length // stretch - 1)
    finish_past(0, length - 1)

    first(0)
    retreat(1, begin - 1)
    retreat(0, length - 2)
    retreat(1, begin - 2)
    fetched = (half_len - begin - 5) // 2
    left = back_pairs - fetched
    after = left + 2

    def turn(step, carry):
        retreat(0, length - 1 - 2 * step)
        pl.when(step == 1)(lambda: last(1))
        pl.when(step >= 3)(lambda: fetch(0, front_pairs + 2 - step))
        remaining = jnp.logical_and(step >= 2, step < left + 2)
        pl.when(remaining)(lambda: fetch(1, left + 1 - step))
        for stage in range(5):
            pl.when(step == after + stage)(lambda stage=stage: embed_stage(1, stage))
        pl.when(step == after)(lambda: start_swaps(1))
        pl.when(step == after + 2)(lambda: finish_inputs(1))
        retreat(0, length - 2 - 2 * step)
        pl.when(step >= 3)(lambda: accumulate(0, front_pairs + 2 - step))
        pl.when(remaining)(lambda: accumulate(1, left + 1 - step))
        out_steps(0, step - 1)
        out_steps(1, step - 1)
        return carry

    final = half_len - 1
    assert begin == 3 and after + 5 <= final
    lax.fori_loop(1, final, turn, 0)
    retreat(0, 1)
    fetch(0, 3)
    last(0)
    fetch(0, 2)
    accumulate(0, 3)
    accumulate(0, 2)
    fetch(0, 1)
    for m in range(2):
        for j in range(groups - 1):
            out_share(m, j).wait()
        r.grad_out[:, m, :] = r.out_total[m, :vocab, :units]
        r.grad_bout[m : m + 1, :] = r.out_total[m, :, units:].T[:1, :vocab]
    finish_swaps(1)
    accumulate(0, 1)
    fetch(0, 0)
    accumulate(0, 0)
    embed_stage(0, 0)
    start_swaps(0)
    embed_stage(0, 1)
    for m in range(2):
        for j in range(groups - 1):
            part = wides[m].at[:, 0]
            to_group(part, part, r.wide_send.at[m, j], r.wide_recv.at[m, 0], others[j]).wait_send()
    embed_stage(0, 2)
    finish_inputs(0)
    finish_swaps(0)
    embed_stage(0, 3)
    embed_stage(0, 4)


def run_step(count, groups, factor, char_ids, prefix, embedding, w_in, w_rec, gate_bias, w_out, b_out):
    seq_dev, length = char_ids.shape
    half_len = length // 2
    units, shard_units = w_rec.shape[2:]
    vocab, embed = embedding.shape[1:]
    rows = seq_dev * count
    wide = units // (groups // 2)
    depth = -(-(embed + 1) // LANES) * LANES
    lanes = -(-vocab // LANES) * LANES
    reduced = -(-vocab // (16 * count)) * 8 * count
    padded = 2 * reduced
    piece = lanes // groups
    links = count - 1
    far = groups - 1
    dma = pltpu.SemaphoreType.DMA
    ins = dict(
        chars=(char_ids, VMEM),
        prefix=(prefix[None], VMEM),
        embedding=(embedding.transpose(1, 0, 2), VMEM),
        w_in=(w_in.transpose(0, 2, 1, 3), VMEM),
        gate_bias=(gate_bias, VMEM),
        w_out=(w_out.transpose(2, 0, 1), VMEM),
        b_out=(b_out, VMEM),
        w_rec=(w_rec, ANYWHERE),
    )
    outs = dict(
        grad_embed=((vocab, 2, embed), F32, VMEM),
        grad_in=((2, embed, 4, shard_units), F32, VMEM),
        rec_grad=((2, 4, wide // 2, shard_units), F32, ANYWHERE),
        grad_bias=((2, 4, shard_units), F32, VMEM),
        grad_out=((vocab, 2, shard_units), F32, VMEM),
        grad_bout=((2, vocab), F32, VMEM),
        past_front=((length, groups, rows, wide), B16, ANYWHERE),
        past_back=((half_len, groups, rows, wide), B16, ANYWHERE),
        wide_front=((length, groups, rows, 2 * shard_units), B16, ANYWHERE),
        wide_back=((half_len, groups, rows, 2 * shard_units), B16, ANYWHERE),
    )
    arrays = dict(
        weights=(w_rec.shape, B16),
        out_bias=((2, lanes), F32),
        out_full=((2, count, groups, shard_units // groups, lanes), B16),
        id_blocks=((groups, count, max(8, seq_dev), LANES), jnp.int32),
        group_ids=((rows, LANES), jnp.int32),
        every_ids=((groups * rows, LANES), jnp.int32),
        blank=((groups, rows, wide), B16),
        full_front=((length, rows, units), B16),
        full_back=((half_len, rows, units), B16),
        acts_front=((length, 4, rows, shard_units), F32),
        acts_back=((half_len, 4, rows, shard_units), F32),
        cell_front=((length, rows, shard_units), F32),
        cell_back=((half_len, rows, shard_units), F32),
        logits_front=((length, rows, lanes), B16),
        logits_back=((half_len, rows, lanes), B16),
        out_sums=((2, lanes, shard_units + LANES), F32),
        out_inbox=((2, far, piece, shard_units + LANES), F32),
        out_total=((2, lanes, shard_units + LANES), F32),
        outbox=((2, 2, links, rows, shard_units), B16),
        inbox=((2, 2, links, rows, shard_units), B16),
        own_part=((2, rows, shard_units), F32),
        cell_grad=((2, rows, shard_units), F32),
        rec_sums=((2, wide, 2 * shard_units), F32),
        in_sums=((2, depth, 2 * shard_units), F32),
        in_all=((2, 4, -(-(embed + 1) // 8) * 8, shard_units), F32),
        table=((2, padded, depth), B16),
        inputs=((2, 4, depth, shard_units), B16),
        out_own=((2, lanes, shard_units), B16),
        embed_part=((2, padded, depth), F32),
        embed_half=((2, reduced, depth), F32),
        embed_full=((2, padded, depth), F32),
        embed_inbox=((2, links, reduced // count, depth), F32),
        wide_slot=((2, 2, 2, groups, rows, 2 * shard_units), B16),
        past_slot=((2, 2, 2, groups, rows, wide), B16),
    )
    semaphores = dict(
        load_sem=(2,),
        id_send=(links,),
        id_recv=(links,),
        ids_send=(far,),
        ids_recv=(far,),
        share_send=(2 * links,),
        share_recv=(2 * links,),
        all_send=(far, links),
        all_recv=(far, links),
        past_send=(2, far),
        past_recv=(2, far),
        past_local=(2,),
        hidden_send=(2, 2, links),
        hidden_recv=(2, 2, links),
        out_send=(2, far),
        out_recv=(2, far),
        total_send=(2, far),
        total_recv=(2, far),
        wide_send=(2, far),
        wide_recv=(2, length // 2),
        wide_local=(2, length // 2),
        fetch_sem=(2, 2, 2),
        grad_send=(2, 2, links),
        grad_recv=(2, 2, links),
        swap_send=(2, 2, 2),
        swap_recv=(2, 2, 2),
        keep_sem=(2, 2),
        embed_send=(2, 2),
        embed_recv=(2, 2),
        reduce_send=(2, links),
        reduce_recv=(2, links),
        gather_send=(2, links),
        gather_recv=(2, links),
    )
    scratch = {key: pltpu.VMEM(shape, kind) for key, (shape, kind) in arrays.items()}
    scratch |= {key: dma(shape) for key, shape in semaphores.items()}
    body = functools.partial(step_body, count, groups, factor)
    return call(body, "lstm_step", ins, outs, scratch, 2, 10**11, resident=True)


def shifted(values):
    return jnp.concatenate([jnp.zeros_like(values[:1]), values[:-1]], axis=0)


def reduced_grads(ran, gates, embedding, w_in, ids, group_size):
    embed = embedding.shape[2]

    def per_model(full, grads, ids, m):
        grads = grads.reshape(grads.shape[0], group_size, 4, -1)
        rec = jnp.einsum("tbk,tbgn->gkn", shifted(full), grads, preferred_element_type=F32)
        spots = one_hot(ids, embedding.shape[1], B16)
        x = jnp.einsum("tbv,ve->tbe", spots, embedding[m], preferred_element_type=F32).astype(B16)
        in_grad = jnp.einsum("tbe,tbgn->gen", x, grads, preferred_element_type=F32)
        bias = jnp.sum(grads, axis=(0, 1), dtype=F32)
        dx = jnp.einsum("tbgn,gen->tbe", grads, w_in[m], preferred_element_type=F32)
        embed_grad = jnp.einsum("tbv,tbe->ve", spots.astype(F32), dx, precision=PRECISE)
        return rec, in_grad, bias, embed_grad

    parts = (
        per_model(ran.full_front, gates.gates_front, ids[0], 0),
        per_model(ran.full_back, gates.gates_back, ids[1], 1),
    )
    rec, in_grad, bias, embed_grad = (jnp.stack(values) for values in zip(*parts))
    rec_grad = lax.psum_scatter(rec, "rep", scatter_dimension=2, tiled=True)
    in_sum, bias_sum = lax.psum((in_grad, bias), "rep")
    embed_sum = lax.psum(embed_grad, ("rep", "shard"))
    return embed_sum, in_sum, rec_grad, bias_sum


def shards(char_ids, prefix, embedding, w_in, w_rec, gate_bias, w_out, b_out):
    seq_dev, length = char_ids.shape
    half_len = length // 2
    vocab_size, embed = embedding.shape[1:]
    shard_units = w_rec.shape[3]
    count, groups = lax.axis_size("shard"), lax.axis_size("rep")
    group_size = seq_dev * count
    factor = 1.0 / math.sqrt(groups * count * seq_dev * length)
    if groups == 8 and count == 4 and length == 48:
        done = run_step(
            count, groups, factor, char_ids, prefix, embedding, w_in, w_rec, gate_bias, w_out, b_out
        )
        return (
            done.grad_embed.transpose(1, 0, 2),
            done.grad_in.transpose(0, 2, 1, 3),
            done.rec_grad,
            done.grad_bias,
            done.grad_out.transpose(1, 2, 0),
            done.grad_bout,
        )
    own_ids = jnp.concatenate([char_ids, prefix[:, None]], axis=1)
    own_ids = jnp.pad(own_ids, ((0, 0), (0, LANES - length - 1)))
    full_out = lax.all_gather(w_out, "shard", axis=1, tiled=True)
    depth = -(-(embed + 1) // LANES) * LANES
    padded = -(-vocab_size // LANES) * LANES
    table = jnp.pad(embedding, ((0, 0), (0, 0), (0, 1)), constant_values=1)
    table = jnp.pad(table, ((0, 0), (0, padded - vocab_size), (0, depth - embed - 1)))
    inputs = jnp.pad(w_in, ((0, 0), (0, 0), (0, depth - embed), (0, 0)))
    ran = run_forward(count, length, own_ids, table, inputs, gate_bias.astype(F32), w_rec)
    group_chars, group_prefix = ran.group_ids[:, :length], ran.group_ids[:, length]
    front_in = group_chars.T
    front_target = jnp.concatenate([group_chars[:, 1:], group_chars[:, :1]], axis=1).T
    timeline = jnp.arange(length, dtype=jnp.int32)[:, None]
    front_active = jnp.broadcast_to((timeline < length - 1).astype(F32), (length, group_size))
    reverse_steps = jnp.arange(half_len, dtype=jnp.int32)[:, None]

    def back_pick(offset):
        spot = jnp.maximum(group_prefix[None, :] - offset - reverse_steps, 0)
        chosen = one_hot(spot, length, jnp.int32) * group_chars[None]
        return jnp.sum(chosen, axis=-1)

    back_target = back_pick(2)
    back_active = (reverse_steps <= group_prefix[None, :] - 2).astype(F32)
    first_unit = lax.axis_index("shard") * shard_units

    def decode(full, m, target, active):
        rows = full.reshape(-1, full.shape[-1])
        logits = dot(rows, full_out[m]) + b_out[m].astype(F32)
        grad = loss_grad(logits, target.reshape(-1), active.reshape(-1), factor)
        dec = dot_last(grad, w_out[m])
        own = lax.dynamic_slice_in_dim(rows, first_unit, shard_units, axis=1)
        out_grad = dot_first(own, grad)
        bout = jnp.sum(grad, axis=0, dtype=F32)
        return dec.reshape(full.shape[0], group_size, shard_units), out_grad, bout

    front_dec, front_out_grad, front_bout = decode(ran.full_front, 0, front_target, front_active)
    back_dec, back_out_grad, back_bout = decode(ran.full_back, 1, back_target, back_active)
    out_and_bout = jnp.stack(
        [
            jnp.concatenate([front_out_grad, front_bout[None]], axis=0),
            jnp.concatenate([back_out_grad, back_bout[None]], axis=0),
        ]
    )
    out_and_bout = lax.psum(out_and_bout, "rep")
    out_sum, bout_sum = out_and_bout[:, :shard_units], out_and_bout[:, shard_units]
    done = run_backward(count, ran, (front_dec, back_dec))
    embed_sum, in_sum, rec_grad, bias_sum = reduced_grads(
        ran, done, embedding, w_in, (front_in, back_pick(1)), group_size
    )
    return (embed_sum, in_sum, rec_grad, bias_sum, out_sum, bout_sum)


def solution(mesh):
    in_specs = (
        P(("rep", "shard"), None),
        P(("rep", "shard")),
        P(),
        P(None, None, None, "shard"),
        P(None, None, None, "shard"),
        P(None, None, "shard"),
        P(None, "shard", None),
        P(),
    )
    out_specs = (
        P(),
        P(None, None, None, "shard"),
        P(None, None, "rep", "shard"),
        P(None, None, "shard"),
        P(None, "shard", None),
        P(),
    )
    return jax.shard_map(shards, mesh=mesh, in_specs=in_specs, out_specs=out_specs, check_vma=False)
```

```python
import functools
import math
import types

import jax
import jax.numpy as jnp
from jax import lax
from jax.experimental import pallas as pl
from jax.experimental.pallas import tpu as pltpu
from jax.sharding import PartitionSpec as P

PRECISE = lax.Precision.HIGHEST
MESH = pl.DeviceIdType.MESH
LANES = 128
MIB = 1 << 20
B16 = jnp.bfloat16
F32 = jnp.float32
VMEM = pl.BlockSpec(memory_space=pltpu.VMEM)
ANYWHERE = pl.BlockSpec(memory_space=pl.ANY)


def one_hot(ids, width, out_type):
    return (ids[..., None] == jnp.arange(width, dtype=jnp.int32)).astype(out_type)


def loss_grad(logits, targets, active, factor):
    probabilities = jax.nn.softmax(logits, axis=-1)
    picked = one_hot(targets, logits.shape[-1], F32)
    return ((probabilities - picked) * (active * factor)[:, None]).astype(B16)


def peers_of(place, count):
    if count == 4:
        return [place + 1 - 2 * lax.rem(place, 2), lax.rem(place + 2, 4), 3 - place]
    if count == 2:
        return [1 - place]
    assert count == 1
    return []


def others_of(group, groups):
    return [lax.rem(group + j, groups) for j in range(1, groups)]


def greet(peers, others):
    barrier = pltpu.get_barrier_semaphore()
    for peer in peers:
        pl.semaphore_signal(barrier, inc=1, device_id={"shard": peer}, device_id_type=MESH)
    for other in others:
        pl.semaphore_signal(barrier, inc=1, device_id={"rep": other}, device_id_type=MESH)
    pl.semaphore_wait(barrier, len(peers) + len(others))


def span(index, size):
    return pl.ds(pl.multiple_of(index * size, size), size)


def dot(left, right):
    return jnp.dot(left, right, preferred_element_type=F32)


def dot_last(left, right):
    return lax.dot_general(left, right, (((1,), (1,)), ((), ())), preferred_element_type=F32)


def dot_first(left, right):
    return lax.dot_general(left, right, (((0,), (0,)), ((), ())), preferred_element_type=F32)


def column_of(ids, spot):
    lane = lax.broadcasted_iota(jnp.int32, ids.shape, 1)
    return jnp.sum(jnp.where(lane == spot, ids, 0), axis=1, keepdims=True)


def marks(column, width):
    lane = lax.broadcasted_iota(jnp.int32, (column.shape[0], width), 1)
    return (lane == column).astype(F32).astype(B16)


def id_column(ids, ends, m, t):
    return column_of(ids, t) if m == 0 else column_of(ids, jnp.maximum(ends - 1 - t, 0))


def split_three(value):
    first = value.astype(B16)
    rest = value - first.astype(F32)
    second = rest.astype(B16)
    return first, second, (rest - second.astype(F32)).astype(B16)


def call(body, name, ins, outs, scratch, collective_id, cost, resident=False):
    names = [*ins, *outs, *scratch]

    def result(shape, kind, spec):
        if resident and spec is VMEM:
            return pltpu.VMEM(shape, kind)
        return jax.ShapeDtypeStruct(shape, kind)

    def kernel(*refs):
        body(types.SimpleNamespace(**dict(zip(names, refs))))

    results = pl.pallas_call(
        kernel,
        out_shape=tuple(result(*out) for out in outs.values()),
        in_specs=[spec for _, spec in ins.values()],
        out_specs=tuple(spec for _, _, spec in outs.values()),
        scratch_shapes=list(scratch.values()),
        compiler_params=pltpu.CompilerParams(
            collective_id=collective_id,
            has_side_effects=True,
            vmem_limit_bytes=(59 if resident else 62) * MIB,
        ),
        cost_estimate=pl.CostEstimate(flops=cost, bytes_accessed=50 * MIB, transcendentals=0),
        name=name,
    )(*[value for value, _ in ins.values()])
    return types.SimpleNamespace(**dict(zip(outs, results)))


def forward_body(count, length, r):
    place = lax.axis_index("shard")
    peers = peers_of(place, count)
    units = r.weights.shape[3]
    half_len = length // 2
    seq_dev = r.own_ids.shape[0]
    loads = [pltpu.make_async_copy(r.w_rec.at[m], r.weights.at[m], r.load_sem.at[m]) for m in range(2)]
    for load in loads:
        load.start()
    r.id_blocks[place, :seq_dev] = r.own_ids[...]
    greet(peers, [])

    def id_copy(k):
        block = r.id_blocks.at[place]
        return pltpu.make_async_remote_copy(
            src_ref=block,
            dst_ref=block,
            send_sem=r.id_send.at[k],
            recv_sem=r.id_recv.at[k],
            device_id={"shard": peers[k]},
            device_id_type=MESH,
        )

    for k in range(len(peers)):
        id_copy(k).start()
    fulls = (r.full_front, r.full_back)
    acts = (r.acts_front, r.acts_back)
    cells = (r.cell_front, r.cell_back)
    def exchange(m, t, k):
        slot = lax.rem(t, 2)
        own = fulls[m].at[t, :, span(place, units)]
        return pltpu.make_async_remote_copy(
            src_ref=own,
            dst_ref=own,
            send_sem=r.send_sem.at[m, slot, k],
            recv_sem=r.recv_sem.at[m, slot, k],
            device_id={"shard": peers[k]},
            device_id_type=MESH,
        )

    def finish(m, t, sums, memory):
        in_gate = jax.nn.sigmoid(sums[0])
        forget = jax.nn.sigmoid(sums[1])
        candidate = jnp.tanh(sums[2])
        out_gate = jax.nn.sigmoid(sums[3])
        new_memory = in_gate * candidate if memory is None else forget * memory + in_gate * candidate
        fulls[m][t, :, span(place, units)] = (out_gate * jnp.tanh(new_memory)).astype(B16)
        for k in reversed(range(len(peers))):
            exchange(m, t, k).start()
        for g, value in enumerate((in_gate, forget, candidate, out_gate)):
            acts[m][t, g] = value
        cells[m][t] = new_memory

    def start_sums(m, t):
        ids, ends = r.group_ids[...], r.group_ids[:, length : length + 1]
        spots = marks(id_column(ids, ends, m, t), r.table.shape[1])
        x_t = dot(spots, r.table[m]).astype(B16)
        return [r.bias[m, g : g + 1] + dot(x_t, r.w_in[m, g]) for g in range(4)]

    def add_chunk(m, t, owner, sums):
        part = fulls[m][t, :, span(owner, units)]
        return [sums[g] + dot(part, r.weights[m, g, span(owner, units), :]) for g in range(4)]

    def advance(m, t):
        sums = add_chunk(m, t - 1, place, start_sums(m, t))
        for k in range(len(peers)):
            exchange(m, t - 1, k).wait_recv()
            sums = add_chunk(m, t - 1, peers[k], sums)
        for k in range(len(peers)):
            exchange(m, t - 1, k).wait_send()
        finish(m, t, sums, cells[m][t - 1])

    def turn_copy(slot, m, g, p):
        return pltpu.make_async_copy(
            r.turned.at[slot],
            r.w_turned.at[m, span(g, units), span(p, units)],
            r.turn_sem.at[slot],
        )

    blocks = 8 * count

    def turn(block, slot):
        m, g, p = block // (4 * count), lax.rem(block // count, 4), lax.rem(block, count)

        @pl.when(block < blocks)
        def _():
            @pl.when(block >= 2)
            def _():
                turn_copy(slot, 0, 0, 0).wait()

            r.turned[slot] = r.weights[m, g, span(p, units), :].T
            turn_copy(slot, m, g, p).start()

    for k in range(len(peers)):
        id_copy(k).wait_send()
        id_copy(k).wait_recv()
    for s in range(count):
        r.group_ids[s * seq_dev : (s + 1) * seq_dev] = r.id_blocks[s, :seq_dev]
    finish(0, 0, start_sums(0, 0), None)
    finish(1, 0, start_sums(1, 0), None)
    for load in loads:
        load.wait()

    def both(t, carry):
        advance(0, t)
        advance(1, t)
        return carry

    def front_only(t, carry):
        advance(0, t)
        turn(2 * (t - half_len), 0)
        turn(2 * (t - half_len) + 1, 1)
        return carry

    assert blocks <= 2 * (length - half_len)
    lax.fori_loop(1, half_len, both, 0)
    lax.fori_loop(half_len, length, front_only, 0)
    for m, end in ((0, length), (1, half_len)):
        for k in range(len(peers)):
            copy = exchange(m, end - 1, k)
            copy.wait_send()
            copy.wait_recv()
    for slot in range(2):
        turn_copy(slot, 0, 0, 0).wait()


def run_forward(count, length, own_ids, table, w_in, bias, w_rec):
    half_len = length // 2
    units, shard_units = w_rec.shape[2:]
    seq_dev = own_ids.shape[0]
    rows = seq_dev * count
    dma = pltpu.SemaphoreType.DMA
    links = max(count - 1, 1)
    ins = dict(
        own_ids=(own_ids, VMEM),
        table=(table, VMEM),
        w_in=(w_in, VMEM),
        bias=(bias, VMEM),
        w_rec=(w_rec, ANYWHERE),
    )
    outs = dict(
        full_front=((length, rows, units), B16, VMEM),
        full_back=((half_len, rows, units), B16, VMEM),
        acts_front=((length, 4, rows, shard_units), F32, VMEM),
        acts_back=((half_len, 4, rows, shard_units), F32, VMEM),
        cell_front=((length, rows, shard_units), F32, VMEM),
        cell_back=((half_len, rows, shard_units), F32, VMEM),
        group_ids=((rows, LANES), jnp.int32, VMEM),
        w_turned=((2, 4 * shard_units, units), B16, ANYWHERE),
    )
    scratch = dict(
        weights=(pltpu.VMEM(w_rec.shape, B16)),
        turned=(pltpu.VMEM((2, shard_units, shard_units), B16)),
        id_blocks=(pltpu.VMEM((count, max(8, seq_dev), LANES), jnp.int32)),
        load_sem=(dma((2,))),
        turn_sem=(dma((2,))),
        send_sem=(dma((2, 2, links))),
        recv_sem=(dma((2, 2, links))),
        id_send=(dma((links,))),
        id_recv=(dma((links,))),
    )
    body = functools.partial(forward_body, count, length)
    return call(body, "recurrence_forward", ins, outs, scratch, 0, 10**11)


def backward_body(count, r):
    place = lax.axis_index("shard")
    peers = peers_of(place, count)
    units = r.cell_front.shape[2]
    length, half_len = r.cell_front.shape[0], r.cell_back.shape[0]
    loads = [pltpu.make_async_copy(r.w_turned.at[m], r.weights.at[m], r.load_sem.at[m]) for m in range(2)]
    for load in loads:
        load.start()
    acts = (r.acts_front, r.acts_back)
    cells = (r.cell_front, r.cell_back)
    decs = (r.dec_front, r.dec_back)
    gates = (r.gates_front, r.gates_back)
    ends = (length, half_len)
    greet(peers, [])

    def box(side, m, t, k):
        slot = lax.rem(t, 2)
        if k == 0:
            return (r.outbox if side == 0 else r.inbox).at[m, slot]
        return (r.outbox_far if side == 0 else r.inbox_far).at[m, slot, k - 1]

    def exchange(m, t, k):
        slot = lax.rem(t, 2)
        return pltpu.make_async_remote_copy(
            src_ref=box(0, m, t, k),
            dst_ref=box(1, m, t, k),
            send_sem=r.send_sem.at[m, slot, k],
            recv_sem=r.recv_sem.at[m, slot, k],
            device_id={"shard": peers[k]},
            device_id_type=MESH,
        )

    def gate_grads(m, t, grad_hidden, carried, prev_memory):
        in_gate, forget, candidate, out_gate = (acts[m][t, g] for g in range(4))
        squashed = jnp.tanh(cells[m][t])
        grad_memory = grad_hidden * out_gate * (1.0 - squashed * squashed)
        if carried is not None:
            grad_memory = carried + grad_memory
        r.cell_grad[m] = grad_memory * forget
        forget_part = jnp.zeros_like(grad_memory)
        if prev_memory is not None:
            forget_part = grad_memory * prev_memory * forget * (1.0 - forget)
        values = (
            grad_memory * candidate * in_gate * (1.0 - in_gate),
            forget_part,
            grad_memory * in_gate * (1.0 - candidate * candidate),
            grad_hidden * squashed * out_gate * (1.0 - out_gate),
        )
        for g, value in enumerate(values):
            gates[m][t, :, g * units : (g + 1) * units] = value.astype(B16)

    def product(m, t, owner):
        return dot(gates[m][t], r.weights[m, :, span(owner, units)])

    def send_products(m, t):
        for k in reversed(range(len(peers))):
            target = box(0, m, t, k)
            target[...] = product(m, t, peers[k]).astype(target.dtype)
            exchange(m, t, k).start()
        r.own_part[m] = product(m, t, place)

    def incoming(m, t):
        total = decs[m][t - 1] + r.own_part[m]
        for k in range(len(peers)):
            exchange(m, t, k).wait_recv()
            total = total + box(1, m, t, k)[...].astype(F32)
        return total

    def sent(m, t):
        for k in range(len(peers)):
            exchange(m, t, k).wait_send()

    def retreat(m, t):
        gate_grads(m, t, incoming(m, t + 1), r.cell_grad[m], cells[m][t - 1])
        send_products(m, t)
        sent(m, t + 1)

    def first(m):
        t = ends[m] - 1
        gate_grads(m, t, decs[m][t], None, cells[m][t - 1])
        loads[m].wait()
        send_products(m, t)

    def last(m):
        gate_grads(m, 0, incoming(m, 1), r.cell_grad[m], None)
        sent(m, 1)

    assert half_len % 2 == 0 and length == 2 * half_len
    final = half_len - 1
    first(0)
    first(1)
    retreat(0, length - 2)

    def turn(step, carry):
        retreat(0, length - 1 - 2 * step)
        retreat(1, half_len - 1 - step)
        retreat(0, length - 2 - 2 * step)
        return carry

    lax.fori_loop(1, final, turn, 0)
    retreat(0, 1)
    last(1)
    last(0)


def run_backward(count, ran, decs):
    length, rows, shard_units = ran.cell_front.shape
    half_len = ran.cell_back.shape[0]
    units = ran.w_turned.shape[2]
    links = max(count - 1, 1)
    dma = pltpu.SemaphoreType.DMA
    box = (2, 2, rows, shard_units)
    far_box = (2, 2, max(links - 1, 1), rows, shard_units)
    ins = dict(
        acts_front=(ran.acts_front, VMEM),
        acts_back=(ran.acts_back, VMEM),
        cell_front=(ran.cell_front, VMEM),
        cell_back=(ran.cell_back, VMEM),
        dec_front=(decs[0], VMEM),
        dec_back=(decs[1], VMEM),
        w_turned=(ran.w_turned, ANYWHERE),
    )
    gates = dict(
        gates_front=(length, rows, 4 * shard_units),
        gates_back=(half_len, rows, 4 * shard_units),
    )
    scratch = dict(
        weights=(pltpu.VMEM(ran.w_turned.shape, B16)),
        outbox=(pltpu.VMEM(box, F32)),
        inbox=(pltpu.VMEM(box, F32)),
        outbox_far=(pltpu.VMEM(far_box, B16)),
        inbox_far=(pltpu.VMEM(far_box, B16)),
        own_part=(pltpu.VMEM((2, rows, shard_units), F32)),
        cell_grad=(pltpu.VMEM((2, rows, shard_units), F32)),
        load_sem=(dma((2,))),
        send_sem=(dma((2, 2, links))),
        recv_sem=(dma((2, 2, links))),
    )
    outs = {key: (shape, B16, VMEM) for key, shape in gates.items()}
    body = functools.partial(backward_body, count)
    return call(body, "recurrence_backward", ins, outs, scratch, 1, 10**11)


def step_body(count, groups, factor, r):
    place = lax.axis_index("shard")
    group = lax.axis_index("rep")
    core = lax.rem(group, 2)
    sibling = group + 1 - 2 * core
    peers = peers_of(place, count)
    others = others_of(group, groups)
    units = r.weights.shape[3]
    length, half_len = r.full_front.shape[0], r.full_back.shape[0]
    ends = (length, half_len)
    rows = r.group_ids.shape[0]
    seq_dev = r.chars.shape[0]
    vocab, _, embed = r.embedding.shape
    wide = r.past_front.shape[3]
    fulls = (r.full_front, r.full_back)
    acts = (r.acts_front, r.acts_back)
    cells = (r.cell_front, r.cell_back)
    logit_grads = (r.logits_front, r.logits_back)
    pasts = (r.past_front, r.past_back)
    wides = (r.wide_front, r.wide_back)
    own_columns = span(place, units)

    inner = (place * (count - 1 - place)) // 2
    urgent = [
        (a + inner * (c - a), peers[a] + inner * (peers[c] - peers[a])) for a, c in ((2, 1), (1, 0), (0, 2))
    ]

    def to_peer(src, dst, send, recv, peer):
        return pltpu.make_async_remote_copy(
            src_ref=src,
            dst_ref=dst,
            send_sem=send,
            recv_sem=recv,
            device_id={"shard": peer},
            device_id_type=MESH,
        )

    def to_group(src, dst, send, recv, other):
        return pltpu.make_async_remote_copy(
            src_ref=src,
            dst_ref=dst,
            send_sem=send,
            recv_sem=recv,
            device_id={"rep": other},
            device_id_type=MESH,
        )

    loads = [pltpu.make_async_copy(r.w_rec.at[m], r.weights.at[m], r.load_sem.at[m]) for m in range(2)]
    for load in loads:
        load.start()
    barrier = pltpu.get_barrier_semaphore()
    for peer in peers:
        pl.semaphore_signal(barrier, inc=1, device_id={"shard": peer}, device_id_type=MESH)
    for other in others:
        pl.semaphore_signal(barrier, inc=1, device_id={"rep": other}, device_id_type=MESH)
    r.id_blocks[group, place, :seq_dev, :length] = r.chars[...]
    corner = (seq_dev, seq_dev)
    diagonal = lax.broadcasted_iota(jnp.int32, corner, 0) == lax.broadcasted_iota(jnp.int32, corner, 1)
    stops_across = jnp.broadcast_to(r.prefix[...], corner)
    r.id_blocks[group, place, :seq_dev, length : length + 1] = jnp.sum(
        jnp.where(diagonal, stops_across, 0), axis=1, keepdims=True
    )
    pl.semaphore_wait(barrier, len(peers) + len(others))

    def id_copy(k):
        block = r.id_blocks.at[group, place]
        return to_peer(block, block, r.id_send.at[k], r.id_recv.at[k], peers[k])

    def id_spread(j):
        block = r.id_blocks.at[group]
        return to_group(block, block, r.ids_send.at[j], r.ids_recv.at[j], others[j])

    for k in range(len(peers)):
        id_copy(k).start()
    lane = lax.broadcasted_iota(jnp.int32, r.table.shape, 2)
    r.table[...] = jnp.where(lane == embed, 1.0, 0.0).astype(B16)
    r.inputs[...] = jnp.zeros_like(r.inputs)
    for m in range(2):
        r.table[m, :vocab, :embed] = r.embedding[:, m, :]
        for g in range(4):
            r.inputs[m, g, :embed] = r.w_in[m, :, g, :]

    blanks = [pltpu.make_async_copy(r.blank, pasts[m].at[0], r.past_local.at[m]) for m in range(2)]

    def prepare_decoder():
        r.out_own[...] = jnp.zeros_like(r.out_own)
        r.out_bias[...] = jnp.full_like(r.out_bias, -1e30)
        r.out_bias[:, :vocab] = r.b_out[...].astype(F32)
        for m in range(2):
            r.out_own[m, :vocab] = r.w_out[:, m, :]
            r.out_full[m, place] = r.out_own[m].T.reshape(groups, units // groups, -1)
        r.out_sums[...] = jnp.zeros_like(r.out_sums)

    def prepare_sums():
        r.in_sums[...] = jnp.zeros_like(r.in_sums)
        r.embed_part[...] = jnp.zeros_like(r.embed_part)
        r.rec_sums[...] = jnp.zeros_like(r.rec_sums)

    def share_copy(n):
        k, m = len(peers) - 1 - n // 2, n % 2
        block = r.out_full.at[m, place, group]
        return to_peer(block, block, r.share_send.at[n], r.share_recv.at[n], peers[k])

    def share_spread(j, k):
        source = r.out_full.at[:, peers[k], group]
        other = lax.rem(group + 1 + j, groups)
        return to_group(source, source, r.all_send.at[j, k], r.all_recv.at[j, k], other)

    first_spread = 2 * len(peers) + 3

    def send_shares(t):
        for n in range(2 * len(peers)):
            pl.when(t == n + 1)(share_copy(n).start)

        @pl.when(t == first_spread - 1)
        def _():
            for n in range(2 * len(peers)):
                share_copy(n).wait()

        @pl.when(jnp.logical_and(t >= first_spread, t < first_spread + groups - 1))
        def _():
            for k in range(len(peers)):
                share_spread(t - first_spread, k).start()

    def spread_past(m, t):
        for j, other in enumerate(others):
            to_group(
                fulls[m].at[t, :, span(other // 2, wide)],
                pasts[m].at[t + 1, group],
                r.past_send.at[m, j],
                r.past_recv.at[m, j],
                other,
            ).start()
        pltpu.make_async_copy(
            fulls[m].at[t, :, span(group // 2, wide)], pasts[m].at[t + 1, group], r.past_local.at[m]
        ).start()

    def finish_past(m, steps):
        for j, other in enumerate(others):
            part = pasts[m].at[pl.ds(1, steps), 0]
            copy = to_group(part, part, r.past_send.at[m, j], r.past_recv.at[m, j], other)
            copy.wait_send()
            copy.wait_recv()
        mine = pasts[m].at[pl.ds(1, steps), 0]
        pltpu.make_async_copy(mine, mine, r.past_local.at[m]).wait()

    def exchange(m, t, k, peer):
        slot = lax.rem(t, 2)
        own = fulls[m].at[t, :, own_columns]
        return to_peer(own, own, r.hidden_send.at[m, slot, k], r.hidden_recv.at[m, slot, k], peer)

    def finish(m, t, sums, memory):
        in_gate = jax.nn.sigmoid(sums[0])
        forget = jax.nn.sigmoid(sums[1])
        candidate = jnp.tanh(sums[2])
        out_gate = jax.nn.sigmoid(sums[3])
        new_memory = in_gate * candidate if memory is None else forget * memory + in_gate * candidate
        fulls[m][t, :, own_columns] = (out_gate * jnp.tanh(new_memory)).astype(B16)
        for k, peer in urgent:
            exchange(m, t, k, peer).start()
        for g, value in enumerate((in_gate, forget, candidate, out_gate)):
            acts[m][t, g] = value
        cells[m][t] = new_memory

    def start_sums(m, t):
        ids, stops = r.group_ids[...], r.group_ids[:, length : length + 1]
        x_t = dot(marks(id_column(ids, stops, m, t), r.table.shape[1]), r.table[m]).astype(B16)
        return [
            r.gate_bias[m, g : g + 1, :].astype(F32) + dot(x_t, r.inputs[m, g]) for g in range(4)
        ]

    def add_chunk(m, t, owner, sums):
        part = fulls[m][t, :, span(owner, units)]
        return [sums[g] + dot(part, r.weights[m, g, span(owner, units), :]) for g in range(4)]

    def advance(m, t):
        sums = add_chunk(m, t - 1, place, start_sums(m, t))
        for k in range(len(peers)):
            exchange(m, t - 1, k, peers[k]).wait_recv()
            sums = add_chunk(m, t - 1, peers[k], sums)
        finish(m, t, sums, cells[m][t - 1])
        for k in range(len(peers)):
            exchange(m, t - 1, k, peers[k]).wait_send()
        spread_past(m, t - 1)

    def turn_block(m, g, p):
        r.weights[m, g, span(p, units), :] = r.weights[m, g, span(p, units), :].T

    stretch = 4

    def decode(m, chunk):
        t0 = stretch * chunk
        hidden = fulls[m][pl.ds(t0, stretch)].reshape(stretch * rows, count * units)
        logits = dot(hidden, r.out_full[m].reshape(count * units, -1)) + r.out_bias[m : m + 1, :]
        grown = jnp.exp(logits - jnp.max(logits, axis=1, keepdims=True))
        chances = grown / jnp.sum(grown, axis=1, keepdims=True)
        ids, stops = r.group_ids[...], r.group_ids[:, length : length + 1]
        targets, active = [], []
        for i in range(stretch):
            t = t0 + i
            if m == 0:
                targets.append(column_of(ids, lax.rem(t + 1, length)))
                live = jnp.full((rows, 1), t, jnp.int32) < length - 1
            else:
                targets.append(column_of(ids, jnp.maximum(stops - 2 - t, 0)))
                live = stops >= t + 2
            active.append(jnp.where(live, factor, 0.0).astype(F32))
        target, weight = jnp.concatenate(targets, axis=0), jnp.concatenate(active, axis=0)
        lane = lax.broadcasted_iota(jnp.int32, logits.shape, 1)
        picked = (lane == target).astype(F32)
        grad = ((chances - picked) * weight).astype(B16)
        logit_grads[m][pl.ds(t0, stretch)] = grad.reshape(stretch, rows, -1)
        own = fulls[m][pl.ds(t0, stretch), :, own_columns].reshape(stretch * rows, units)
        ones = jnp.ones((stretch * rows, LANES), B16)
        r.out_sums[m] += dot_first(grad, jnp.concatenate([own, ones], axis=1))

    piece = r.out_inbox.shape[2]

    def out_send(m, j):
        other = lax.rem(group + 1 + j, groups)
        return to_group(
            r.out_sums.at[m, span(other, piece)],
            r.out_inbox.at[m, j],
            r.out_send.at[m, j],
            r.out_recv.at[m, j],
            other,
        )

    def out_share(m, j):
        own = r.out_total.at[m, span(group, piece)]
        other = lax.rem(group + 1 + j, groups)
        return to_group(own, own, r.total_send.at[m, j], r.total_recv.at[m, j], other)

    def out_reduce(m):
        total = r.out_sums[m, span(group, piece)]
        for j in range(groups - 1):
            copy = out_send(m, j)
            copy.wait_send()
            copy.wait_recv()
        for j in range(groups - 1):
            total = total + r.out_inbox[m, j]
        r.out_total[m, span(group, piece)] = total

    def out_steps(m, n):
        pl.when(jnp.logical_and(n >= 0, n < groups - 1))(lambda: out_send(m, n).start())
        pl.when(n == groups)(lambda: out_reduce(m))
        ready = jnp.logical_and(n > groups, n < 2 * groups)
        pl.when(ready)(lambda: out_share(m, n - groups - 1).start())

    gates = fulls

    def spread_gates(m, t):
        for j, other in enumerate(others):
            to_group(
                gates[m].at[t, :, span(lax.rem(other, 2), 2 * units)],
                wides[m].at[t, group],
                r.wide_send.at[m, j],
                r.wide_recv.at[m, t // 2],
                other,
            ).start()
        pltpu.make_async_copy(
            gates[m].at[t, :, span(core, 2 * units)], wides[m].at[t, group], r.wide_local.at[m, t // 2]
        ).start()

    def arrive(m, pair):
        far = wides[m].at[pl.ds(2 * pair, 2), pl.ds(0, groups - 1)]
        to_group(far, far, r.wide_send.at[m, 0], r.wide_recv.at[m, pair], others[0]).wait_recv()
        near = wides[m].at[pl.ds(2 * pair, 2), 0]
        pltpu.make_async_copy(near, near, r.wide_local.at[m, pair]).wait()

    def fetches(m, pair):
        slot = lax.rem(pair, 2)
        return (
            pltpu.make_async_copy(
                wides[m].at[pl.ds(2 * pair, 2)], r.wide_slot.at[m, slot], r.fetch_sem.at[m, slot, 0]
            ),
            pltpu.make_async_copy(
                pasts[m].at[pl.ds(2 * pair, 2)], r.past_slot.at[m, slot], r.fetch_sem.at[m, slot, 1]
            ),
        )

    def fetch(m, pair):
        arrive(m, pair)
        for copy in fetches(m, pair):
            copy.start()

    def accumulate(m, pair):
        slot = lax.rem(pair, 2)
        for copy in fetches(m, pair):
            copy.wait()
        dz = r.wide_slot[m, slot].reshape(-1, 2 * units)
        past = r.past_slot[m, slot].reshape(dz.shape[0], -1)
        r.rec_sums[m] += dot_first(past, dz)
        ids, stops = r.every_ids[...], r.every_ids[:, length : length + 1]
        spots = [marks(id_column(ids, stops, m, 2 * pair + i), r.table.shape[1]) for i in range(2)]
        spots = jnp.concatenate(spots, axis=0)
        r.in_sums[m] += dot_first(dot(spots, r.table[m]).astype(B16), dz)
        grad_x = None
        for g in range(2):
            term = dot_last(dz[:, g * units : (g + 1) * units], r.inputs[m, 2 * core + g])
            grad_x = term if grad_x is None else grad_x + term
        width = grad_x.shape[1]
        three = dot_first(spots, jnp.concatenate(split_three(grad_x), axis=1))
        r.embed_part[m] += three[:, :width] + three[:, width : 2 * width] + three[:, 2 * width :]

    def give(m, t, k, peer):
        slot = lax.rem(t, 2)
        return to_peer(
            r.outbox.at[m, slot, k],
            r.inbox.at[m, slot, k],
            r.grad_send.at[m, slot, k],
            r.grad_recv.at[m, slot, k],
            peer,
        )

    def slopes(m, t, prev_memory):
        in_gate, forget, candidate, out_gate = (acts[m][t, g] for g in range(4))
        squashed = jnp.tanh(cells[m][t])
        forget_slope = jnp.zeros_like(forget)
        if prev_memory is not None:
            forget_slope = prev_memory * forget * (1.0 - forget)
        return (
            candidate * in_gate * (1.0 - in_gate),
            forget_slope,
            in_gate * (1.0 - candidate * candidate),
            squashed * out_gate * (1.0 - out_gate),
            out_gate * (1.0 - squashed * squashed),
            forget,
        )

    def gate_grads(m, t, slope, grad_hidden, carried):
        grad_memory = grad_hidden * slope[4]
        if carried is not None:
            grad_memory = carried + grad_memory
        values = [grad_memory * slope[g] for g in range(3)] + [grad_hidden * slope[3]]
        for g, value in enumerate(values):
            gates[m][t, :, g * units : (g + 1) * units] = value.astype(B16)
        r.cell_grad[m] = grad_memory * slope[5]

    def product(m, t, owner):
        total = None
        for g in range(4):
            part = dot(
                gates[m][t, :, g * units : (g + 1) * units], r.weights[m, g, span(owner, units), :]
            )
            total = part if total is None else total + part
        return total

    def from_decoder(m, t):
        return dot(logit_grads[m][t], r.out_own[m])

    def send_products(m, t):
        for k, peer in urgent:
            r.outbox[m, lax.rem(t, 2), k] = product(m, t, peer).astype(B16)
            give(m, t, k, peer).start()
        r.own_part[m] = product(m, t, place) + from_decoder(m, t - 1)
        spread_gates(m, t)

    def incoming(m, t):
        total = r.own_part[m]
        for k in range(len(peers)):
            give(m, t, k, peers[k]).wait_recv()
            total = total + r.inbox[m, lax.rem(t, 2), k].astype(F32)
        return total

    def sent(m, t):
        for k in range(len(peers)):
            give(m, t, k, peers[k]).wait_send()

    def retreat(m, t):
        slope = slopes(m, t, cells[m][t - 1])
        gate_grads(m, t, slope, incoming(m, t + 1), r.cell_grad[m])
        send_products(m, t)
        sent(m, t + 1)

    def first(m):
        t = ends[m] - 1
        gate_grads(m, t, slopes(m, t, cells[m][t - 1]), from_decoder(m, t), None)
        send_products(m, t)

    def last(m):
        slope = slopes(m, 0, None)
        gate_grads(m, 0, slope, incoming(m, 1), r.cell_grad[m])
        spread_gates(m, 0)
        sent(m, 1)

    depth = r.rec_grad.shape[2]
    kept = r.in_all.shape[2]

    def swap(m, g, i):
        source, target = (
            (r.rec_sums.at[m, span(1 - core, depth), pl.ds(g * units, units)], r.rec_grad),
            (r.in_sums.at[m, pl.ds(0, kept), pl.ds(g * units, units)], r.in_all),
        )[i]
        target = target.at[m, 2 * core + g]
        return to_group(source, target, r.swap_send.at[i, m, g], r.swap_recv.at[i, m, g], sibling)

    def keep(m, g):
        return pltpu.make_async_copy(
            r.rec_sums.at[m, span(core, depth), pl.ds(g * units, units)],
            r.rec_grad.at[m, 2 * core + g],
            r.keep_sem.at[m, g],
        )

    def start_swaps(m):
        for g in range(2):
            swap(m, g, 1).start()
        for g in range(2):
            swap(m, g, 0).start()
            keep(m, g).start()
            r.in_all[m, 2 * core + g] = r.in_sums[m, :kept, g * units : (g + 1) * units]

    def finish_inputs(m):
        for g in range(2):
            swap(m, g, 1).wait()
        for g in range(4):
            r.grad_in[m, :, g, :] = r.in_all[m, g, :embed]
        r.grad_bias[m] = r.in_all[m, :, embed, :]

    def finish_swaps(m):
        for g in range(2):
            swap(m, g, 0).wait()
            keep(m, g).wait()

    half = r.embed_half.shape[1]
    slice_rows = half // count

    def embed_pair(m):
        return to_group(
            r.embed_part.at[m, span(1 - core, half)],
            r.embed_half.at[m],
            r.embed_send.at[m, 0],
            r.embed_recv.at[m, 0],
            sibling,
        )

    def embed_reduce(m, k):
        return to_peer(
            r.embed_half.at[m, span(peers[k], slice_rows)],
            r.embed_inbox.at[m, k],
            r.reduce_send.at[m, k],
            r.reduce_recv.at[m, k],
            peers[k],
        )

    def own_slice(m):
        first_row = pl.multiple_of(core * half + place * slice_rows, 8)
        return r.embed_full.at[m, pl.ds(first_row, slice_rows)]

    def embed_gather(m, k):
        return to_peer(
            own_slice(m), own_slice(m), r.gather_send.at[m, k], r.gather_recv.at[m, k], peers[k]
        )

    def embed_return(m):
        whole = r.embed_full.at[m, span(core, half)]
        return to_group(whole, whole, r.embed_send.at[m, 1], r.embed_recv.at[m, 1], sibling)

    def embed_stage(m, stage):
        if stage == 0:
            embed_pair(m).start()
        elif stage == 1:
            embed_pair(m).wait()
            r.embed_half[m] += r.embed_part[m, span(core, half)]
            for k in reversed(range(len(peers))):
                embed_reduce(m, k).start()
        elif stage == 2:
            total = r.embed_half[m, span(place, slice_rows)]
            for k in range(len(peers)):
                embed_reduce(m, k).wait()
                total = total + r.embed_inbox[m, k]
            own_slice(m)[...] = total
            for k in reversed(range(len(peers))):
                embed_gather(m, k).start()
        elif stage == 3:
            for k in range(len(peers)):
                embed_gather(m, k).wait()
            embed_return(m).start()
        else:
            embed_return(m).wait()
            r.grad_embed[:, m, :] = r.embed_full[m, :vocab, :embed]

    for k in range(len(peers)):
        id_copy(k).wait()
    for s in range(count):
        r.group_ids[s * seq_dev : (s + 1) * seq_dev] = r.id_blocks[group, s, :seq_dev]
    for j in range(len(others)):
        id_spread(j).start()
    for m in range(2):
        finish(m, 0, start_sums(m, 0), None)
    r.blank[...] = jnp.zeros_like(r.blank)
    for copy in blanks:
        copy.start()
    prepare_decoder()
    for copy in blanks:
        copy.wait()
    for load in loads:
        load.wait()

    shared = first_spread + groups

    def both(t, carry):
        advance(0, t)
        advance(1, t)
        send_shares(t)
        pl.when(t == 2)(prepare_sums)

        @pl.when(t == shared)
        def _():
            for j in range(groups - 1):
                for k in range(len(peers)):
                    share_spread(j, k).wait()

        chunk = t - shared - 1
        pl.when(jnp.logical_and(chunk >= 0, stretch * (chunk + 1) <= t))(lambda: decode(0, chunk))
        return carry

    decoded = 0
    while stretch * (decoded + 1) <= shared + 1 + decoded and shared + 1 + decoded < half_len:
        decoded += 1

    def settle(m):
        for k in range(len(peers)):
            exchange(m, ends[m] - 1, k, peers[k]).wait()

    back_chunks = half_len // stretch
    blocks = 4 * count
    begin = 3
    back_pairs = half_len // 2
    front_pairs = length // 2
    assert half_len % stretch == 0 and length == 2 * half_len and half_len % 2 == 0
    assert first_spread + groups - 1 <= half_len
    assert back_chunks == 2 * begin and blocks <= 6 * begin and groups < half_len // 2

    def front_only(t, carry):
        advance(0, t)
        n = t - half_len

        @pl.when(n < begin)
        def _():
            for i in range(2):
                decode(1, back_chunks - 1 - 2 * n - i)
            for i in range(6):
                block = 6 * n + i
                pl.when(block < blocks)(lambda: turn_block(1, block // count, lax.rem(block, count)))

        @pl.when(n == begin)
        def _():
            finish_past(1, half_len - 1)
            first(1)

        pl.when(n > begin)(lambda: retreat(1, half_len - 1 - (n - begin)))
        begun = n >= begin
        chunk = n - begin + decoded
        early = jnp.logical_and(begun, stretch * (chunk + 1) <= t)
        late = jnp.logical_and(stretch * (chunk + 1) > t, lax.rem(t, stretch) == 0)
        pl.when(early)(lambda: decode(0, chunk))
        pl.when(jnp.logical_and(begun, late))(lambda: decode(0, t // stretch - 1))
        behind = n - begin - 5
        even = jnp.logical_and(behind >= 0, lax.rem(n - begin, 2) == 1)
        odd = jnp.logical_and(behind >= 1, lax.rem(n - begin, 2) == 0)
        pl.when(even)(lambda: fetch(1, back_pairs - 1 - behind // 2))
        pl.when(odd)(lambda: accumulate(1, back_pairs - 1 - behind // 2))
        return carry

    lax.fori_loop(1, half_len, both, 0)
    settle(1)
    for j in range(len(others)):
        id_spread(j).wait()
    r.every_ids[...] = r.id_blocks[:, :, :seq_dev].reshape(r.every_ids.shape)
    lax.fori_loop(half_len, length, front_only, 0)
    for g in range(4):
        for p in range(count):
            turn_block(0, g, p)
    settle(0)
    decode(0, length // stretch - 1)
    finish_past(0, length - 1)

    first(0)
    retreat(1, begin - 1)
    retreat(0, length - 2)
    retreat(1, begin - 2)
    fetched = (half_len - begin - 5) // 2
    left = back_pairs - fetched
    after = left + 2

    def turn(step, carry):
        retreat(0, length - 1 - 2 * step)
        pl.when(step == 1)(lambda: last(1))
        pl.when(step >= 3)(lambda: fetch(0, front_pairs + 2 - step))
        remaining = jnp.logical_and(step >= 2, step < left + 2)
        pl.when(remaining)(lambda: fetch(1, left + 1 - step))
        for stage in range(5):
            pl.when(step == after + stage)(lambda stage=stage: embed_stage(1, stage))
        pl.when(step == after)(lambda: start_swaps(1))
        pl.when(step == after + 2)(lambda: finish_inputs(1))
        retreat(0, length - 2 - 2 * step)
        pl.when(step >= 3)(lambda: accumulate(0, front_pairs + 2 - step))
        pl.when(remaining)(lambda: accumulate(1, left + 1 - step))
        out_steps(0, step - 1)
        out_steps(1, step - 1)
        return carry

    final = half_len - 1
    assert begin == 3 and after + 5 <= final
    lax.fori_loop(1, final, turn, 0)
    retreat(0, 1)
    fetch(0, 3)
    last(0)
    fetch(0, 2)
    accumulate(0, 3)
    accumulate(0, 2)
    fetch(0, 1)
    for m in range(2):
        for j in range(groups - 1):
            out_share(m, j).wait()
        r.grad_out[:, m, :] = r.out_total[m, :vocab, :units]
        r.grad_bout[m : m + 1, :] = r.out_total[m, :, units:].T[:1, :vocab]
    finish_swaps(1)
    accumulate(0, 1)
    fetch(0, 0)
    accumulate(0, 0)
    embed_stage(0, 0)
    start_swaps(0)
    embed_stage(0, 1)
    for m in range(2):
        for j in range(groups - 1):
            part = wides[m].at[:, 0]
            to_group(part, part, r.wide_send.at[m, j], r.wide_recv.at[m, 0], others[j]).wait_send()
    embed_stage(0, 2)
    finish_inputs(0)
    finish_swaps(0)
    embed_stage(0, 3)
    embed_stage(0, 4)


def run_step(count, groups, factor, char_ids, prefix, embedding, w_in, w_rec, gate_bias, w_out, b_out):
    seq_dev, length = char_ids.shape
    half_len = length // 2
    units, shard_units = w_rec.shape[2:]
    vocab, embed = embedding.shape[1:]
    rows = seq_dev * count
    wide = units // (groups // 2)
    depth = -(-(embed + 1) // LANES) * LANES
    lanes = -(-vocab // LANES) * LANES
    reduced = -(-vocab // (16 * count)) * 8 * count
    padded = 2 * reduced
    piece = lanes // groups
    links = count - 1
    far = groups - 1
    dma = pltpu.SemaphoreType.DMA
    ins = dict(
        chars=(char_ids, VMEM),
        prefix=(prefix[None], VMEM),
        embedding=(embedding.transpose(1, 0, 2), VMEM),
        w_in=(w_in.transpose(0, 2, 1, 3), VMEM),
        gate_bias=(gate_bias, VMEM),
        w_out=(w_out.transpose(2, 0, 1), VMEM),
        b_out=(b_out, VMEM),
        w_rec=(w_rec, ANYWHERE),
    )
    outs = dict(
        grad_embed=((vocab, 2, embed), F32, VMEM),
        grad_in=((2, embed, 4, shard_units), F32, VMEM),
        rec_grad=((2, 4, wide // 2, shard_units), F32, ANYWHERE),
        grad_bias=((2, 4, shard_units), F32, VMEM),
        grad_out=((vocab, 2, shard_units), F32, VMEM),
        grad_bout=((2, vocab), F32, VMEM),
        past_front=((length, groups, rows, wide), B16, ANYWHERE),
        past_back=((half_len, groups, rows, wide), B16, ANYWHERE),
        wide_front=((length, groups, rows, 2 * shard_units), B16, ANYWHERE),
        wide_back=((half_len, groups, rows, 2 * shard_units), B16, ANYWHERE),
    )
    arrays = dict(
        weights=(w_rec.shape, B16),
        out_bias=((2, lanes), F32),
        out_full=((2, count, groups, shard_units // groups, lanes), B16),
        id_blocks=((groups, count, max(8, seq_dev), LANES), jnp.int32),
        group_ids=((rows, LANES), jnp.int32),
        every_ids=((groups * rows, LANES), jnp.int32),
        blank=((groups, rows, wide), B16),
        full_front=((length, rows, units), B16),
        full_back=((half_len, rows, units), B16),
        acts_front=((length, 4, rows, shard_units), F32),
        acts_back=((half_len, 4, rows, shard_units), F32),
        cell_front=((length, rows, shard_units), F32),
        cell_back=((half_len, rows, shard_units), F32),
        logits_front=((length, rows, lanes), B16),
        logits_back=((half_len, rows, lanes), B16),
        out_sums=((2, lanes, shard_units + LANES), F32),
        out_inbox=((2, far, piece, shard_units + LANES), F32),
        out_total=((2, lanes, shard_units + LANES), F32),
        outbox=((2, 2, links, rows, shard_units), B16),
        inbox=((2, 2, links, rows, shard_units), B16),
        own_part=((2, rows, shard_units), F32),
        cell_grad=((2, rows, shard_units), F32),
        rec_sums=((2, wide, 2 * shard_units), F32),
        in_sums=((2, depth, 2 * shard_units), F32),
        in_all=((2, 4, -(-(embed + 1) // 8) * 8, shard_units), F32),
        table=((2, padded, depth), B16),
        inputs=((2, 4, depth, shard_units), B16),
        out_own=((2, lanes, shard_units), B16),
        embed_part=((2, padded, depth), F32),
        embed_half=((2, reduced, depth), F32),
        embed_full=((2, padded, depth), F32),
        embed_inbox=((2, links, reduced // count, depth), F32),
        wide_slot=((2, 2, 2, groups, rows, 2 * shard_units), B16),
        past_slot=((2, 2, 2, groups, rows, wide), B16),
    )
    semaphores = dict(
        load_sem=(2,),
        id_send=(links,),
        id_recv=(links,),
        ids_send=(far,),
        ids_recv=(far,),
        share_send=(2 * links,),
        share_recv=(2 * links,),
        all_send=(far, links),
        all_recv=(far, links),
        past_send=(2, far),
        past_recv=(2, far),
        past_local=(2,),
        hidden_send=(2, 2, links),
        hidden_recv=(2, 2, links),
        out_send=(2, far),
        out_recv=(2, far),
        total_send=(2, far),
        total_recv=(2, far),
        wide_send=(2, far),
        wide_recv=(2, length // 2),
        wide_local=(2, length // 2),
        fetch_sem=(2, 2, 2),
        grad_send=(2, 2, links),
        grad_recv=(2, 2, links),
        swap_send=(2, 2, 2),
        swap_recv=(2, 2, 2),
        keep_sem=(2, 2),
        embed_send=(2, 2),
        embed_recv=(2, 2),
        reduce_send=(2, links),
        reduce_recv=(2, links),
        gather_send=(2, links),
        gather_recv=(2, links),
    )
    scratch = {key: pltpu.VMEM(shape, kind) for key, (shape, kind) in arrays.items()}
    scratch |= {key: dma(shape) for key, shape in semaphores.items()}
    body = functools.partial(step_body, count, groups, factor)
    return call(body, "lstm_step", ins, outs, scratch, 2, 10**11, resident=True)


def shifted(values):
    return jnp.concatenate([jnp.zeros_like(values[:1]), values[:-1]], axis=0)


def reduced_grads(ran, gates, embedding, w_in, ids, group_size):
    embed = embedding.shape[2]

    def per_model(full, grads, ids, m):
        grads = grads.reshape(grads.shape[0], group_size, 4, -1)
        rec = jnp.einsum("tbk,tbgn->gkn", shifted(full), grads, preferred_element_type=F32)
        spots = one_hot(ids, embedding.shape[1], B16)
        x = jnp.einsum("tbv,ve->tbe", spots, embedding[m], preferred_element_type=F32).astype(B16)
        in_grad = jnp.einsum("tbe,tbgn->gen", x, grads, preferred_element_type=F32)
        bias = jnp.sum(grads, axis=(0, 1), dtype=F32)
        dx = jnp.einsum("tbgn,gen->tbe", grads, w_in[m], preferred_element_type=F32)
        embed_grad = jnp.einsum("tbv,tbe->ve", spots.astype(F32), dx, precision=PRECISE)
        return rec, in_grad, bias, embed_grad

    parts = (
        per_model(ran.full_front, gates.gates_front, ids[0], 0),
        per_model(ran.full_back, gates.gates_back, ids[1], 1),
    )
    rec, in_grad, bias, embed_grad = (jnp.stack(values) for values in zip(*parts))
    rec_grad = lax.psum_scatter(rec, "rep", scatter_dimension=2, tiled=True)
    in_sum, bias_sum = lax.psum((in_grad, bias), "rep")
    embed_sum = lax.psum(embed_grad, ("rep", "shard"))
    return embed_sum, in_sum, rec_grad, bias_sum


def shards(char_ids, prefix, embedding, w_in, w_rec, gate_bias, w_out, b_out):
    seq_dev, length = char_ids.shape
    half_len = length // 2
    vocab_size, embed = embedding.shape[1:]
    shard_units = w_rec.shape[3]
    count, groups = lax.axis_size("shard"), lax.axis_size("rep")
    group_size = seq_dev * count
    factor = 1.0 / math.sqrt(groups * count * seq_dev * length)
    if groups == 8 and count == 4 and length == 48:
        done = run_step(
            count, groups, factor, char_ids, prefix, embedding, w_in, w_rec, gate_bias, w_out, b_out
        )
        return (
            done.grad_embed.transpose(1, 0, 2),
            done.grad_in.transpose(0, 2, 1, 3),
            done.rec_grad,
            done.grad_bias,
            done.grad_out.transpose(1, 2, 0),
            done.grad_bout,
        )
    own_ids = jnp.concatenate([char_ids, prefix[:, None]], axis=1)
    own_ids = jnp.pad(own_ids, ((0, 0), (0, LANES - length - 1)))
    full_out = lax.all_gather(w_out, "shard", axis=1, tiled=True)
    depth = -(-(embed + 1) // LANES) * LANES
    padded = -(-vocab_size // LANES) * LANES
    table = jnp.pad(embedding, ((0, 0), (0, 0), (0, 1)), constant_values=1)
    table = jnp.pad(table, ((0, 0), (0, padded - vocab_size), (0, depth - embed - 1)))
    inputs = jnp.pad(w_in, ((0, 0), (0, 0), (0, depth - embed), (0, 0)))
    ran = run_forward(count, length, own_ids, table, inputs, gate_bias.astype(F32), w_rec)
    group_chars, group_prefix = ran.group_ids[:, :length], ran.group_ids[:, length]
    front_in = group_chars.T
    front_target = jnp.concatenate([group_chars[:, 1:], group_chars[:, :1]], axis=1).T
    timeline = jnp.arange(length, dtype=jnp.int32)[:, None]
    front_active = jnp.broadcast_to((timeline < length - 1).astype(F32), (length, group_size))
    reverse_steps = jnp.arange(half_len, dtype=jnp.int32)[:, None]

    def back_pick(offset):
        spot = jnp.maximum(group_prefix[None, :] - offset - reverse_steps, 0)
        chosen = one_hot(spot, length, jnp.int32) * group_chars[None]
        return jnp.sum(chosen, axis=-1)

    back_target = back_pick(2)
    back_active = (reverse_steps <= group_prefix[None, :] - 2).astype(F32)
    first_unit = lax.axis_index("shard") * shard_units

    def decode(full, m, target, active):
        rows = full.reshape(-1, full.shape[-1])
        logits = dot(rows, full_out[m]) + b_out[m].astype(F32)
        grad = loss_grad(logits, target.reshape(-1), active.reshape(-1), factor)
        dec = dot_last(grad, w_out[m])
        own = lax.dynamic_slice_in_dim(rows, first_unit, shard_units, axis=1)
        out_grad = dot_first(own, grad)
        bout = jnp.sum(grad, axis=0, dtype=F32)
        return dec.reshape(full.shape[0], group_size, shard_units), out_grad, bout

    front_dec, front_out_grad, front_bout = decode(ran.full_front, 0, front_target, front_active)
    back_dec, back_out_grad, back_bout = decode(ran.full_back, 1, back_target, back_active)
    out_and_bout = jnp.stack(
        [
            jnp.concatenate([front_out_grad, front_bout[None]], axis=0),
            jnp.concatenate([back_out_grad, back_bout[None]], axis=0),
        ]
    )
    out_and_bout = lax.psum(out_and_bout, "rep")
    out_sum, bout_sum = out_and_bout[:, :shard_units], out_and_bout[:, shard_units]
    done = run_backward(count, ran, (front_dec, back_dec))
    embed_sum, in_sum, rec_grad, bias_sum = reduced_grads(
        ran, done, embedding, w_in, (front_in, back_pick(1)), group_size
    )
    return (embed_sum, in_sum, rec_grad, bias_sum, out_sum, bout_sum)


def solution(mesh):
    in_specs = (
        P(("rep", "shard"), None),
        P(("rep", "shard")),
        P(),
        P(None, None, None, "shard"),
        P(None, None, None, "shard"),
        P(None, None, "shard"),
        P(None, "shard", None),
        P(),
    )
    out_specs = (
        P(),
        P(None, None, None, "shard"),
        P(None, None, "rep", "shard"),
        P(None, None, "shard"),
        P(None, "shard", None),
        P(),
    )
    return jax.shard_map(shards, mesh=mesh, in_specs=in_specs, out_specs=out_specs, check_vma=False)
```
